32 devices in a mesh: dp: 16 (over z, x, core), seq: 2 (over y).
Axes of the slice: x: 2, y: 2, z: 4, core: 2. Of those that a mesh axis runs over, the one named last changes fastest.
Arguments:
- tokens: bfloat16 [16, 1152, 1024], P('dp', 'seq'), may hold values from -6 to 6
- w_qkv: bfloat16 [1024, 3072], P('dp'), may hold values from -0.1875 to 0.1875
- w_out: bfloat16 [1024, 1024], P('dp'), may hold values from -1 to 1
- w_up: bfloat16 [1024, 4096], P('dp'), may hold values from -0.1875 to 0.1875
- w_down: bfloat16 [4096, 1024], P('dp'), may hold values from -0.09375 to 0.09375
- gains: bfloat16 [1024, 2], P('dp'), may hold values from 0.5 to 1.5
- biases: bfloat16 [1024, 6], P('dp'), may hold values from -1.1953125 to 1.1953125
- up_bias: bfloat16 [4096], P('dp'), may hold values from -1.1953125 to 1.1953125
- valid: int32 [16], P('dp'), may hold values from 577 to 1152
- cotangent: bfloat16 [16, 1152, 1024], P('dp', 'seq'), may hold values from -6 to 6
Outputs:
- out_tokens: bfloat16 [16, 1152, 1024], P('dp', 'seq')
- grad_tokens: float32 [16, 1152, 1024], P('dp', 'seq')
- grad_qkv: float32 [1024, 3072], P('dp')
- grad_out: float32 [1024, 1024], P('dp')
- grad_up: float32 [1024, 4096], P('dp')
- grad_down: float32 [4096, 1024], P('dp')
- grad_gains: float32 [1024, 2], P('dp')
- grad_biases: float32 [1024, 6], P('dp')
- grad_up_bias: float32 [4096], P('dp')
The draws below stay inside these ranges and needn't reach their ends.
Inputs may be any that keep to these rules, and one draw needn't show every extreme that they name: valid counts of the images; keys at positions from valid on are padding.
All inputs are finite; a program needn't handle non-finite values.
Results may differ from the reference program's by a relative error of at most 0.019.
Values may be sent and summed in bfloat16 or wider, within the bound.
A program may use at most 256 MiB of HBM per device.

```python
import jax
import jax.numpy as jnp
from jax import lax

D = 1024
FF = 4096
H = 16
SEQ = 1152
HD = 64
IMAGES = 16


def set_ends(drawn, own_key, least, top_value):
    spot = [jax.random.randint(jax.random.fold_in(own_key, axis), (), 0, length) for axis, length in enumerate(drawn.shape)]
    main_axis = drawn.shape.index(max(drawn.shape))
    neighbour = spot[:main_axis] + [(spot[main_axis] + 1) % drawn.shape[main_axis]] + spot[main_axis + 1:]
    return drawn.at[tuple(spot)].set(least).at[tuple(neighbour)].set(top_value)


def shard_levels(key, dims, split, smallest, high):
    def one(axis_at, shards_of):
        draws = jax.random.uniform(jax.random.fold_in(jax.random.fold_in(key, 6), axis_at), (shards_of,), jnp.float32, smallest / len(split), high / len(split))
        return jnp.repeat(jnp.exp(draws), dims[axis_at] // shards_of).reshape((-1,) + (1,) * (len(dims) - axis_at - 1))

    factor_of = one(*split[0])
    for cut in split[1:]:
        factor_of = factor_of * one(*cut)
    return factor_of


def gaussian(stream_key, extent, deviation, bound, split=(), kind=jnp.bfloat16):
    drawn = jax.random.normal(stream_key, extent, jnp.float32) * deviation
    if len(split) > 0:
        drawn = shard_levels(stream_key, extent, split, -0.22, 0.18) * drawn
    return jnp.clip(drawn, min=-bound, max=bound).astype(kind)


def setup_inputs(seed: int = 0) -> dict:
    key_of = jax.random.split(jax.random.key(seed), 11)
    return {
        "tokens": gaussian(key_of[0], (IMAGES, SEQ, D), 1.0, 6.0, ((0, 16), (1, 2))),
        "w_qkv": gaussian(key_of[1], (D, 3 * D), D ** -0.5, 0.1875, ((0, 16),)),
        "w_out": gaussian(key_of[2], (D, D), (D // 32) ** -0.5, 1.0, ((0, 16),)),
        "w_up": gaussian(key_of[3], (D, FF), D ** -0.5, 0.1875, ((0, 16),)),
        "w_down": gaussian(key_of[4], (FF, D), FF ** -0.5, 0.09375, ((0, 16),)),
        "gains": jnp.clip(1.0 + 0.1 * jax.random.normal(key_of[5], (D, 2), jnp.float32), 0.5, 1.5).astype(jnp.bfloat16),
        "biases": gaussian(key_of[6], (D, 6), 0.2, 1.1953125, ((0, 16),)),
        "up_bias": gaussian(key_of[7], (FF,), 0.2, 1.1953125, ((0, 16),)),
        "valid": set_ends(jax.random.randint(key_of[8], (IMAGES,), SEQ // 2 + 1, SEQ + 1), jax.random.fold_in(key_of[8], 1), SEQ // 2 + 1, SEQ).astype(jnp.int32),
        "cotangent": gaussian(key_of[9], (IMAGES, SEQ, D), 1.0, 6.0, ((0, 16), (1, 2))),
    }


EPSILON = 1e-06
NEG_FILL = -1e+30

@jax.custom_vjp
def low(v):
    return lax.optimization_barrier(v.astype(jnp.bfloat16)).astype(jnp.float32)

@jax.custom_vjp
def low_back(v):
    return v

def low_keep(v):
    return (low(v), None)

def low_pass(kept, grad):
    return (grad,)

def back_keep(v):
    return (v, None)

def back_low(kept, grad):
    return (low(grad),)
low.defvjp(low_keep, low_pass)
low_back.defvjp(back_keep, back_low)

def layer_norm(values, scales, offset):
    average = lax.optimization_barrier(jnp.mean(values, axis=-1, keepdims=True))
    centered = values - average
    variance = lax.optimization_barrier(jnp.mean(centered * centered, axis=-1, keepdims=True))
    return centered * lax.rsqrt(variance + EPSILON) * scales + offset

def attend_one(packed):
    queries, keyset, values, length = packed
    scores = jnp.einsum('qhd,khd->hqk', queries, keyset, precision=lax.Precision.HIGHEST) * HD ** (-0.5)
    scores = low_back(scores)
    allowed = jnp.arange(SEQ, dtype=jnp.int32) < length
    scores = jnp.where(allowed[None, None, :], scores, NEG_FILL)
    row_max = lax.optimization_barrier(jnp.max(scores, axis=-1, keepdims=True))
    exp_scores = jnp.exp(scores - row_max)
    probs = exp_scores / lax.optimization_barrier(jnp.sum(exp_scores, axis=-1, keepdims=True))
    return jnp.einsum('hqk,khd->qhd', low(probs), values, precision=lax.Precision.HIGHEST)

def forward(tokens, w_qkv, w_out, w_up, w_down, gains, biases, up_bias, valid):
    highest = lax.Precision.HIGHEST
    first = low(layer_norm(tokens, gains[:, 0], biases[:, 0]))
    mixed = jnp.einsum('isd,de->ise', first, w_qkv, precision=highest)
    queries = low(low_back(mixed[..., :D] + biases[:, 1]))
    keyset = low(low_back(mixed[..., D:2 * D]))
    values = low(low_back(mixed[..., 2 * D:] + biases[:, 2]))
    head_shape = (IMAGES, SEQ, H, HD)
    attended = lax.map(jax.checkpoint(attend_one), (queries.reshape(head_shape), keyset.reshape(head_shape), values.reshape(head_shape), valid))
    attended = low(low_back(attended.reshape(IMAGES, SEQ, D)))
    branch = low_back(jnp.einsum('isd,de->ise', attended, w_out, precision=highest) + biases[:, 3])
    residual = tokens + branch
    second = low(layer_norm(residual, gains[:, 1], biases[:, 4]))
    upward = low_back(jnp.einsum('isd,df->isf', second, w_up, precision=highest) + up_bias)
    activated = low(jax.nn.gelu(upward, approximate=False))
    return residual + jnp.einsum('isf,fd->isd', activated, w_down, precision=highest) + biases[:, 5]

def reference(tokens, w_qkv, w_out, w_up, w_down, gains, biases, up_bias, valid, cotangent):
    floats = tuple((entry_array.astype(jnp.float32) for entry_array in (tokens, w_qkv, w_out, w_up, w_down, gains, biases, up_bias)))

    def wrapped(*inputs):
        return forward(*inputs, valid)
    output, pull_back = jax.vjp(wrapped, *floats)
    grads = pull_back(cotangent.astype(jnp.float32))
    return (output.astype(jnp.bfloat16), grads[0], grads[1], grads[2], grads[3], grads[4], grads[5], grads[6], grads[7])
```

```python
import functools

import jax
import jax.numpy as jnp
from jax import lax
from jax.experimental import pallas as pl
from jax.experimental.pallas import tpu as pltpu
from jax.sharding import PartitionSpec as P

HD = 64
PAIR = 2 * HD
EPSILON = 1e-06
NEG_FILL = -1e30
SMALL = 128
GROUPS = 2


def dot_f32(a, b, dims):
    return lax.dot_general(a, b, (dims, ((), ())), preferred_element_type=jnp.float32)


def mat(a, b):
    return dot_f32(a, b, ((1,), (0,)))


def norm_parts(values):
    average = jnp.mean(values, axis=-1, keepdims=True)
    centered = values - average
    variance = jnp.mean(centered * centered, axis=-1, keepdims=True)
    inverse = lax.rsqrt(variance + EPSILON)
    return centered * inverse, inverse


def norm_back(hat, inverse, scales, grad):
    scaled = grad * scales
    first = jnp.mean(scaled, axis=-1, keepdims=True)
    second = jnp.mean(scaled * hat, axis=-1, keepdims=True)
    return inverse * (scaled - first - hat * second)


def lanes(head):
    lane = lax.broadcasted_iota(jnp.int32, (1, PAIR), 1)
    own = (lane < HD) if head == 0 else (lane >= HD)
    return own, lane - (HD if head == 0 else 0)


def key_bias(place_ref, valid_ref, length, shards):
    row = lax.broadcasted_iota(jnp.int32, (shards * length, 1), 0)
    position = row + place_ref[0] * length
    position = jnp.where(position >= shards * length, position - shards * length, position)
    allowed = position < valid_ref[pl.program_id(0)]
    return jnp.where(allowed, 0.0, NEG_FILL).astype(jnp.float32)


def augmented(values, head, extra):
    own, free = lanes(head)
    out = jnp.where(own, values, 0.0)
    for at, column in enumerate(extra):
        out = jnp.where(free == at, column, out)
    return out.astype(jnp.bfloat16)


def rows_with(values_t, head, extra):
    row = lax.broadcasted_iota(jnp.int32, (PAIR, 1), 0)
    own = (row < HD) if head == 0 else (row >= HD)
    free = row - (HD if head == 0 else 0)
    out = jnp.where(own, values_t, 0.0)
    for at, line in enumerate(extra):
        out = jnp.where(free == at, line, out)
    return out.astype(jnp.bfloat16)


def split_three(line):
    high = line.astype(jnp.bfloat16).astype(jnp.float32)
    rest = line - high
    middle = rest.astype(jnp.bfloat16).astype(jnp.float32)
    return high, middle, rest - middle


def forward_kernel(place_ref, valid_ref, q_ref, k_ref, v_ref, out_ref, lse_ref):
    shards, length, _ = q_ref.shape
    bias = key_bias(place_ref, valid_ref, length, shards)
    keys = k_ref[...].reshape(shards * length, PAIR).astype(jnp.float32)
    values = v_ref[...].reshape(shards * length, PAIR).astype(jnp.float32)
    keys_of = [augmented(keys, head, [bias]) for head in range(2)]
    values_of = [augmented(values, head, [1.0]).T for head in range(2)]
    for shard in range(shards):
        queries = q_ref[shard].astype(jnp.float32).T * HD**-0.5
        halves = []
        for head in range(2):
            scores = mat(keys_of[head], rows_with(queries, head, [1.0]))
            top = jnp.max(scores, axis=0, keepdims=True)
            weight = jnp.exp(scores - top).astype(jnp.bfloat16)
            part = mat(values_of[head], weight)
            at = HD * (1 - head)
            row_total = part[at : at + 1, :]
            halves.append(part[HD * head : HD * (head + 1), :] / row_total)
            lse_ref[0, 0, shard, head : head + 1, :] = top + jnp.log(row_total)
        out_ref[shard] = jnp.concatenate(halves, axis=0).T.astype(out_ref.dtype)


def backward_kernel(place_ref, valid_ref, q_ref, k_ref, v_ref, out_ref, lse_ref, da_ref, dq_ref, dk_ref, dv_ref):
    shards, length, _ = q_ref.shape
    bias = key_bias(place_ref, valid_ref, length, shards)
    keys = k_ref[...].reshape(shards * length, PAIR).astype(jnp.float32)
    values = v_ref[...].reshape(shards * length, PAIR).astype(jnp.float32)
    keys_of = [augmented(keys, head, [bias, 1.0, 1.0, 1.0]) for head in range(2)]
    values_of = [augmented(values, head, [1.0, 1.0, 1.0]) for head in range(2)]
    plain_keys = [augmented(keys, head, []).T for head in range(2)]
    dk = dv = None
    for shard in range(shards):
        queries = q_ref[shard].astype(jnp.float32) * HD**-0.5
        grads = da_ref[shard].astype(jnp.float32)
        queries_t, grads_t = queries.T, grads.T
        product = grads_t * out_ref[shard].astype(jnp.float32).T
        dq = None
        for head in range(2):
            lse = lse_ref[0, 0, shard, head : head + 1, :]
            delta = jnp.sum(product[HD * head : HD * (head + 1), :], axis=0, keepdims=True)
            scores = mat(keys_of[head], rows_with(queries_t, head, (1.0,) + split_three(-lse)))
            probs = jnp.exp(scores)
            moved = mat(values_of[head], rows_with(grads_t, head, split_three(-delta)))
            dscores = (probs * moved).astype(jnp.bfloat16)
            part_v = mat(probs.astype(jnp.bfloat16), augmented(grads, head, []))
            part_k = mat(dscores, augmented(queries, head, []))
            part_q = mat(plain_keys[head], dscores)
            dq = part_q if dq is None else dq + part_q
            dk = part_k if dk is None else dk + part_k
            dv = part_v if dv is None else dv + part_v
        dq_ref[shard] = (dq * HD**-0.5).T.astype(dq_ref.dtype)
    dk_ref[...] = dk.astype(dk_ref.dtype).reshape(dk_ref.shape)
    dv_ref[...] = dv.astype(dv_ref.dtype).reshape(dv_ref.shape)


def attention_specs(shards, length, pairs_all, first_pair):
    smem = pl.BlockSpec(memory_space=pltpu.SMEM)
    mixed = [
        pl.BlockSpec((shards, length, PAIR), lambda i, h, t=t: (0, i, t * pairs_all + first_pair + h))
        for t in range(3)
    ]
    plain = pl.BlockSpec((shards, length, PAIR), lambda i, h: (0, i, h))
    lse = pl.BlockSpec((1, 1, shards, 2, length), lambda i, h: (i, h, 0, 0, 0))
    return smem, mixed, plain, lse


def attend_forward(images, place, valid, mixed, first_pair, pairs):
    shards, rows, width3 = mixed.shape
    length = rows // images
    smem, block3, plain, lse = attention_specs(shards, length, width3 // 3 // PAIR, first_pair)
    work = shards * shards * rows * length * pairs
    return pl.pallas_call(
        forward_kernel,
        grid=(images, pairs),
        in_specs=[smem, smem] + block3,
        out_specs=[plain, lse],
        out_shape=[
            jax.ShapeDtypeStruct((shards, rows, pairs * PAIR), jnp.bfloat16),
            jax.ShapeDtypeStruct((images, pairs, shards, 2, length), jnp.float32),
        ],
        compiler_params=pltpu.CompilerParams(vmem_limit_bytes=40 * 2**20),
        cost_estimate=pl.CostEstimate(
            flops=8 * work * PAIR, bytes_accessed=8 * shards * rows * pairs * PAIR, transcendentals=2 * work,
        ),
    )(place, valid, mixed, mixed, mixed)


def attend_backward(images, place, valid, mixed, first_pair, pairs, attended, lse_in, da):
    shards, rows, width3 = mixed.shape
    length = rows // images
    smem, block3, plain, lse = attention_specs(shards, length, width3 // 3 // PAIR, first_pair)
    low = jax.ShapeDtypeStruct((shards, rows, pairs * PAIR), jnp.bfloat16)
    work = shards * shards * rows * length * pairs
    return pl.pallas_call(
        backward_kernel,
        grid=(images, pairs),
        in_specs=[smem, smem] + block3 + [plain, lse, plain],
        out_specs=[plain] * 3,
        out_shape=[low] * 3,
        compiler_params=pltpu.CompilerParams(vmem_limit_bytes=48 * 2**20),
        cost_estimate=pl.CostEstimate(
            flops=20 * work * PAIR, bytes_accessed=16 * shards * rows * pairs * PAIR, transcendentals=2 * work,
        ),
    )(place, valid, mixed, mixed, mixed, attended, lse_in, da)


def shift(values, shards, step):
    return lax.ppermute(values, "seq", [(i, (i + step) % shards) for i in range(shards)])


def everyone(values, shards, step_axis=0):
    return jnp.stack([values] + [shift(values, shards, -j) for j in range(1, shards)], axis=step_axis)


def in_order(values, shards, place):
    if shards == 2:
        other = shift(values, shards, 1)
        low = jnp.where(place == 0, values, other)
        high = jnp.where(place == 0, other, values)
        return jnp.stack([low, high])
    return lax.all_gather(values, "seq", axis=0)


def token_sum(values):
    return jnp.sum(values.astype(jnp.float32), axis=0)


def per_device(tokens, w_qkv, w_out, w_up, w_down, gains, biases, up_bias, valid, cotangent):
    images, length, width = tokens.shape
    rows = images * length
    shard_rows = w_qkv.shape[0]
    hidden = w_up.shape[1]
    ups = up_bias.shape[0] // shard_rows
    shards = lax.axis_size("seq")
    dps = lax.axis_size("dp")
    at = lax.axis_index("seq").astype(jnp.int32)
    place = at.reshape(1)
    part = width // shards
    own_hidden = hidden // shards
    sub = w_down.shape[0] // shards
    pairs_all = part // PAIR

    gather = functools.partial(lax.all_gather, axis_name="dp", axis=0, tiled=True)
    scatter = functools.partial(lax.psum_scatter, axis_name="dp", scatter_dimension=0, tiled=True)

    def pick(values, axis):
        return lax.dynamic_index_in_dim(values, at, axis, keepdims=False)

    smalls = jnp.concatenate([gains, biases, up_bias.reshape(shard_rows, ups)], axis=1)
    smalls = jnp.pad(smalls, ((0, 0), (0, SMALL - smalls.shape[1])))
    part_qkv = pick(w_qkv.reshape(shard_rows, 3, shards, part), 2).reshape(shard_rows, 3 * part)
    part_up = pick(w_up.reshape(shard_rows, dps, shards, sub), 2).reshape(shard_rows, own_hidden)
    part_down = pick(w_down.reshape(shards, sub, width), 0)
    full_qkvs = gather(jnp.concatenate([part_qkv, smalls], axis=1))
    w_out, full_qkvs = lax.optimization_barrier((w_out, full_qkvs))
    full_out = gather(w_out)
    part_up, full_out = lax.optimization_barrier((part_up, full_out))
    full_up = gather(part_up)
    part_down, full_up = lax.optimization_barrier((part_down, full_up))
    full_down = gather(part_down)

    flat_tokens = tokens.reshape(rows, width)
    flat_grad = cotangent.reshape(rows, width)
    all_tokens = everyone(flat_tokens, shards)
    flat_grad, all_tokens = lax.optimization_barrier((flat_grad, all_tokens))
    all_grad = everyone(flat_grad, shards).reshape(shards * rows, width)

    full_qkv = full_qkvs[:, : 3 * part]
    small = full_qkvs[:, 3 * part :].astype(jnp.float32).T
    gain_one, gain_two = small[0], small[1]
    bias_one, bias_q, bias_v, bias_out, bias_two, bias_down = (small[2 + i] for i in range(6))
    bias_up = pick(small[8 : 8 + ups].T.reshape(dps, shards, sub), 1).reshape(-1)
    bias_mixed = jnp.concatenate(
        [pick(bias_q.reshape(shards, part), 0), jnp.zeros((part,), jnp.float32), pick(bias_v.reshape(shards, part), 0)]
    )

    every_tokens = all_tokens.reshape(shards * rows, width).astype(jnp.float32)
    hat_one, inverse_one = norm_parts(every_tokens)
    first = (hat_one * gain_one + bias_one).astype(jnp.bfloat16)
    mixed = (mat(first, full_qkv) + bias_mixed).astype(jnp.bfloat16).reshape(shards, rows, 3 * part)

    groups = GROUPS if pairs_all % GROUPS == 0 else 1
    pairs = pairs_all // groups
    wide = pairs * PAIR
    forward = [attend_forward(images, place, valid, mixed, g * pairs, pairs) for g in range(groups)]
    blocks = []
    for j in range(shards):
        for g in range(groups):
            attended = forward[g][0]
            if j > 0:
                attended = jnp.roll(shift(attended, shards, -j), j, axis=0)
            blocks.append(attended.reshape(shards * rows, wide))
    merged = jnp.concatenate(blocks, axis=1)
    turned_out = jnp.roll(full_out, -at * part, axis=0)

    branch = mat(merged, turned_out) + bias_out
    residual = every_tokens + branch
    hat_two, inverse_two = norm_parts(residual)
    second = (hat_two * gain_two + bias_two).astype(jnp.bfloat16)
    upward = mat(second, full_up) + bias_up
    cdf = 0.5 * (1.0 + lax.erf(upward * 0.5**0.5))
    activated = (upward * cdf).astype(jnp.bfloat16)
    slope = cdf + upward * (jnp.exp(-0.5 * upward * upward) * 0.3989422804014327)
    slope = slope.astype(jnp.bfloat16)

    grad_act = dot_f32(all_grad, full_down, ((1,), (1,)))
    grad_upward = (grad_act * slope.astype(jnp.float32)).astype(jnp.bfloat16)

    def summed(left, right, dims):
        parts = [
            dot_f32(left[j * rows : (j + 1) * rows], right, dims) for j in range(shards)
        ]
        total = parts[0]
        for j in range(1, shards):
            total = total + shift(parts[j].astype(jnp.bfloat16), shards, j).astype(jnp.float32)
        return total

    grad_second = summed(grad_upward, full_up, ((1,), (1,)))
    grad_down = dot_f32(activated, all_grad, ((0,), (0,))).astype(jnp.bfloat16)
    piece_down = scatter(grad_down)
    grad_up = dot_f32(second, grad_upward, ((0,), (0,))).astype(jnp.bfloat16)
    grad_up, piece_down = lax.optimization_barrier((grad_up, piece_down))
    piece_up = scatter(grad_up)

    own_hat = hat_two[:rows]
    grad_resid = flat_grad.astype(jnp.float32) + norm_back(own_hat, inverse_two[:rows], gain_two, grad_second)
    grad_gain_two, grad_bias_two = token_sum(grad_second * own_hat), token_sum(grad_second)
    grad_branch = grad_resid.astype(jnp.bfloat16)
    grad_merged = dot_f32(grad_branch, turned_out, ((1,), (1,))).astype(jnp.bfloat16)
    received = [None] * shards
    for g in range(groups):
        lo = g * wide
        blocks = [grad_merged[:, lo : lo + wide]] + [None] * (shards - 1)
        for j in range(1, shards):
            blocks[shards - j] = shift(grad_merged[:, j * part + lo : j * part + lo + wide], shards, j)
        received[g] = jnp.stack(blocks)

    grad_out = dot_f32(merged[:rows], grad_branch, ((0,), (0,))).astype(jnp.bfloat16)
    grad_out = jnp.roll(grad_out, at * part, axis=0)
    grad_out, piece_up = lax.optimization_barrier((grad_out, piece_up))
    piece_out = scatter(grad_out)

    backs = [
        attend_backward(images, place, valid, mixed, g * pairs, pairs, *forward[g], received[g]) for g in range(groups)
    ]
    grad_mixed = jnp.concatenate(
        [back[t].reshape(shards * rows, wide) for t in range(3) for back in backs], axis=1
    )
    grad_first = summed(grad_mixed, full_qkv, ((1,), (1,)))
    grad_qkv = dot_f32(first, grad_mixed, ((0,), (0,))).astype(jnp.bfloat16)

    grad_tokens = grad_resid + norm_back(hat_one[:rows], inverse_one[:rows], gain_one, grad_first)
    grad_gain_one, grad_bias_one = token_sum(grad_first * hat_one[:rows]), token_sum(grad_first)

    def spread(values, before):
        out = jnp.zeros((before, shards, values.size // before), jnp.float32)
        return lax.dynamic_update_slice_in_dim(out, values.reshape(before, 1, -1), at, 1).reshape(-1)

    bias_sums = token_sum(grad_mixed)
    small_grads = jnp.stack(
        [
            grad_gain_one, grad_gain_two, grad_bias_one, spread(bias_sums[:part], 1), spread(bias_sums[2 * part :], 1),
            token_sum(grad_branch), grad_bias_two, token_sum(flat_grad),
        ],
        axis=1,
    )
    up_sums = spread(token_sum(grad_upward), dps).reshape(width, ups)
    small_grads = jnp.concatenate([small_grads, up_sums], axis=1)
    small_grads = jnp.pad(small_grads, ((0, 0), (0, SMALL - small_grads.shape[1])))
    grad_qkvs = jnp.concatenate([grad_qkv, small_grads.astype(jnp.bfloat16)], axis=1)
    grad_qkvs, piece_out = lax.optimization_barrier((grad_qkvs, piece_out))
    piece_qkvs = scatter(grad_qkvs)

    output = summed(activated, full_down, ((1,), (0,)))
    out_tokens = (residual[:rows] + output + bias_down).astype(jnp.bfloat16)

    total_down = in_order(piece_down, shards, at).astype(jnp.float32).reshape(shards * sub, width)
    total_up = in_order(piece_up.reshape(shard_rows, dps, sub), shards, at).astype(jnp.float32)
    total_up = total_up.transpose(1, 2, 0, 3).reshape(shard_rows, hidden)
    total_out = in_order(piece_out, shards, at).astype(jnp.float32).sum(0)
    every_qkvs = in_order(piece_qkvs, shards, at).astype(jnp.float32)
    total_qkv = every_qkvs[:, :, : 3 * part].reshape(shards, shard_rows, 3, part)
    total_qkv = total_qkv.transpose(1, 2, 0, 3).reshape(shard_rows, 3 * width)
    total_small = every_qkvs[:, :, 3 * part :].sum(0)
    return (
        out_tokens.reshape(tokens.shape),
        grad_tokens.reshape(tokens.shape),
        total_qkv,
        total_out,
        total_up,
        total_down,
        total_small[:, :2],
        total_small[:, 2:8],
        total_small[:, 8 : 8 + ups].reshape(-1),
    )


def solution(mesh):
    return jax.shard_map(
        per_device,
        mesh=mesh,
        in_specs=(
            P("dp", "seq", None),
            P("dp", None),
            P("dp", None),
            P("dp", None),
            P("dp", None),
            P("dp", None),
            P("dp", None),
            P("dp"),
            P("dp"),
            P("dp", "seq", None),
        ),
        out_specs=(
            P("dp", "seq", None),
            P("dp", "seq", None),
            P("dp", None),
            P("dp", None),
            P("dp", None),
            P("dp", None),
            P("dp", None),
            P("dp", None),
            P("dp"),
        ),
        check_vma=False,
    )
```

```python
import functools

import jax
import jax.numpy as jnp
from jax import lax
from jax.experimental import pallas as pl
from jax.experimental.pallas import tpu as pltpu
from jax.sharding import PartitionSpec as P

HD = 64
PAIR = 2 * HD
EPSILON = 1e-06
NEG_FILL = -1e30
SMALL = 128
GROUPS = 2


def dot_f32(a, b, dims):
    return lax.dot_general(a, b, (dims, ((), ())), preferred_element_type=jnp.float32)


def mat(a, b):
    return dot_f32(a, b, ((1,), (0,)))


def norm_parts(values):
    average = jnp.mean(values, axis=-1, keepdims=True)
    centered = values - average
    variance = jnp.mean(centered * centered, axis=-1, keepdims=True)
    inverse = lax.rsqrt(variance + EPSILON)
    return centered * inverse, inverse


def norm_back(hat, inverse, scales, grad):
    scaled = grad * scales
    first = jnp.mean(scaled, axis=-1, keepdims=True)
    second = jnp.mean(scaled * hat, axis=-1, keepdims=True)
    return inverse * (scaled - first - hat * second)


def lanes(head):
    lane = lax.broadcasted_iota(jnp.int32, (1, PAIR), 1)
    own = (lane < HD) if head == 0 else (lane >= HD)
    return own, lane - (HD if head == 0 else 0)


def key_bias(place_ref, valid_ref, length, shards):
    row = lax.broadcasted_iota(jnp.int32, (shards * length, 1), 0)
    position = row + place_ref[0] * length
    position = jnp.where(position >= shards * length, position - shards * length, position)
    allowed = position < valid_ref[pl.program_id(0)]
    return jnp.where(allowed, 0.0, NEG_FILL).astype(jnp.float32)


def augmented(values, head, extra):
    own, free = lanes(head)
    out = jnp.where(own, values, 0.0)
    for at, column in enumerate(extra):
        out = jnp.where(free == at, column, out)
    return out.astype(jnp.bfloat16)


def rows_with(values_t, head, extra):
    row = lax.broadcasted_iota(jnp.int32, (PAIR, 1), 0)
    own = (row < HD) if head == 0 else (row >= HD)
    free = row - (HD if head == 0 else 0)
    out = jnp.where(own, values_t, 0.0)
    for at, line in enumerate(extra):
        out = jnp.where(free == at, line, out)
    return out.astype(jnp.bfloat16)


def split_three(line):
    high = line.astype(jnp.bfloat16).astype(jnp.float32)
    rest = line - high
    middle = rest.astype(jnp.bfloat16).astype(jnp.float32)
    return high, middle, rest - middle


def forward_kernel(place_ref, valid_ref, q_ref, k_ref, v_ref, out_ref, lse_ref):
    shards, length, _ = q_ref.shape
    bias = key_bias(place_ref, valid_ref, length, shards)
    keys = k_ref[...].reshape(shards * length, PAIR).astype(jnp.float32)
    values = v_ref[...].reshape(shards * length, PAIR).astype(jnp.float32)
    keys_of = [augmented(keys, head, [bias]) for head in range(2)]
    values_of = [augmented(values, head, [1.0]).T for head in range(2)]
    for shard in range(shards):
        queries = q_ref[shard].astype(jnp.float32).T * HD**-0.5
        halves = []
        for head in range(2):
            scores = mat(keys_of[head], rows_with(queries, head, [1.0]))
            top = jnp.max(scores, axis=0, keepdims=True)
            weight = jnp.exp(scores - top).astype(jnp.bfloat16)
            part = mat(values_of[head], weight)
            at = HD * (1 - head)
            row_total = part[at : at + 1, :]
            halves.append(part[HD * head : HD * (head + 1), :] / row_total)
            lse_ref[0, 0, shard, head : head + 1, :] = top + jnp.log(row_total)
        out_ref[shard] = jnp.concatenate(halves, axis=0).T.astype(out_ref.dtype)


def backward_kernel(place_ref, valid_ref, q_ref, k_ref, v_ref, out_ref, lse_ref, da_ref, dq_ref, dk_ref, dv_ref):
    shards, length, _ = q_ref.shape
    bias = key_bias(place_ref, valid_ref, length, shards)
    keys = k_ref[...].reshape(shards * length, PAIR).astype(jnp.float32)
    values = v_ref[...].reshape(shards * length, PAIR).astype(jnp.float32)
    keys_of = [augmented(keys, head, [bias, 1.0, 1.0, 1.0]) for head in range(2)]
    values_of = [augmented(values, head, [1.0, 1.0, 1.0]) for head in range(2)]
    plain_keys = [augmented(keys, head, []).T for head in range(2)]
    dk = dv = None
    for shard in range(shards):
        queries = q_ref[shard].astype(jnp.float32) * HD**-0.5
        grads = da_ref[shard].astype(jnp.float32)
        queries_t, grads_t = queries.T, grads.T
        product = grads_t * out_ref[shard].astype(jnp.float32).T
        dq = None
        for head in range(2):
            lse = lse_ref[0, 0, shard, head : head + 1, :]
            delta = jnp.sum(product[HD * head : HD * (head + 1), :], axis=0, keepdims=True)
            scores = mat(keys_of[head], rows_with(queries_t, head, (1.0,) + split_three(-lse)))
            probs = jnp.exp(scores)
            moved = mat(values_of[head], rows_with(grads_t, head, split_three(-delta)))
            dscores = (probs * moved).astype(jnp.bfloat16)
            part_v = mat(probs.astype(jnp.bfloat16), augmented(grads, head, []))
            part_k = mat(dscores, augmented(queries, head, []))
            part_q = mat(plain_keys[head], dscores)
            dq = part_q if dq is None else dq + part_q
            dk = part_k if dk is None else dk + part_k
            dv = part_v if dv is None else dv + part_v
        dq_ref[shard] = (dq * HD**-0.5).T.astype(dq_ref.dtype)
    dk_ref[...] = dk.astype(dk_ref.dtype).reshape(dk_ref.shape)
    dv_ref[...] = dv.astype(dv_ref.dtype).reshape(dv_ref.shape)


def attention_specs(shards, length, pairs_all, first_pair):
    smem = pl.BlockSpec(memory_space=pltpu.SMEM)
    mixed = [
        pl.BlockSpec((shards, length, PAIR), lambda i, h, t=t: (0, i, t * pairs_all + first_pair + h))
        for t in range(3)
    ]
    plain = pl.BlockSpec((shards, length, PAIR), lambda i, h: (0, i, h))
    lse = pl.BlockSpec((1, 1, shards, 2, length), lambda i, h: (i, h, 0, 0, 0))
    return smem, mixed, plain, lse


def attend_forward(images, place, valid, mixed, first_pair, pairs):
    shards, rows, width3 = mixed.shape
    length = rows // images
    smem, block3, plain, lse = attention_specs(shards, length, width3 // 3 // PAIR, first_pair)
    work = shards * shards * rows * length * pairs
    return pl.pallas_call(
        forward_kernel,
        grid=(images, pairs),
        in_specs=[smem, smem] + block3,
        out_specs=[plain, lse],
        out_shape=[
            jax.ShapeDtypeStruct((shards, rows, pairs * PAIR), jnp.bfloat16),
            jax.ShapeDtypeStruct((images, pairs, shards, 2, length), jnp.float32),
        ],
        compiler_params=pltpu.CompilerParams(vmem_limit_bytes=40 * 2**20),
        cost_estimate=pl.CostEstimate(
            flops=8 * work * PAIR, bytes_accessed=8 * shards * rows * pairs * PAIR, transcendentals=2 * work,
        ),
    )(place, valid, mixed, mixed, mixed)


def attend_backward(images, place, valid, mixed, first_pair, pairs, attended, lse_in, da):
    shards, rows, width3 = mixed.shape
    length = rows // images
    smem, block3, plain, lse = attention_specs(shards, length, width3 // 3 // PAIR, first_pair)
    low = jax.ShapeDtypeStruct((shards, rows, pairs * PAIR), jnp.bfloat16)
    work = shards * shards * rows * length * pairs
    return pl.pallas_call(
        backward_kernel,
        grid=(images, pairs),
        in_specs=[smem, smem] + block3 + [plain, lse, plain],
        out_specs=[plain] * 3,
        out_shape=[low] * 3,
        compiler_params=pltpu.CompilerParams(vmem_limit_bytes=48 * 2**20),
        cost_estimate=pl.CostEstimate(
            flops=20 * work * PAIR, bytes_accessed=16 * shards * rows * pairs * PAIR, transcendentals=2 * work,
        ),
    )(place, valid, mixed, mixed, mixed, attended, lse_in, da)


def shift(values, shards, step):
    return lax.ppermute(values, "seq", [(i, (i + step) % shards) for i in range(shards)])


def everyone(values, shards, step_axis=0):
    return jnp.stack([values] + [shift(values, shards, -j) for j in range(1, shards)], axis=step_axis)


def in_order(values, shards, place):
    if shards == 2:
        other = shift(values, shards, 1)
        low = jnp.where(place == 0, values, other)
        high = jnp.where(place == 0, other, values)
        return jnp.stack([low, high])
    return lax.all_gather(values, "seq", axis=0)


def token_sum(values):
    return jnp.sum(values.astype(jnp.float32), axis=0)


MESH = pl.DeviceIdType.MESH


class Peers:
    def __init__(self, dps):
        self.dp = lax.axis_index("dp")
        self.seq = lax.axis_index("seq")
        self.levels = dps // 4
        self.z = self.dp // 4
        self.x = self.dp % 4 // 2
        self.core = self.dp % 2

    def up(self, step):
        return ((self.z + step) % self.levels * 4 + self.dp % 4, self.seq)

    def across(self):
        return (self.dp + 2 - 4 * self.x, self.seq)

    def sibling(self):
        return (self.dp + 1 - 2 * self.core, self.seq)

    def other(self):
        return (self.dp, 1 - self.seq)

    def all(self):
        return [self.up(s) for s in range(1, self.levels)] + [self.across(), self.sibling(), self.other()]

    def greet(self):
        barrier = pltpu.get_barrier_semaphore()
        for device in self.all():
            pl.semaphore_signal(barrier, inc=1, device_id=device, device_id_type=MESH)
        pl.semaphore_wait(barrier, len(self.all()))


def remote(src, dst, send, recv, device):
    return pltpu.make_async_remote_copy(
        src_ref=src, dst_ref=dst, send_sem=send, recv_sem=recv, device_id=device, device_id_type=MESH
    )


class Gather:
    def __init__(self, peers, src, full, sems):
        levels = peers.levels
        at = (peers.z, peers.x, peers.core)
        self.local = pltpu.make_async_copy(src, full.at[at], sems.at[0])
        self.first = [
            remote(src, full.at[at], sems.at[2 * s + 3], sems.at[2 * s + 4], peers.up(s)) for s in range(1, levels)
        ]
        column = full.at[:, peers.x, peers.core]
        self.second = remote(column, column, sems.at[1], sems.at[2], peers.across())
        half = full.at[:, :, peers.core]
        self.third = remote(half, half, sems.at[3], sems.at[4], peers.sibling())

    def start(self):
        self.local.start()
        for copy in self.first:
            copy.start()

    def cross(self):
        self.local.wait()
        for copy in self.first:
            copy.wait_recv()
        self.second.start()

    def share(self):
        self.second.wait_recv()
        self.third.start()

    def arrive(self):
        self.third.wait_recv()

    def finish(self):
        for copy in self.first + [self.second, self.third]:
            copy.wait_send()


def gather_sems(levels):
    return 2 * levels + 3


def attend_pair(valid_ref, mixed, att, lse_ref, pair, base):
    shards, length, width3 = mixed.shape
    part = width3 // 3

    def columns(t):
        return pl.ds(pl.multiple_of(t * part + pair * PAIR, PAIR), PAIR)

    row = lax.broadcasted_iota(jnp.int32, (shards * length, 1), 0)
    bias = jnp.where(row < valid_ref[0], 0.0, NEG_FILL).astype(jnp.float32)
    keys = mixed[:, :, columns(1)].reshape(shards * length, PAIR).astype(jnp.float32)
    values = mixed[:, :, columns(2)].reshape(shards * length, PAIR).astype(jnp.float32)
    keys_of = [augmented(keys, head, [bias]) for head in range(2)]
    values_of = [augmented(values, head, [1.0]).T for head in range(2)]
    out_columns = pl.ds(pl.multiple_of(base + pair * PAIR, PAIR), PAIR)
    for shard in range(shards):
        queries = mixed[shard, :, columns(0)].astype(jnp.float32).T * HD**-0.5
        halves = []
        for head in range(2):
            scores = mat(keys_of[head], rows_with(queries, head, [1.0]))
            top = jnp.max(scores, axis=0, keepdims=True)
            weight = jnp.exp(scores - top).astype(jnp.bfloat16)
            product = mat(values_of[head], weight)
            at = HD * (1 - head)
            row_total = product[at : at + 1, :]
            halves.append(product[HD * head : HD * (head + 1), :] / row_total)
            lse_ref[pair, shard, head : head + 1, :] = top + jnp.log(row_total)
        att[shard, :, out_columns] = jnp.concatenate(halves, axis=0).T.astype(att.dtype)


ROW_TILE = 192
COL_TILE = 512


def forward_layer(
    valid_ref, tokens, cotangent, w_qkv, w_out, w_up, w_down, small,
    dy_out, first_out, mixed_out, att_out, lse_ref, resid_out, second_out, act_out, slope_out,
    q_out, k_out, v_out, o_out, up_out, down_out, rows_ref, bup_ref,
    tok, first, mixed, att, resid, second, act, slope, fsmall, fq, fk, fv, fo, fup, fdown, my_up, gsems, sems,
):
    levels = fq.shape[0]
    peers = Peers(4 * levels)
    p = peers.seq
    length, width = tokens.shape
    part = width // 2
    sub = fdown.shape[3]
    shard_rows = w_out.shape[0]
    peers.greet()

    send_tok = remote(tokens, tok.at[p], sems.at[0], sems.at[1], peers.other())
    send_tok.start()
    gathers = []
    own = lambda t: w_qkv.at[:, pl.ds(pl.multiple_of(t * width + p * part, PAIR), part)]
    sources = [
        small, own(0), own(1), own(2), w_out, my_up, w_down.at[pl.ds(pl.multiple_of(p * sub, 16), sub)]
    ]
    fulls = [fsmall, fq, fk, fv, fo, fup, fdown]
    for i, (src, full) in enumerate(zip(sources, fulls)):
        gathers.append(Gather(peers, src, full, gsems.at[i]))
    g_small, g_q, g_k, g_v, g_out, g_up, g_down = gathers
    for g in (g_small, g_q, g_k, g_v):
        g.start()
    for d in range(4 * levels):
        my_up[:, d * sub : (d + 1) * sub] = w_up[:, pl.ds(pl.multiple_of((2 * d + p) * sub, PAIR), sub)]

    own_tok = pltpu.make_async_copy(tokens, tok.at[p], sems.at[2])
    own_tok.start()
    own_dy = pltpu.make_async_copy(cotangent, dy_out.at[p], sems.at[3])
    own_dy.start()

    def normed(shard):
        @pl.loop(0, length // ROW_TILE)
        def _(i):
            at = pl.ds(pl.multiple_of(i * ROW_TILE, 16), ROW_TILE)
            resid[shard, at, :] = norm_parts(tok[shard, at, :].astype(jnp.float32))[0]

    g_small.cross()
    g_q.cross()
    own_tok.wait()
    normed(p)
    g_k.cross()
    g_v.cross()
    g_out.start()
    g_small.share()
    g_q.share()
    g_k.share()
    send_tok.wait_recv()
    send_dy = remote(cotangent, dy_out.at[p], sems.at[4], sems.at[5], peers.other())
    send_dy.start()
    normed(1 - p)
    g_small.arrive()
    vectors = fsmall[:, :, :, 0:shard_rows, :].reshape(width, SMALL).astype(jnp.float32).T
    rows_ref[...] = vectors[0:16, :]
    for d in range(4 * levels):
        at = (d // 4, d % 4 // 2, d % 2)
        pair_rows = fsmall[at + (slice(shard_rows, shard_rows + 16),)].astype(jnp.float32)
        bup_ref[0:1, d * sub : (d + 1) * sub] = jnp.where(p == 0, pair_rows[0:1, :sub], pair_rows[1:2, :sub])

    for shard in range(2):
        @pl.loop(0, length // ROW_TILE)
        def _(i):
            at = pl.ds(pl.multiple_of(i * ROW_TILE, 16), ROW_TILE)
            first[shard, at, :] = (resid[shard, at, :] * rows_ref[0:1, :] + rows_ref[2:3, :]).astype(jnp.bfloat16)

    own_columns = pl.ds(pl.multiple_of(p * part, PAIR), part)

    def project(t, full, bias):
        weight = full[...].reshape(width, part)
        @pl.loop(0, 2)
        def _(shard):
            out = mat(first[shard], weight)
            if bias is not None:
                out = out + rows_ref[bias : bias + 1, own_columns]
            mixed[shard, :, t * part : (t + 1) * part] = out.astype(jnp.bfloat16)

    saves = []

    def save(src, dst):
        copy = pltpu.make_async_copy(src, dst, sems.at[16 + len(saves)])
        saves.append(copy)
        copy.start()

    save(first, first_out)
    g_v.share()
    g_q.arrive()
    project(0, fq, 3)
    g_out.cross()
    g_up.start()
    g_k.arrive()
    project(1, fk, None)
    g_v.arrive()
    project(2, fv, 4)
    save(mixed, mixed_out)
    save(fq, q_out)
    save(fk, k_out)
    save(fv, v_out)

    pairs = part // PAIR
    att_copies = []
    for pair in range(pairs):
        columns = pl.ds(pl.multiple_of(p * part + pair * PAIR, PAIR), PAIR)
        att_copies.append(
            remote(
                att.at[:, :, columns], att.at[:, :, columns], sems.at[8 + 2 * pair], sems.at[9 + 2 * pair],
                peers.other(),
            )
        )

    @pl.loop(0, pairs)
    def _(pair):
        attend_pair(valid_ref, mixed, att, lse_ref, pair, p * part)
        for i in range(pairs):
            @pl.when(pair == i)
            def _():
                att_copies[i].start()
                if i == 0:
                    g_out.share()
                if i == min(1, pairs - 1):
                    g_up.cross()
                    g_down.start()

    g_out.arrive()
    save(fo, o_out)
    for copy in att_copies:
        copy.wait_recv()
    save(att, att_out)
    out_weight = fo[...].reshape(width, width)

    def finish_rows(shard):
        @pl.loop(0, length // ROW_TILE)
        def _(i):
            at = pl.ds(pl.multiple_of(i * ROW_TILE, 16), ROW_TILE)
            value = mat(att[shard, at, :], out_weight) + rows_ref[5:6, :] + tok[shard, at, :].astype(jnp.float32)
            resid[shard, at, :] = value
            hat, _ = norm_parts(value)
            second[shard, at, :] = (hat * rows_ref[1:2, :] + rows_ref[6:7, :]).astype(jnp.bfloat16)

    finish_rows(0)
    finish_rows(1)
    save(resid.at[p], resid_out)
    save(second, second_out)
    g_up.share()
    g_down.cross()
    g_up.arrive()
    save(fup, up_out)
    own_hidden = act.shape[2]
    tiles = own_hidden // COL_TILE

    @pl.loop(0, 2 * tiles)
    def _(step):
        shard = step // tiles
        at = pl.ds(pl.multiple_of(step % tiles * COL_TILE, PAIR), COL_TILE)
        upward = mat(second[shard], fup[:, :, :, :, at].reshape(width, COL_TILE)) + bup_ref[0:1, at]
        cdf = 0.5 * (1.0 + lax.erf(upward * 0.5**0.5))
        act[shard, :, at] = (upward * cdf).astype(jnp.bfloat16)
        value = cdf + upward * (jnp.exp(-0.5 * upward * upward) * 0.3989422804014327)
        slope[shard, :, at] = value.astype(jnp.bfloat16)

    save(act, act_out)
    save(slope, slope_out)
    g_down.share()
    g_down.arrive()
    save(fdown, down_out)
    send_tok.wait_send()
    send_dy.wait()
    own_dy.wait()
    for copy in att_copies:
        copy.wait_send()
    for g in gathers:
        g.finish()
    for copy in saves:
        copy.wait()


def run_forward(dps, tokens, cotangent, w_qkv, w_out, w_up, w_down, small, valid):
    length, width = tokens.shape
    levels = dps // 4
    part = width // 2
    shard_rows = w_out.shape[0]
    own_hidden = w_up.shape[1] // 2
    sub = w_down.shape[0] // 2
    pairs = part // PAIR
    bf, f32 = jnp.bfloat16, jnp.float32
    any_spec = pl.BlockSpec(memory_space=pl.ANY)
    vmem = pl.BlockSpec(memory_space=pltpu.VMEM)
    smem = pl.BlockSpec(memory_space=pltpu.SMEM)
    grid = (levels, 2, 2)
    whole = [
        ((2, length, width), bf),
        ((2, length, width), bf),
        ((2, length, 3 * part), bf),
        ((2, length, width), bf),
        ((pairs, 2, 2, length), f32),
        ((length, width), f32),
        ((2, length, width), bf),
        ((2, length, own_hidden), bf),
        ((2, length, own_hidden), bf),
        (grid + (shard_rows, part), bf),
        (grid + (shard_rows, part), bf),
        (grid + (shard_rows, part), bf),
        (grid + (shard_rows, width), bf),
        (grid + (shard_rows, own_hidden), bf),
        (grid + (sub, width), bf),
        ((16, width), f32),
        ((8, own_hidden), f32),
    ]
    in_vmem = (4, 15, 16)
    scratch = [
        pltpu.VMEM((2, length, width), bf),
        pltpu.VMEM((2, length, width), bf),
        pltpu.VMEM((2, length, 3 * part), bf),
        pltpu.VMEM((2, length, width), bf),
        pltpu.VMEM((2, length, width), f32),
        pltpu.VMEM((2, length, width), bf),
        pltpu.VMEM((2, length, own_hidden), bf),
        pltpu.VMEM((2, length, own_hidden), bf),
        pltpu.VMEM(grid + (shard_rows + 16, SMALL), bf),
        pltpu.VMEM(grid + (shard_rows, part), bf),
        pltpu.VMEM(grid + (shard_rows, part), bf),
        pltpu.VMEM(grid + (shard_rows, part), bf),
        pltpu.VMEM(grid + (shard_rows, width), bf),
        pltpu.VMEM(grid + (shard_rows, own_hidden), bf),
        pltpu.VMEM(grid + (sub, width), bf),
        pltpu.VMEM((shard_rows, own_hidden), bf),
        pltpu.SemaphoreType.DMA((7, gather_sems(levels))),
        pltpu.SemaphoreType.DMA((32,)),
    ]
    return pl.pallas_call(
        forward_layer,
        in_specs=[smem, any_spec, any_spec, vmem, vmem, vmem, vmem, vmem],
        out_specs=[vmem if i in in_vmem else any_spec for i in range(len(whole))],
        out_shape=[jax.ShapeDtypeStruct(*s) for s in whole],
        scratch_shapes=scratch,
        compiler_params=pltpu.CompilerParams(
            vmem_limit_bytes=60 * 2**20, collective_id=0, has_side_effects=True
        ),
        cost_estimate=pl.CostEstimate(flops=3 * 10**10, bytes_accessed=8 * 10**7, transcendentals=2 * 10**7),
    )(valid, tokens, cotangent, w_qkv, w_out, w_up, w_down, small)


def per_device_pair(tokens, w_qkv, w_out, w_up, w_down, gains, biases, up_bias, valid, cotangent):
    images, length, width = tokens.shape
    rows = length
    shard_rows = w_qkv.shape[0]
    hidden = w_up.shape[1]
    ups = up_bias.shape[0] // shard_rows
    dps = lax.axis_size("dp")
    at = lax.axis_index("seq").astype(jnp.int32)
    part = width // 2
    sub = w_down.shape[0] // 2
    pairs = part // PAIR
    own_hidden = hidden // 2
    scatter = functools.partial(lax.psum_scatter, axis_name="dp", scatter_dimension=0, tiled=True)

    def pick(values, axis, where=at):
        return lax.dynamic_index_in_dim(values, where, axis, keepdims=False)

    smalls = jnp.concatenate([gains, biases], axis=1)
    smalls = jnp.concatenate(
        [
            jnp.pad(smalls, ((0, 0), (0, SMALL - smalls.shape[1]))),
            jnp.pad(up_bias.reshape(2, sub), ((0, 14), (0, 0))),
        ],
        axis=0,
    )
    flat_tokens = tokens.reshape(rows, width)
    flat_grad = cotangent.reshape(rows, width)
    (
        dy, first, mixed, att, lse, residual, second, act, slope, fq, fk, fv, fo, fup, fdown, vectors, _
    ) = run_forward(dps, flat_tokens, flat_grad, w_qkv, w_out, w_up, w_down, smalls, valid)
    gain_one, gain_two = vectors[0], vectors[1]
    bias_down = vectors[7]
    full_qkv = jnp.concatenate([f.reshape(width, part) for f in (fq, fk, fv)], axis=1)
    full_out = fo.reshape(width, width)
    full_up = fup.reshape(width, own_hidden)
    full_down = fdown.reshape(own_hidden, width)
    flat = lambda v: v.reshape(2 * rows, v.shape[-1])

    grad_act = dot_f32(flat(dy), full_down, ((1,), (1,)))
    grad_upward = (grad_act * flat(slope).astype(jnp.float32)).astype(jnp.bfloat16)

    def summed(left, right, dims):
        left = left.reshape(2, rows, -1)
        mine = dot_f32(pick(left, 0), right, dims)
        theirs = dot_f32(pick(left, 0, 1 - at), right, dims).astype(jnp.bfloat16)
        return mine + shift(theirs, 2, 1).astype(jnp.float32)

    grad_second = summed(grad_upward, full_up, ((1,), (1,)))
    grad_down = dot_f32(flat(act), flat(dy), ((0,), (0,))).astype(jnp.bfloat16)
    piece_down = scatter(grad_down)
    grad_up = dot_f32(flat(second), grad_upward, ((0,), (0,))).astype(jnp.bfloat16)
    grad_up, piece_down = lax.optimization_barrier((grad_up, piece_down))
    piece_up = scatter(grad_up)

    own_hat, inverse_two = norm_parts(residual)
    grad_resid = flat_grad.astype(jnp.float32) + norm_back(own_hat, inverse_two, gain_two, grad_second)
    grad_gain_two, grad_bias_two = token_sum(grad_second * own_hat), token_sum(grad_second)
    grad_branch = grad_resid.astype(jnp.bfloat16)
    grad_merged = dot_f32(grad_branch, full_out, ((1,), (1,))).astype(jnp.bfloat16).reshape(rows, 2, part)
    own_merged = pick(grad_merged, 1)
    other_merged = shift(pick(grad_merged, 1, 1 - at), 2, 1)
    received = jnp.stack([jnp.where(at == 0, own_merged, other_merged), jnp.where(at == 0, other_merged, own_merged)])

    grad_out = dot_f32(pick(att, 0), grad_branch, ((0,), (0,))).astype(jnp.bfloat16)
    grad_out, piece_up = lax.optimization_barrier((grad_out, piece_up))
    piece_out = scatter(grad_out)

    own_att = pick(att.reshape(2, rows, 2, part), 2)
    back = attend_backward(1, jnp.zeros((1,), jnp.int32), valid, mixed, 0, pairs, own_att, lse[None], received)
    grad_mixed = jnp.concatenate([flat(b) for b in back], axis=1)
    grad_first = summed(grad_mixed, full_qkv, ((1,), (1,)))
    grad_qkv = dot_f32(flat(first), grad_mixed, ((0,), (0,))).astype(jnp.bfloat16)

    hat_one, inverse_one = norm_parts(flat_tokens.astype(jnp.float32))
    grad_tokens = grad_resid + norm_back(hat_one, inverse_one, gain_one, grad_first)
    grad_gain_one, grad_bias_one = token_sum(grad_first * hat_one), token_sum(grad_first)

    def spread(values, before):
        out = jnp.zeros((before, 2, values.size // before), jnp.float32)
        return lax.dynamic_update_slice_in_dim(out, values.reshape(before, 1, -1), at, 1).reshape(-1)

    bias_sums = token_sum(grad_mixed)
    small_grads = jnp.stack(
        [
            grad_gain_one, grad_gain_two, grad_bias_one, spread(bias_sums[:part], 1), spread(bias_sums[2 * part :], 1),
            token_sum(grad_branch), grad_bias_two, token_sum(flat_grad),
        ],
        axis=1,
    )
    up_sums = spread(token_sum(grad_upward), dps).reshape(width, ups)
    small_grads = jnp.concatenate([small_grads, up_sums], axis=1)
    small_grads = jnp.pad(small_grads, ((0, 0), (0, SMALL - small_grads.shape[1])))
    grad_qkvs = jnp.concatenate([grad_qkv, small_grads.astype(jnp.bfloat16)], axis=1)
    grad_qkvs, piece_out = lax.optimization_barrier((grad_qkvs, piece_out))
    piece_qkvs = scatter(grad_qkvs)

    output = summed(flat(act), full_down, ((1,), (0,)))
    out_tokens = (residual + output + bias_down).astype(jnp.bfloat16)

    total_down = in_order(piece_down, 2, at).astype(jnp.float32).reshape(2 * sub, width)
    total_up = in_order(piece_up.reshape(shard_rows, dps, sub), 2, at).astype(jnp.float32)
    total_up = total_up.transpose(1, 2, 0, 3).reshape(shard_rows, hidden)
    total_out = in_order(piece_out, 2, at).astype(jnp.float32).sum(0)
    every_qkvs = in_order(piece_qkvs, 2, at).astype(jnp.float32)
    total_qkv = every_qkvs[:, :, : 3 * part].reshape(2, shard_rows, 3, part)
    total_qkv = total_qkv.transpose(1, 2, 0, 3).reshape(shard_rows, 3 * width)
    total_small = every_qkvs[:, :, 3 * part :].sum(0)
    return (
        out_tokens.reshape(tokens.shape),
        grad_tokens.reshape(tokens.shape),
        total_qkv,
        total_out,
        total_up,
        total_down,
        total_small[:, :2],
        total_small[:, 2:8],
        total_small[:, 8 : 8 + ups].reshape(-1),
    )


def per_device(tokens, w_qkv, w_out, w_up, w_down, gains, biases, up_bias, valid, cotangent):
    images, length, width = tokens.shape
    rows = images * length
    shard_rows = w_qkv.shape[0]
    hidden = w_up.shape[1]
    ups = up_bias.shape[0] // shard_rows
    shards = lax.axis_size("seq")
    dps = lax.axis_size("dp")
    at = lax.axis_index("seq").astype(jnp.int32)
    place = at.reshape(1)
    part = width // shards
    own_hidden = hidden // shards
    sub = w_down.shape[0] // shards
    pairs_all = part // PAIR

    gather = functools.partial(lax.all_gather, axis_name="dp", axis=0, tiled=True)
    scatter = functools.partial(lax.psum_scatter, axis_name="dp", scatter_dimension=0, tiled=True)

    def pick(values, axis):
        return lax.dynamic_index_in_dim(values, at, axis, keepdims=False)

    smalls = jnp.concatenate([gains, biases, up_bias.reshape(shard_rows, ups)], axis=1)
    smalls = jnp.pad(smalls, ((0, 0), (0, SMALL - smalls.shape[1])))
    part_qkv = pick(w_qkv.reshape(shard_rows, 3, shards, part), 2).reshape(shard_rows, 3 * part)
    part_up = pick(w_up.reshape(shard_rows, dps, shards, sub), 2).reshape(shard_rows, own_hidden)
    part_down = pick(w_down.reshape(shards, sub, width), 0)
    full_qkvs = gather(jnp.concatenate([part_qkv, smalls], axis=1))
    w_out, full_qkvs = lax.optimization_barrier((w_out, full_qkvs))
    full_out = gather(w_out)
    part_up, full_out = lax.optimization_barrier((part_up, full_out))
    full_up = gather(part_up)
    part_down, full_up = lax.optimization_barrier((part_down, full_up))
    full_down = gather(part_down)

    flat_tokens = tokens.reshape(rows, width)
    flat_grad = cotangent.reshape(rows, width)
    all_tokens = everyone(flat_tokens, shards)
    flat_grad, all_tokens = lax.optimization_barrier((flat_grad, all_tokens))
    all_grad = everyone(flat_grad, shards).reshape(shards * rows, width)

    full_qkv = full_qkvs[:, : 3 * part]
    small = full_qkvs[:, 3 * part :].astype(jnp.float32).T
    gain_one, gain_two = small[0], small[1]
    bias_one, bias_q, bias_v, bias_out, bias_two, bias_down = (small[2 + i] for i in range(6))
    bias_up = pick(small[8 : 8 + ups].T.reshape(dps, shards, sub), 1).reshape(-1)
    bias_mixed = jnp.concatenate(
        [pick(bias_q.reshape(shards, part), 0), jnp.zeros((part,), jnp.float32), pick(bias_v.reshape(shards, part), 0)]
    )

    every_tokens = all_tokens.reshape(shards * rows, width).astype(jnp.float32)
    hat_one, inverse_one = norm_parts(every_tokens)
    first = (hat_one * gain_one + bias_one).astype(jnp.bfloat16)
    mixed = (mat(first, full_qkv) + bias_mixed).astype(jnp.bfloat16).reshape(shards, rows, 3 * part)

    groups = GROUPS if pairs_all % GROUPS == 0 else 1
    pairs = pairs_all // groups
    wide = pairs * PAIR
    forward = [attend_forward(images, place, valid, mixed, g * pairs, pairs) for g in range(groups)]
    blocks = []
    for j in range(shards):
        for g in range(groups):
            attended = forward[g][0]
            if j > 0:
                attended = jnp.roll(shift(attended, shards, -j), j, axis=0)
            blocks.append(attended.reshape(shards * rows, wide))
    merged = jnp.concatenate(blocks, axis=1)
    turned_out = jnp.roll(full_out, -at * part, axis=0)

    branch = mat(merged, turned_out) + bias_out
    residual = every_tokens + branch
    hat_two, inverse_two = norm_parts(residual)
    second = (hat_two * gain_two + bias_two).astype(jnp.bfloat16)
    upward = mat(second, full_up) + bias_up
    cdf = 0.5 * (1.0 + lax.erf(upward * 0.5**0.5))
    activated = (upward * cdf).astype(jnp.bfloat16)
    slope = cdf + upward * (jnp.exp(-0.5 * upward * upward) * 0.3989422804014327)
    slope = slope.astype(jnp.bfloat16)

    grad_act = dot_f32(all_grad, full_down, ((1,), (1,)))
    grad_upward = (grad_act * slope.astype(jnp.float32)).astype(jnp.bfloat16)

    def summed(left, right, dims):
        parts = [
            dot_f32(left[j * rows : (j + 1) * rows], right, dims) for j in range(shards)
        ]
        total = parts[0]
        for j in range(1, shards):
            total = total + shift(parts[j].astype(jnp.bfloat16), shards, j).astype(jnp.float32)
        return total

    grad_second = summed(grad_upward, full_up, ((1,), (1,)))
    grad_down = dot_f32(activated, all_grad, ((0,), (0,))).astype(jnp.bfloat16)
    piece_down = scatter(grad_down)
    grad_up = dot_f32(second, grad_upward, ((0,), (0,))).astype(jnp.bfloat16)
    grad_up, piece_down = lax.optimization_barrier((grad_up, piece_down))
    piece_up = scatter(grad_up)

    own_hat = hat_two[:rows]
    grad_resid = flat_grad.astype(jnp.float32) + norm_back(own_hat, inverse_two[:rows], gain_two, grad_second)
    grad_gain_two, grad_bias_two = token_sum(grad_second * own_hat), token_sum(grad_second)
    grad_branch = grad_resid.astype(jnp.bfloat16)
    grad_merged = dot_f32(grad_branch, turned_out, ((1,), (1,))).astype(jnp.bfloat16)
    received = [None] * shards
    for g in range(groups):
        lo = g * wide
        blocks = [grad_merged[:, lo : lo + wide]] + [None] * (shards - 1)
        for j in range(1, shards):
            blocks[shards - j] = shift(grad_merged[:, j * part + lo : j * part + lo + wide], shards, j)
        received[g] = jnp.stack(blocks)

    grad_out = dot_f32(merged[:rows], grad_branch, ((0,), (0,))).astype(jnp.bfloat16)
    grad_out = jnp.roll(grad_out, at * part, axis=0)
    grad_out, piece_up = lax.optimization_barrier((grad_out, piece_up))
    piece_out = scatter(grad_out)

    backs = [
        attend_backward(images, place, valid, mixed, g * pairs, pairs, *forward[g], received[g]) for g in range(groups)
    ]
    grad_mixed = jnp.concatenate(
        [back[t].reshape(shards * rows, wide) for t in range(3) for back in backs], axis=1
    )
    grad_first = summed(grad_mixed, full_qkv, ((1,), (1,)))
    grad_qkv = dot_f32(first, grad_mixed, ((0,), (0,))).astype(jnp.bfloat16)

    grad_tokens = grad_resid + norm_back(hat_one[:rows], inverse_one[:rows], gain_one, grad_first)
    grad_gain_one, grad_bias_one = token_sum(grad_first * hat_one[:rows]), token_sum(grad_first)

    def spread(values, before):
        out = jnp.zeros((before, shards, values.size // before), jnp.float32)
        return lax.dynamic_update_slice_in_dim(out, values.reshape(before, 1, -1), at, 1).reshape(-1)

    bias_sums = token_sum(grad_mixed)
    small_grads = jnp.stack(
        [
            grad_gain_one, grad_gain_two, grad_bias_one, spread(bias_sums[:part], 1), spread(bias_sums[2 * part :], 1),
            token_sum(grad_branch), grad_bias_two, token_sum(flat_grad),
        ],
        axis=1,
    )
    up_sums = spread(token_sum(grad_upward), dps).reshape(width, ups)
    small_grads = jnp.concatenate([small_grads, up_sums], axis=1)
    small_grads = jnp.pad(small_grads, ((0, 0), (0, SMALL - small_grads.shape[1])))
    grad_qkvs = jnp.concatenate([grad_qkv, small_grads.astype(jnp.bfloat16)], axis=1)
    grad_qkvs, piece_out = lax.optimization_barrier((grad_qkvs, piece_out))
    piece_qkvs = scatter(grad_qkvs)

    output = summed(activated, full_down, ((1,), (0,)))
    out_tokens = (residual[:rows] + output + bias_down).astype(jnp.bfloat16)

    total_down = in_order(piece_down, shards, at).astype(jnp.float32).reshape(shards * sub, width)
    total_up = in_order(piece_up.reshape(shard_rows, dps, sub), shards, at).astype(jnp.float32)
    total_up = total_up.transpose(1, 2, 0, 3).reshape(shard_rows, hidden)
    total_out = in_order(piece_out, shards, at).astype(jnp.float32).sum(0)
    every_qkvs = in_order(piece_qkvs, shards, at).astype(jnp.float32)
    total_qkv = every_qkvs[:, :, : 3 * part].reshape(shards, shard_rows, 3, part)
    total_qkv = total_qkv.transpose(1, 2, 0, 3).reshape(shard_rows, 3 * width)
    total_small = every_qkvs[:, :, 3 * part :].sum(0)
    return (
        out_tokens.reshape(tokens.shape),
        grad_tokens.reshape(tokens.shape),
        total_qkv,
        total_out,
        total_up,
        total_down,
        total_small[:, :2],
        total_small[:, 2:8],
        total_small[:, 8 : 8 + ups].reshape(-1),
    )


def solution(mesh):
    paired = mesh.shape["seq"] == 2 and mesh.shape["dp"] == 16
    return jax.shard_map(
        per_device_pair if paired else per_device,
        mesh=mesh,
        in_specs=(
            P("dp", "seq", None),
            P("dp", None),
            P("dp", None),
            P("dp", None),
            P("dp", None),
            P("dp", None),
            P("dp", None),
            P("dp"),
            P("dp"),
            P("dp", "seq", None),
        ),
        out_specs=(
            P("dp", "seq", None),
            P("dp", "seq", None),
            P("dp", None),
            P("dp", None),
            P("dp", None),
            P("dp", None),
            P("dp", None),
            P("dp", None),
            P("dp"),
        ),
        check_vma=False,
    )
```

```python
import functools

import jax
import jax.numpy as jnp
from jax import lax
from jax.experimental import pallas as pl
from jax.experimental.pallas import tpu as pltpu
from jax.sharding import PartitionSpec as P

HD = 64
PAIR = 2 * HD
EPSILON = 1e-06
NEG_FILL = -1e30
SMALL = 128
GROUPS = 2


def dot_f32(a, b, dims):
    return lax.dot_general(a, b, (dims, ((), ())), preferred_element_type=jnp.float32)


def mat(a, b):
    return dot_f32(a, b, ((1,), (0,)))


def norm_parts(values):
    average = jnp.mean(values, axis=-1, keepdims=True)
    centered = values - average
    variance = jnp.mean(centered * centered, axis=-1, keepdims=True)
    inverse = lax.rsqrt(variance + EPSILON)
    return centered * inverse, inverse


def norm_back(hat, inverse, scales, grad):
    scaled = grad * scales
    first = jnp.mean(scaled, axis=-1, keepdims=True)
    second = jnp.mean(scaled * hat, axis=-1, keepdims=True)
    return inverse * (scaled - first - hat * second)


def lanes(head):
    lane = lax.broadcasted_iota(jnp.int32, (1, PAIR), 1)
    own = (lane < HD) if head == 0 else (lane >= HD)
    return own, lane - (HD if head == 0 else 0)


def key_bias(place_ref, valid_ref, length, shards):
    row = lax.broadcasted_iota(jnp.int32, (shards * length, 1), 0)
    position = row + place_ref[0] * length
    position = jnp.where(position >= shards * length, position - shards * length, position)
    allowed = position < valid_ref[pl.program_id(0)]
    return jnp.where(allowed, 0.0, NEG_FILL).astype(jnp.float32)


def augmented(values, head, extra):
    own, free = lanes(head)
    out = jnp.where(own, values, 0.0)
    for at, column in enumerate(extra):
        out = jnp.where(free == at, column, out)
    return out.astype(jnp.bfloat16)


def rows_with(values_t, head, extra):
    row = lax.broadcasted_iota(jnp.int32, (PAIR, 1), 0)
    own = (row < HD) if head == 0 else (row >= HD)
    free = row - (HD if head == 0 else 0)
    out = jnp.where(own, values_t, 0.0)
    for at, line in enumerate(extra):
        out = jnp.where(free == at, line, out)
    return out.astype(jnp.bfloat16)


def split_three(line):
    high = line.astype(jnp.bfloat16).astype(jnp.float32)
    rest = line - high
    middle = rest.astype(jnp.bfloat16).astype(jnp.float32)
    return high, middle, rest - middle


def forward_kernel(place_ref, valid_ref, q_ref, k_ref, v_ref, out_ref, lse_ref):
    shards, length, _ = q_ref.shape
    bias = key_bias(place_ref, valid_ref, length, shards)
    keys = k_ref[...].reshape(shards * length, PAIR).astype(jnp.float32)
    values = v_ref[...].reshape(shards * length, PAIR).astype(jnp.float32)
    keys_of = [augmented(keys, head, [bias]) for head in range(2)]
    values_of = [augmented(values, head, [1.0]).T for head in range(2)]
    for shard in range(shards):
        queries = q_ref[shard].astype(jnp.float32).T * HD**-0.5
        halves = []
        for head in range(2):
            scores = mat(keys_of[head], rows_with(queries, head, [1.0]))
            top = jnp.max(scores, axis=0, keepdims=True)
            weight = jnp.exp(scores - top).astype(jnp.bfloat16)
            part = mat(values_of[head], weight)
            at = HD * (1 - head)
            row_total = part[at : at + 1, :]
            halves.append(part[HD * head : HD * (head + 1), :] / row_total)
            lse_ref[0, 0, shard, head : head + 1, :] = top + jnp.log(row_total)
        out_ref[shard] = jnp.concatenate(halves, axis=0).T.astype(out_ref.dtype)


def backward_kernel(place_ref, valid_ref, q_ref, k_ref, v_ref, out_ref, lse_ref, da_ref, dq_ref, dk_ref, dv_ref):
    shards, length, _ = q_ref.shape
    bias = key_bias(place_ref, valid_ref, length, shards)
    keys = k_ref[...].reshape(shards * length, PAIR).astype(jnp.float32)
    values = v_ref[...].reshape(shards * length, PAIR).astype(jnp.float32)
    keys_of = [augmented(keys, head, [bias, 1.0, 1.0, 1.0]) for head in range(2)]
    values_of = [augmented(values, head, [1.0, 1.0, 1.0]) for head in range(2)]
    plain_keys = [augmented(keys, head, []).T for head in range(2)]
    dk = dv = None
    for shard in range(shards):
        queries = q_ref[shard].astype(jnp.float32) * HD**-0.5
        grads = da_ref[shard].astype(jnp.float32)
        queries_t, grads_t = queries.T, grads.T
        product = grads_t * out_ref[shard].astype(jnp.float32).T
        dq = None
        for head in range(2):
            lse = lse_ref[0, 0, shard, head : head + 1, :]
            delta = jnp.sum(product[HD * head : HD * (head + 1), :], axis=0, keepdims=True)
            scores = mat(keys_of[head], rows_with(queries_t, head, (1.0,) + split_three(-lse)))
            probs = jnp.exp(scores)
            moved = mat(values_of[head], rows_with(grads_t, head, split_three(-delta)))
            dscores = (probs * moved).astype(jnp.bfloat16)
            part_v = mat(probs.astype(jnp.bfloat16), augmented(grads, head, []))
            part_k = mat(dscores, augmented(queries, head, []))
            part_q = mat(plain_keys[head], dscores)
            dq = part_q if dq is None else dq + part_q
            dk = part_k if dk is None else dk + part_k
            dv = part_v if dv is None else dv + part_v
        dq_ref[shard] = (dq * HD**-0.5).T.astype(dq_ref.dtype)
    dk_ref[...] = dk.astype(dk_ref.dtype).reshape(dk_ref.shape)
    dv_ref[...] = dv.astype(dv_ref.dtype).reshape(dv_ref.shape)


def attention_specs(shards, length, pairs_all, first_pair):
    smem = pl.BlockSpec(memory_space=pltpu.SMEM)
    mixed = [
        pl.BlockSpec((shards, length, PAIR), lambda i, h, t=t: (0, i, t * pairs_all + first_pair + h))
        for t in range(3)
    ]
    plain = pl.BlockSpec((shards, length, PAIR), lambda i, h: (0, i, h))
    lse = pl.BlockSpec((1, 1, shards, 2, length), lambda i, h: (i, h, 0, 0, 0))
    return smem, mixed, plain, lse


def attend_forward(images, place, valid, mixed, first_pair, pairs):
    shards, rows, width3 = mixed.shape
    length = rows // images
    smem, block3, plain, lse = attention_specs(shards, length, width3 // 3 // PAIR, first_pair)
    work = shards * shards * rows * length * pairs
    return pl.pallas_call(
        forward_kernel,
        grid=(images, pairs),
        in_specs=[smem, smem] + block3,
        out_specs=[plain, lse],
        out_shape=[
            jax.ShapeDtypeStruct((shards, rows, pairs * PAIR), jnp.bfloat16),
            jax.ShapeDtypeStruct((images, pairs, shards, 2, length), jnp.float32),
        ],
        compiler_params=pltpu.CompilerParams(vmem_limit_bytes=40 * 2**20),
        cost_estimate=pl.CostEstimate(
            flops=8 * work * PAIR, bytes_accessed=8 * shards * rows * pairs * PAIR, transcendentals=2 * work,
        ),
    )(place, valid, mixed, mixed, mixed)


def attend_backward(images, place, valid, mixed, first_pair, pairs, attended, lse_in, da):
    shards, rows, width3 = mixed.shape
    length = rows // images
    smem, block3, plain, lse = attention_specs(shards, length, width3 // 3 // PAIR, first_pair)
    low = jax.ShapeDtypeStruct((shards, rows, pairs * PAIR), jnp.bfloat16)
    work = shards * shards * rows * length * pairs
    return pl.pallas_call(
        backward_kernel,
        grid=(images, pairs),
        in_specs=[smem, smem] + block3 + [plain, lse, plain],
        out_specs=[plain] * 3,
        out_shape=[low] * 3,
        compiler_params=pltpu.CompilerParams(vmem_limit_bytes=48 * 2**20),
        cost_estimate=pl.CostEstimate(
            flops=20 * work * PAIR, bytes_accessed=16 * shards * rows * pairs * PAIR, transcendentals=2 * work,
        ),
    )(place, valid, mixed, mixed, mixed, attended, lse_in, da)


def shift(values, shards, step):
    return lax.ppermute(values, "seq", [(i, (i + step) % shards) for i in range(shards)])


def everyone(values, shards, step_axis=0):
    return jnp.stack([values] + [shift(values, shards, -j) for j in range(1, shards)], axis=step_axis)


def in_order(values, shards, place):
    if shards == 2:
        other = shift(values, shards, 1)
        low = jnp.where(place == 0, values, other)
        high = jnp.where(place == 0, other, values)
        return jnp.stack([low, high])
    return lax.all_gather(values, "seq", axis=0)


def token_sum(values):
    return jnp.sum(values.astype(jnp.float32), axis=0)


MESH = pl.DeviceIdType.MESH


class Peers:
    def __init__(self, dps):
        self.dp = lax.axis_index("dp")
        self.seq = lax.axis_index("seq")
        self.levels = dps // 4
        self.z = self.dp // 4
        self.x = self.dp % 4 // 2
        self.core = self.dp % 2

    def up(self, step):
        return ((self.z + step) % self.levels * 4 + self.dp % 4, self.seq)

    def across(self):
        return (self.dp + 2 - 4 * self.x, self.seq)

    def sibling(self):
        return (self.dp + 1 - 2 * self.core, self.seq)

    def other(self):
        return (self.dp, 1 - self.seq)

    def all(self):
        return [self.up(s) for s in range(1, self.levels)] + [self.across(), self.sibling(), self.other()]

    def greet(self):
        barrier = pltpu.get_barrier_semaphore()
        for device in self.all():
            pl.semaphore_signal(barrier, inc=1, device_id=device, device_id_type=MESH)
        pl.semaphore_wait(barrier, len(self.all()))


def remote(src, dst, send, recv, device):
    return pltpu.make_async_remote_copy(
        src_ref=src, dst_ref=dst, send_sem=send, recv_sem=recv, device_id=device, device_id_type=MESH
    )


class Gather:
    def __init__(self, peers, src, full, sems):
        levels = peers.levels
        at = (peers.z, peers.x, peers.core)
        self.local = pltpu.make_async_copy(src, full.at[at], sems.at[0])
        self.first = [
            remote(src, full.at[at], sems.at[2 * s + 3], sems.at[2 * s + 4], peers.up(s)) for s in range(1, levels)
        ]
        column = full.at[:, peers.x, peers.core]
        self.second = remote(column, column, sems.at[1], sems.at[2], peers.across())
        half = full.at[:, :, peers.core]
        self.third = remote(half, half, sems.at[3], sems.at[4], peers.sibling())

    def start(self):
        self.local.start()
        for copy in self.first:
            copy.start()

    def cross(self):
        self.local.wait()
        for copy in self.first:
            copy.wait_recv()
        self.second.start()

    def share(self):
        self.second.wait_recv()
        self.third.start()

    def arrive(self):
        self.third.wait_recv()

    def finish(self):
        for copy in self.first + [self.second, self.third]:
            copy.wait_send()


def gather_sems(levels):
    return 2 * levels + 3


def attend_pair(valid_ref, mixed, att, lse_ref, pair, base):
    shards, length, width3 = mixed.shape
    part = width3 // 3

    def columns(t):
        return pl.ds(pl.multiple_of(t * part + pair * PAIR, PAIR), PAIR)

    row = lax.broadcasted_iota(jnp.int32, (shards * length, 1), 0)
    bias = jnp.where(row < valid_ref[0], 0.0, NEG_FILL).astype(jnp.float32)
    keys = mixed[:, :, columns(1)].reshape(shards * length, PAIR).astype(jnp.float32)
    values = mixed[:, :, columns(2)].reshape(shards * length, PAIR).astype(jnp.float32)
    keys_of = [augmented(keys, head, [bias]) for head in range(2)]
    values_of = [augmented(values, head, [1.0]).T for head in range(2)]
    out_columns = pl.ds(pl.multiple_of(base + pair * PAIR, PAIR), PAIR)
    for shard in range(shards):
        queries = mixed[shard, :, columns(0)].astype(jnp.float32).T * HD**-0.5
        halves = []
        for head in range(2):
            scores = mat(keys_of[head], rows_with(queries, head, [1.0]))
            top = jnp.max(scores, axis=0, keepdims=True)
            weight = jnp.exp(scores - top).astype(jnp.bfloat16)
            product = mat(values_of[head], weight)
            at = HD * (1 - head)
            row_total = product[at : at + 1, :]
            halves.append(product[HD * head : HD * (head + 1), :] / row_total)
            lse_ref[pair, shard, head : head + 1, :] = top + jnp.log(row_total)
        att[shard, :, out_columns] = jnp.concatenate(halves, axis=0).T.astype(att.dtype)


ROW_TILE = 192
COL_TILE = 512


def forward_layer(
    valid_ref, tokens, cotangent, w_qkv, w_out, w_up, w_down, small,
    tok_out, dy_out, first_out, mixed_out, att_out, lse_ref, resid_out, second_out, act_out, slope_out,
    q_out, k_out, v_out, o_out, up_out, down_out, rows_ref, bup_ref,
    tok, first, mixed, att, resid, second, act, slope, fsmall, fq, fk, fv, fo, fup, fdown, my_up, gsems, sems,
):
    levels = fq.shape[0]
    peers = Peers(4 * levels)
    p = peers.seq
    length, width = tokens.shape
    part = width // 2
    sub = fdown.shape[3]
    shard_rows = w_out.shape[0]
    peers.greet()

    send_tok = remote(tokens, tok.at[p], sems.at[0], sems.at[1], peers.other())
    send_tok.start()
    gathers = []
    own = lambda t: w_qkv.at[:, pl.ds(pl.multiple_of(t * width + p * part, PAIR), part)]
    sources = [
        small, own(0), own(1), own(2), w_out, my_up, w_down.at[pl.ds(pl.multiple_of(p * sub, 16), sub)]
    ]
    fulls = [fsmall, fq, fk, fv, fo, fup, fdown]
    for i, (src, full) in enumerate(zip(sources, fulls)):
        gathers.append(Gather(peers, src, full, gsems.at[i]))
    g_small, g_q, g_k, g_v, g_out, g_up, g_down = gathers
    for g in (g_small, g_q, g_k, g_v):
        g.start()
    for d in range(4 * levels):
        my_up[:, d * sub : (d + 1) * sub] = w_up[:, pl.ds(pl.multiple_of((2 * d + p) * sub, PAIR), sub)]

    own_tok = pltpu.make_async_copy(tokens, tok.at[p], sems.at[2])
    own_tok.start()
    own_dy = pltpu.make_async_copy(cotangent, dy_out.at[p], sems.at[3])
    own_dy.start()

    def normed(shard):
        @pl.loop(0, length // ROW_TILE)
        def _(i):
            at = pl.ds(pl.multiple_of(i * ROW_TILE, 16), ROW_TILE)
            resid[shard, at, :] = norm_parts(tok[shard, at, :].astype(jnp.float32))[0]

    g_small.cross()
    g_q.cross()
    own_tok.wait()
    normed(p)
    g_k.cross()
    g_v.cross()
    g_out.start()
    g_small.share()
    g_q.share()
    g_k.share()
    send_tok.wait_recv()
    send_dy = remote(cotangent, dy_out.at[p], sems.at[4], sems.at[5], peers.other())
    send_dy.start()
    normed(1 - p)
    g_small.arrive()
    vectors = fsmall[:, :, :, 0:shard_rows, :].reshape(width, SMALL).astype(jnp.float32).T
    rows_ref[...] = vectors[0:16, :]
    for d in range(4 * levels):
        at = (d // 4, d % 4 // 2, d % 2)
        pair_rows = fsmall[at + (slice(shard_rows, shard_rows + 16),)].astype(jnp.float32)
        bup_ref[0:1, d * sub : (d + 1) * sub] = jnp.where(p == 0, pair_rows[0:1, :sub], pair_rows[1:2, :sub])

    for shard in range(2):
        @pl.loop(0, length // ROW_TILE)
        def _(i):
            at = pl.ds(pl.multiple_of(i * ROW_TILE, 16), ROW_TILE)
            first[shard, at, :] = (resid[shard, at, :] * rows_ref[0:1, :] + rows_ref[2:3, :]).astype(jnp.bfloat16)

    own_columns = pl.ds(pl.multiple_of(p * part, PAIR), part)

    def project(t, full, bias):
        weight = full[...].reshape(width, part)
        @pl.loop(0, 2)
        def _(shard):
            out = mat(first[shard], weight)
            if bias is not None:
                out = out + rows_ref[bias : bias + 1, own_columns]
            mixed[shard, :, t * part : (t + 1) * part] = out.astype(jnp.bfloat16)

    saves = []

    def save(src, dst):
        copy = pltpu.make_async_copy(src, dst, sems.at[16 + len(saves)])
        saves.append(copy)
        copy.start()

    save(tok, tok_out)
    save(first, first_out)
    g_v.share()
    g_q.arrive()
    project(0, fq, 3)
    g_out.cross()
    g_up.start()
    g_k.arrive()
    project(1, fk, None)
    g_v.arrive()
    project(2, fv, 4)
    save(mixed, mixed_out)
    save(fq, q_out)
    save(fk, k_out)
    save(fv, v_out)

    pairs = part // PAIR
    att_copies = []
    for pair in range(pairs):
        columns = pl.ds(pl.multiple_of(p * part + pair * PAIR, PAIR), PAIR)
        att_copies.append(
            remote(
                att.at[:, :, columns], att.at[:, :, columns], sems.at[8 + 2 * pair], sems.at[9 + 2 * pair],
                peers.other(),
            )
        )

    @pl.loop(0, pairs)
    def _(pair):
        attend_pair(valid_ref, mixed, att, lse_ref, pair, p * part)
        for i in range(pairs):
            @pl.when(pair == i)
            def _():
                att_copies[i].start()
                if i == 0:
                    g_out.share()
                if i == min(1, pairs - 1):
                    g_up.cross()
                    g_down.start()

    g_out.arrive()
    save(fo, o_out)
    for copy in att_copies:
        copy.wait_recv()
    save(att, att_out)
    out_weight = fo[...].reshape(width, width)

    def finish_rows(shard):
        @pl.loop(0, length // ROW_TILE)
        def _(i):
            at = pl.ds(pl.multiple_of(i * ROW_TILE, 16), ROW_TILE)
            value = mat(att[shard, at, :], out_weight) + rows_ref[5:6, :] + tok[shard, at, :].astype(jnp.float32)
            resid[shard, at, :] = value
            hat, _ = norm_parts(value)
            second[shard, at, :] = (hat * rows_ref[1:2, :] + rows_ref[6:7, :]).astype(jnp.bfloat16)

    finish_rows(0)
    finish_rows(1)
    save(resid.at[p], resid_out)
    save(second, second_out)
    g_up.share()
    g_down.cross()
    g_up.arrive()
    save(fup, up_out)
    own_hidden = act.shape[2]
    tiles = own_hidden // COL_TILE

    @pl.loop(0, 2 * tiles)
    def _(step):
        shard = step // tiles
        at = pl.ds(pl.multiple_of(step % tiles * COL_TILE, PAIR), COL_TILE)
        upward = mat(second[shard], fup[:, :, :, :, at].reshape(width, COL_TILE)) + bup_ref[0:1, at]
        cdf = 0.5 * (1.0 + lax.erf(upward * 0.5**0.5))
        act[shard, :, at] = (upward * cdf).astype(jnp.bfloat16)
        value = cdf + upward * (jnp.exp(-0.5 * upward * upward) * 0.3989422804014327)
        slope[shard, :, at] = value.astype(jnp.bfloat16)

    save(act, act_out)
    save(slope, slope_out)
    g_down.share()
    g_down.arrive()
    save(fdown, down_out)
    send_tok.wait_send()
    send_dy.wait()
    own_dy.wait()
    for copy in att_copies:
        copy.wait_send()
    for g in gathers:
        g.finish()
    for copy in saves:
        copy.wait()


def run_forward(dps, tokens, cotangent, w_qkv, w_out, w_up, w_down, small, valid):
    length, width = tokens.shape
    levels = dps // 4
    part = width // 2
    shard_rows = w_out.shape[0]
    own_hidden = w_up.shape[1] // 2
    sub = w_down.shape[0] // 2
    pairs = part // PAIR
    bf, f32 = jnp.bfloat16, jnp.float32
    any_spec = pl.BlockSpec(memory_space=pl.ANY)
    vmem = pl.BlockSpec(memory_space=pltpu.VMEM)
    smem = pl.BlockSpec(memory_space=pltpu.SMEM)
    grid = (levels, 2, 2)
    whole = [
        ((2, length, width), bf),
        ((2, length, width), bf),
        ((2, length, width), bf),
        ((2, length, 3 * part), bf),
        ((2, length, width), bf),
        ((pairs, 2, 2, length), f32),
        ((length, width), f32),
        ((2, length, width), bf),
        ((2, length, own_hidden), bf),
        ((2, length, own_hidden), bf),
        (grid + (shard_rows, part), bf),
        (grid + (shard_rows, part), bf),
        (grid + (shard_rows, part), bf),
        (grid + (shard_rows, width), bf),
        (grid + (shard_rows, own_hidden), bf),
        (grid + (sub, width), bf),
        ((16, width), f32),
        ((8, own_hidden), f32),
    ]
    in_vmem = (5, 16, 17)
    scratch = [
        pltpu.VMEM((2, length, width), bf),
        pltpu.VMEM((2, length, width), bf),
        pltpu.VMEM((2, length, 3 * part), bf),
        pltpu.VMEM((2, length, width), bf),
        pltpu.VMEM((2, length, width), f32),
        pltpu.VMEM((2, length, width), bf),
        pltpu.VMEM((2, length, own_hidden), bf),
        pltpu.VMEM((2, length, own_hidden), bf),
        pltpu.VMEM(grid + (shard_rows + 16, SMALL), bf),
        pltpu.VMEM(grid + (shard_rows, part), bf),
        pltpu.VMEM(grid + (shard_rows, part), bf),
        pltpu.VMEM(grid + (shard_rows, part), bf),
        pltpu.VMEM(grid + (shard_rows, width), bf),
        pltpu.VMEM(grid + (shard_rows, own_hidden), bf),
        pltpu.VMEM(grid + (sub, width), bf),
        pltpu.VMEM((shard_rows, own_hidden), bf),
        pltpu.SemaphoreType.DMA((7, gather_sems(levels))),
        pltpu.SemaphoreType.DMA((32,)),
    ]
    return pl.pallas_call(
        forward_layer,
        in_specs=[smem, any_spec, any_spec, vmem, vmem, vmem, vmem, vmem],
        out_specs=[vmem if i in in_vmem else any_spec for i in range(len(whole))],
        out_shape=[jax.ShapeDtypeStruct(*s) for s in whole],
        scratch_shapes=scratch,
        compiler_params=pltpu.CompilerParams(
            vmem_limit_bytes=60 * 2**20, collective_id=0, has_side_effects=True
        ),
        cost_estimate=pl.CostEstimate(flops=3 * 10**10, bytes_accessed=8 * 10**7, transcendentals=2 * 10**7),
    )(valid, tokens, cotangent, w_qkv, w_out, w_up, w_down, small)


class Scatter:
    def __init__(self, peers, grad, cored, crossed, risen, own, theirs, sems):
        core, x, z = peers.core, peers.x, peers.z
        self.peers, self.grad, self.cored, self.crossed, self.risen = peers, grad, cored, crossed, risen
        self.own = own
        self.first = remote(grad.at[1 - core], cored, sems.at[0], sems.at[1], peers.sibling())
        self.second = remote(grad.at[core, :, 1 - x], crossed, sems.at[2], sems.at[3], peers.across())
        self.third = [
            remote(
                grad.at[core, (z + s) % peers.levels, x], risen.at[s - 1], sems.at[2 * s + 4], sems.at[2 * s + 5],
                peers.up(s),
            )
            for s in range(1, peers.levels)
        ]
        self.fourth = remote(own, theirs, sems.at[4], sems.at[5], peers.other())

    def start(self):
        self.first.start()

    def cross(self):
        core = self.peers.core
        self.first.wait_recv()

        @pl.loop(0, self.peers.levels)
        def _(z):
            for x in range(2):
                total = self.grad[core, z, x].astype(jnp.float32) + self.cored[z, x].astype(jnp.float32)
                self.grad[core, z, x] = total.astype(self.grad.dtype)

        self.second.start()

    def rise(self):
        core, x = self.peers.core, self.peers.x
        self.second.wait_recv()

        @pl.loop(0, self.peers.levels)
        def _(z):
            total = self.grad[core, z, x].astype(jnp.float32) + self.crossed[z].astype(jnp.float32)
            self.grad[core, z, x] = total.astype(self.grad.dtype)

        for copy in self.third:
            copy.start()

    def over(self):
        for copy in self.third:
            copy.wait_recv()
        total = self.grad[self.peers.core, self.peers.z, self.peers.x].astype(jnp.float32)
        for s in range(self.peers.levels - 1):
            total = total + self.risen[s].astype(jnp.float32)
        self.own[...] = total.astype(self.own.dtype)
        self.fourth.start()

    def arrive(self):
        self.fourth.wait_recv()

    def finish(self):
        for copy in [self.first, self.second, self.fourth] + self.third:
            copy.wait_send()


def scatter_sems(levels):
    return 2 * levels + 4


def scatter_buffers(levels, rows, columns, dtype):
    return [
        pltpu.VMEM((2, levels, 2, rows, columns), dtype),
        pltpu.VMEM((levels, 2, rows, columns), dtype),
        pltpu.VMEM((levels, rows, columns), dtype),
        pltpu.VMEM((levels - 1, rows, columns), dtype),
    ]


def attend_pair_back(valid_ref, mixed, att, lse_ref, datt, dmix, sums, pair, base, place):
    shards, length, width3 = mixed.shape
    part = width3 // 3
    group, within = pair // 2, pair % 2
    wide = dmix.shape[3] // 3

    def columns(t):
        return pl.ds(pl.multiple_of(t * part + pair * PAIR, PAIR), PAIR)

    def out_columns(t):
        return pl.ds(pl.multiple_of(t * wide + within * PAIR, PAIR), PAIR)

    own_columns = pl.ds(pl.multiple_of(base + pair * PAIR, PAIR), PAIR)
    da_columns = pl.ds(pl.multiple_of(pair * PAIR, PAIR), PAIR)
    row = lax.broadcasted_iota(jnp.int32, (shards * length, 1), 0)
    bias = jnp.where(row < valid_ref[0], 0.0, NEG_FILL).astype(jnp.float32)
    keys = mixed[:, :, columns(1)].reshape(shards * length, PAIR).astype(jnp.float32)
    values = mixed[:, :, columns(2)].reshape(shards * length, PAIR).astype(jnp.float32)
    keys_of = [augmented(keys, head, [bias, 1.0, 1.0, 1.0]) for head in range(2)]
    values_of = [augmented(values, head, [1.0, 1.0, 1.0]) for head in range(2)]
    plain_keys = [augmented(keys, head, []).T for head in range(2)]
    dk = dv = None
    dq_sum = None
    for shard in range(shards):
        queries = mixed[shard, :, columns(0)].astype(jnp.float32) * HD**-0.5
        grads = datt[shard, :, da_columns].astype(jnp.float32)
        queries_t, grads_t = queries.T, grads.T
        product = grads_t * att[shard, :, own_columns].astype(jnp.float32).T
        dq = None
        for head in range(2):
            lse = lse_ref[pair, shard, head : head + 1, :]
            delta = jnp.sum(product[HD * head : HD * (head + 1), :], axis=0, keepdims=True)
            scores = mat(keys_of[head], rows_with(queries_t, head, (1.0,) + split_three(-lse)))
            probs = jnp.exp(scores)
            moved = mat(values_of[head], rows_with(grads_t, head, split_three(-delta)))
            dscores = (probs * moved).astype(jnp.bfloat16)
            part_v = mat(probs.astype(jnp.bfloat16), augmented(grads, head, []))
            part_k = mat(dscores, augmented(queries, head, []))
            part_q = mat(plain_keys[head], dscores)
            dq = part_q if dq is None else dq + part_q
            dk = part_k if dk is None else dk + part_k
            dv = part_v if dv is None else dv + part_v
        dq = (dq * HD**-0.5).T.astype(jnp.bfloat16)
        dmix[group, shard, :, out_columns(0)] = dq
        total = jnp.sum(dq.astype(jnp.float32), axis=0, keepdims=True)
        dq_sum = total if dq_sum is None else dq_sum + total
    dk, dv = dk.astype(jnp.bfloat16), dv.astype(jnp.bfloat16)
    dmix[group, :, :, out_columns(1)] = dk.reshape(shards, length, PAIR)
    dmix[group, :, :, out_columns(2)] = dv.reshape(shards, length, PAIR)
    sums[3:4, own_columns] = dq_sum
    sums[4:5, own_columns] = jnp.sum(dv.astype(jnp.float32), axis=0, keepdims=True)


def column_sum(values):
    return jnp.sum(values, axis=0, keepdims=True)


def backward_layer(
    valid_ref, rows_ref, lse_ref,
    tok_in, dy_in, first_in, mixed_in, att_in, resid_in, second_in, act_in, slope_in,
    q_in, k_in, v_in, o_in, up_in, down_in,
    outf_ref, orecv_ref, gtok_ref, gqkv_ref, gout_ref, gup_ref, gdown_ref, gsmall_ref,
    down0, down1, down2, down3, up0, up1, up2, up3, out0, out1, out2, out3, qa0, qa1, qa2, qa3, qb0, qb1, qb2, qb3,
    sm0, sm1, sm2, sm3, out_own, out_theirs, sm_own, sm_theirs,
    ysend, yrecv, osend, dres, datt, sums, dub, ssems, sems,
):
    levels = down2.shape[0]
    peers = Peers(4 * levels)
    p, q = peers.seq, 1 - peers.seq
    _, length, width = dy_in.shape
    part = width // 2
    own_hidden = act_in.shape[2]
    sub = own_hidden // (4 * levels)
    shard_rows = width // (4 * levels)
    wide = part // 2
    bf, f32 = jnp.bfloat16, jnp.float32
    tiles = length // ROW_TILE
    peers.greet()

    s_down = Scatter(peers, down0, down1, down2, down3, gdown_ref.at[p], gdown_ref.at[p], ssems.at[0])
    s_up = Scatter(peers, up0, up1, up2, up3, gup_ref.at[p], gup_ref.at[p], ssems.at[1])
    s_out = Scatter(peers, out0, out1, out2, out3, out_own, out_theirs, ssems.at[2])
    s_qa = Scatter(peers, qa0, qa1, qa2, qa3, gqkv_ref.at[p, 0], gqkv_ref.at[p, 0], ssems.at[3])
    s_qb = Scatter(peers, qb0, qb1, qb2, qb3, gqkv_ref.at[p, 1], gqkv_ref.at[p, 1], ssems.at[4])
    s_small = Scatter(peers, sm0, sm1, sm2, sm3, sm_own, sm_theirs, ssems.at[5])
    send_two = remote(ysend, yrecv, sems.at[0], sems.at[1], peers.other())
    send_one = remote(ysend, yrecv, sems.at[2], sems.at[3], peers.other())
    send_out = remote(osend, orecv_ref, sems.at[4], sems.at[5], peers.other())
    sums[...] = jnp.zeros_like(sums)

    def row_at(i):
        return pl.ds(pl.multiple_of(i * ROW_TILE, 16), ROW_TILE)

    def load(src, dst, at):
        copy = pltpu.make_async_copy(src, dst, sems.at[at])
        copy.start()
        return copy

    def place_blocks(grad, z, value):
        rows = grad.shape[3]
        for x in range(2):
            for core in range(2):
                at = (2 * x + core) * rows
                grad[core, z, x] = value[at : at + rows, :].astype(grad.dtype)

    def hidden_phase(dy, act, du, fdown, fup, second, outt):
        copies = [
            load(dy_in, dy, 16), load(down_in, fdown, 17), load(slope_in, du, 18), load(up_in, fup, 19),
            load(act_in, act, 20), load(second_in, second, 21),
        ]
        for copy in copies[:3]:
            copy.wait()

        def into_hidden(shard):
            @pl.loop(0, levels)
            def _(z):
                at = pl.ds(pl.multiple_of(z * 4 * sub, PAIR), 4 * sub)
                grad = dot_f32(dy[shard], fdown[z].reshape(4 * sub, width), ((1,), (1,)))
                value = (grad * du[shard, :, at].astype(f32)).astype(bf)
                du[shard, :, at] = value
                dub[pl.ds(shard, 1), at] = column_sum(value.astype(f32))

        def back_second(shard, target):
            @pl.loop(0, levels)
            def _(z):
                at = pl.ds(pl.multiple_of(z * 4 * shard_rows, PAIR), 4 * shard_rows)
                value = dot_f32(du[shard], fup[z].reshape(4 * shard_rows, own_hidden), ((1,), (1,)))
                target[:, at] = value.astype(target.dtype)

        into_hidden(q)
        copies[3].wait()
        back_second(q, ysend)
        send_two.start()
        into_hidden(p)
        copies[4].wait()

        @pl.loop(0, levels)
        def _(z):
            at = pl.ds(pl.multiple_of(z * 4 * sub, PAIR), 4 * sub)
            value = dot_f32(act[:, :, at].reshape(2 * length, 4 * sub), dy[...].reshape(2 * length, width), ((0,), (0,)))
            place_blocks(down0, z, value)

        s_down.start()
        back_second(p, dres)
        copies[5].wait()
        s_down.cross()

        @pl.loop(0, levels)
        def _(z):
            at = pl.ds(pl.multiple_of(z * 4 * shard_rows, PAIR), 4 * shard_rows)
            value = dot_f32(
                second[:, :, at].reshape(2 * length, 4 * shard_rows), du[...].reshape(2 * length, own_hidden), ((0,), (0,))
            )
            place_blocks(up0, z, value)

        s_up.start()

        @pl.loop(0, width // COL_TILE)
        def _(t):
            at = pl.ds(pl.multiple_of(t * COL_TILE, PAIR), COL_TILE)
            weight = fdown[:, :, :, :, at].reshape(own_hidden, COL_TILE)
            osend[:, at] = mat(act[q], weight).astype(bf)

        kept = None
        for t in range(width // COL_TILE):
            at = slice(t * COL_TILE, (t + 1) * COL_TILE)
            weight = fdown[:, :, :, :, at].reshape(own_hidden, COL_TILE)
            value = mat(act[p], weight)
            if kept is not None:
                kept.wait()
            outt[...] = value
            kept = load(outt, outf_ref.at[:, at], 22)
        s_up.cross()
        kept.wait()

    pl.run_scoped(
        hidden_phase,
        pltpu.VMEM((2, length, width), bf),
        pltpu.VMEM((2, length, own_hidden), bf),
        pltpu.VMEM((2, length, own_hidden), bf),
        pltpu.VMEM(down_in.shape, bf),
        pltpu.VMEM(up_in.shape, bf),
        pltpu.VMEM((2, length, width), bf),
        pltpu.VMEM((length, COL_TILE), f32),
    )

    def norm_phase(dy, resid, att, fo, dbr, datt_send):
        copies = [
            load(dy_in.at[p], dy, 16), load(resid_in, resid, 17), load(o_in, fo, 18), load(att_in.at[p], att, 19),
        ]
        send_two.wait_recv()
        copies[0].wait()
        copies[1].wait()

        @pl.loop(0, tiles)
        def _(i):
            at = row_at(i)
            hat, inverse = norm_parts(resid[at, :])
            grad = dres[at, :] + yrecv[at, :].astype(f32)
            grad_y = dy[at, :].astype(f32)
            value = grad_y + norm_back(hat, inverse, rows_ref[1:2, :], grad)
            dres[at, :] = value
            low = value.astype(bf)
            dbr[at, :] = low
            sums[1:2, :] += column_sum(grad * hat)
            sums[5:6, :] += column_sum(low.astype(f32))
            sums[6:7, :] += column_sum(grad)
            sums[7:8, :] += column_sum(grad_y)

        copies[2].wait()
        half = levels // 2
        sends = []
        for g in range(2):
            at = slice(g * wide, (g + 1) * wide)
            blocks = pl.ds(q * half + g * (half // 2), half // 2)
            value = dot_f32(dbr[...], fo[blocks].reshape(wide, width), ((1,), (1,)))
            datt_send[:, at] = value.astype(bf)
            copy = remote(
                datt_send.at[:, at], datt.at[p, :, at], sems.at[6 + 2 * g], sems.at[7 + 2 * g], peers.other()
            )
            copy.start()
            sends.append(copy)
        send_out.start()
        datt[p] = dot_f32(dbr[...], fo[pl.ds(p * half, half)].reshape(part, width), ((1,), (1,))).astype(bf)
        copies[3].wait()

        @pl.loop(0, levels)
        def _(z):
            at = pl.ds(pl.multiple_of(z * 4 * shard_rows, PAIR), 4 * shard_rows)
            place_blocks(out0, z, dot_f32(att[:, at], dbr[...], ((0,), (0,))))

        s_out.start()
        s_down.rise()
        for copy in sends:
            copy.wait()
        s_out.cross()

    pl.run_scoped(
        norm_phase,
        pltpu.VMEM((length, width), bf),
        pltpu.VMEM((length, width), f32),
        pltpu.VMEM((length, width), bf),
        pltpu.VMEM(o_in.shape, bf),
        pltpu.VMEM((length, width), bf),
        pltpu.VMEM((length, part), bf),
    )

    def heads_phase(dmix, first):
        loaded = load(first_in, first, 16)

        def weight_grad(g, grad):
            @pl.loop(0, levels)
            def _(z):
                at = pl.ds(pl.multiple_of(z * 4 * shard_rows, PAIR), 4 * shard_rows)
                value = dot_f32(
                    first[:, :, at].reshape(2 * length, 4 * shard_rows),
                    dmix[g].reshape(2 * length, 3 * wide), ((0,), (0,)),
                )
                place_blocks(grad, z, value)

        def attention_phase(mixed, att):
            one, two = load(mixed_in, mixed, 17), load(att_in, att, 18)
            one.wait()
            two.wait()
            loaded.wait()

            @pl.loop(0, part // PAIR)
            def _(pair):
                attend_pair_back(valid_ref, mixed, att, lse_ref, datt, dmix, sums, pair, p * part, p)

                @pl.when(pair == 0)
                def _():
                    s_up.rise()
                    s_down.over()

                @pl.when(pair == 1)
                def _():
                    weight_grad(0, qa0)
                    s_qa.start()
                    s_out.rise()

                @pl.when(pair == 2)
                def _():
                    s_qa.cross()
                    s_up.over()

        pl.run_scoped(
            attention_phase,
            pltpu.VMEM(mixed_in.shape, bf),
            pltpu.VMEM(att_in.shape, bf),
        )

        def last_phase(tok, fq, fk, fv, part_one):
            copies = [load(q_in, fq, 17), load(k_in, fk, 18), load(v_in, fv, 19), load(tok_in, tok, 20)]
            weight_grad(1, qb0)
            s_qb.start()
            for copy in copies:
                copy.wait()
            send_two.wait_send()

            def back_first(shard, target):
                @pl.loop(0, levels)
                def _(z):
                    at = pl.ds(pl.multiple_of(z * 4 * shard_rows, PAIR), 4 * shard_rows)
                    total = None
                    for g in range(2):
                        for t, full in enumerate((fq, fk, fv)):
                            value = dot_f32(
                                dmix[g, shard, :, t * wide : (t + 1) * wide],
                                full[z, :, :, :, g * wide : (g + 1) * wide].reshape(4 * shard_rows, wide),
                                ((1,), (1,)),
                            )
                            total = value if total is None else total + value
                    target[:, at] = total.astype(target.dtype)

            def gain_sums(shard, source):
                @pl.loop(0, tiles)
                def _(i):
                    at = row_at(i)
                    hat, _ = norm_parts(tok[shard, at, :].astype(f32))
                    grad = source[at, :].astype(f32)
                    sums[0:1, :] += column_sum(grad * hat)
                    sums[2:3, :] += column_sum(grad)

            back_first(q, part_one)

            @pl.loop(0, tiles)
            def _(i):
                ysend[row_at(i), :] = part_one[row_at(i), :].astype(bf)

            send_one.start()
            gain_sums(q, part_one)
            s_qa.rise()
            s_qb.cross()
            back_first(p, part_one)
            gain_sums(p, part_one)

            vectors = jnp.concatenate([sums[...], jnp.zeros((SMALL - 16, width), f32)], axis=0).T
            ups = dub[0:1, :] + dub[1:2, :]
            line = lax.broadcasted_iota(jnp.int32, (8, 1), 0)
            for d in range(4 * levels):
                at = (d % 2, d // 4, d % 4 // 2)
                sm0[at + (slice(0, shard_rows),)] = vectors[d * shard_rows : (d + 1) * shard_rows, :]
                sm0[at + (slice(shard_rows, shard_rows + 8),)] = jnp.where(line == p, ups[:, d * sub : (d + 1) * sub], 0.0)
            s_small.start()
            s_out.over()
            s_small.cross()
            s_qb.rise()
            s_small.rise()
            s_qa.over()
            s_out.arrive()
            gout_ref[...] = out_own[...].astype(f32) + out_theirs[...].astype(f32)
            s_small.over()
            s_qb.over()
            send_one.wait_recv()

            @pl.loop(0, tiles)
            def _(i):
                at = row_at(i)
                hat, inverse = norm_parts(tok[p, at, :].astype(f32))
                grad = part_one[at, :] + yrecv[at, :].astype(f32)
                part_one[at, :] = dres[at, :] + norm_back(hat, inverse, rows_ref[0:1, :], grad)

            written = load(part_one, gtok_ref, 20)
            s_small.arrive()
            gsmall_ref[...] = sm_own[...] + sm_theirs[...]
            for s in (s_down, s_up, s_qa, s_qb):
                s.arrive()
            written.wait()

        pl.run_scoped(
            last_phase,
            pltpu.VMEM((2, length, width), bf),
            pltpu.VMEM(q_in.shape, bf),
            pltpu.VMEM(k_in.shape, bf),
            pltpu.VMEM(v_in.shape, bf),
            pltpu.VMEM((length, width), f32),
        )

    pl.run_scoped(
        heads_phase,
        pltpu.VMEM((2, 2, length, 3 * wide), bf),
        pltpu.VMEM((2, length, width), bf),
    )
    send_out.wait()
    send_one.wait_send()
    for s in (s_down, s_up, s_out, s_qa, s_qb, s_small):
        s.finish()


def run_backward(dps, valid, vectors, lse, tok, dy, first, mixed, att, resid, second, act, slope, fq, fk, fv, fo, fup, fdown):
    levels = dps // 4
    _, length, width = dy.shape
    part = width // 2
    wide = part // 2
    own_hidden = act.shape[2]
    shard_rows, sub = width // dps, own_hidden // dps
    bf, f32 = jnp.bfloat16, jnp.float32
    any_spec = pl.BlockSpec(memory_space=pl.ANY)
    vmem = pl.BlockSpec(memory_space=pltpu.VMEM)
    smem = pl.BlockSpec(memory_space=pltpu.SMEM)
    whole = [
        ((length, width), f32),
        ((length, width), bf),
        ((length, width), f32),
        ((2, 2, shard_rows, 3 * wide), bf),
        ((shard_rows, width), f32),
        ((2, shard_rows, own_hidden), bf),
        ((2, sub, width), bf),
        ((shard_rows + 8, SMALL), f32),
    ]
    scratch = (
        scatter_buffers(levels, sub, width, bf)
        + scatter_buffers(levels, shard_rows, own_hidden, bf)
        + scatter_buffers(levels, shard_rows, width, bf)
        + scatter_buffers(levels, shard_rows, 3 * wide, bf)
        + scatter_buffers(levels, shard_rows, 3 * wide, bf)
        + scatter_buffers(levels, shard_rows + 8, SMALL, f32)
        + [
            pltpu.VMEM((shard_rows, width), bf),
            pltpu.VMEM((shard_rows, width), bf),
            pltpu.VMEM((shard_rows + 8, SMALL), f32),
            pltpu.VMEM((shard_rows + 8, SMALL), f32),
            pltpu.VMEM((length, width), bf),
            pltpu.VMEM((length, width), bf),
            pltpu.VMEM((length, width), bf),
            pltpu.VMEM((length, width), f32),
            pltpu.VMEM((2, length, part), bf),
            pltpu.VMEM((16, width), f32),
            pltpu.VMEM((8, own_hidden), f32),
            pltpu.SemaphoreType.DMA((6, scatter_sems(levels))),
            pltpu.SemaphoreType.DMA((24,)),
        ]
    )
    return pl.pallas_call(
        backward_layer,
        in_specs=[smem, vmem, vmem] + [any_spec] * 15,
        out_specs=[any_spec] * 3 + [vmem] * 5,
        out_shape=[jax.ShapeDtypeStruct(*s) for s in whole],
        scratch_shapes=scratch,
        compiler_params=pltpu.CompilerParams(
            vmem_limit_bytes=62 * 2**20, collective_id=1, has_side_effects=True
        ),
        cost_estimate=pl.CostEstimate(flops=5 * 10**10, bytes_accessed=8 * 10**7, transcendentals=2 * 10**7),
    )(valid, vectors, lse, tok, dy, first, mixed, att, resid, second, act, slope, fq, fk, fv, fo, fup, fdown)


def per_device_pair(tokens, w_qkv, w_out, w_up, w_down, gains, biases, up_bias, valid, cotangent):
    _, length, width = tokens.shape
    shard_rows = w_qkv.shape[0]
    hidden = w_up.shape[1]
    dps = lax.axis_size("dp")
    part = width // 2
    sub = w_down.shape[0] // 2

    smalls = jnp.concatenate([gains, biases], axis=1)
    smalls = jnp.concatenate(
        [
            jnp.pad(smalls, ((0, 0), (0, SMALL - smalls.shape[1]))),
            jnp.pad(up_bias.reshape(2, sub), ((0, 14), (0, 0))),
        ],
        axis=0,
    )
    (
        tok, dy, first, mixed, att, lse, residual, second, act, slope, fq, fk, fv, fo, fup, fdown, vectors, _
    ) = run_forward(
        dps, tokens.reshape(length, width), cotangent.reshape(length, width), w_qkv, w_out, w_up, w_down, smalls, valid
    )
    own_part, their_part, grad_tokens, grad_qkv, grad_out, grad_up, grad_down, grad_small = run_backward(
        dps, valid, vectors, lse, tok, dy, first, mixed, att, residual, second, act, slope, fq, fk, fv, fo, fup, fdown
    )
    output = residual + own_part + their_part.astype(jnp.float32) + vectors[7]
    grad_qkv = grad_qkv.reshape(2, 2, shard_rows, 3, part // 2).transpose(2, 3, 0, 1, 4)
    grad_up = grad_up.reshape(2, shard_rows, dps, sub).transpose(1, 2, 0, 3)
    return (
        output.astype(jnp.bfloat16).reshape(tokens.shape),
        grad_tokens.reshape(tokens.shape),
        grad_qkv.reshape(shard_rows, 3 * width).astype(jnp.float32),
        grad_out,
        grad_up.reshape(shard_rows, hidden).astype(jnp.float32),
        grad_down.reshape(2 * sub, width).astype(jnp.float32),
        grad_small[:shard_rows, :2],
        grad_small[:shard_rows, 2:8],
        grad_small[shard_rows : shard_rows + 2, :].reshape(-1),
    )


def per_device(tokens, w_qkv, w_out, w_up, w_down, gains, biases, up_bias, valid, cotangent):
    images, length, width = tokens.shape
    rows = images * length
    shard_rows = w_qkv.shape[0]
    hidden = w_up.shape[1]
    ups = up_bias.shape[0] // shard_rows
    shards = lax.axis_size("seq")
    dps = lax.axis_size("dp")
    at = lax.axis_index("seq").astype(jnp.int32)
    place = at.reshape(1)
    part = width // shards
    own_hidden = hidden // shards
    sub = w_down.shape[0] // shards
    pairs_all = part // PAIR

    gather = functools.partial(lax.all_gather, axis_name="dp", axis=0, tiled=True)
    scatter = functools.partial(lax.psum_scatter, axis_name="dp", scatter_dimension=0, tiled=True)

    def pick(values, axis):
        return lax.dynamic_index_in_dim(values, at, axis, keepdims=False)

    smalls = jnp.concatenate([gains, biases, up_bias.reshape(shard_rows, ups)], axis=1)
    smalls = jnp.pad(smalls, ((0, 0), (0, SMALL - smalls.shape[1])))
    part_qkv = pick(w_qkv.reshape(shard_rows, 3, shards, part), 2).reshape(shard_rows, 3 * part)
    part_up = pick(w_up.reshape(shard_rows, dps, shards, sub), 2).reshape(shard_rows, own_hidden)
    part_down = pick(w_down.reshape(shards, sub, width), 0)
    full_qkvs = gather(jnp.concatenate([part_qkv, smalls], axis=1))
    w_out, full_qkvs = lax.optimization_barrier((w_out, full_qkvs))
    full_out = gather(w_out)
    part_up, full_out = lax.optimization_barrier((part_up, full_out))
    full_up = gather(part_up)
    part_down, full_up = lax.optimization_barrier((part_down, full_up))
    full_down = gather(part_down)

    flat_tokens = tokens.reshape(rows, width)
    flat_grad = cotangent.reshape(rows, width)
    all_tokens = everyone(flat_tokens, shards)
    flat_grad, all_tokens = lax.optimization_barrier((flat_grad, all_tokens))
    all_grad = everyone(flat_grad, shards).reshape(shards * rows, width)

    full_qkv = full_qkvs[:, : 3 * part]
    small = full_qkvs[:, 3 * part :].astype(jnp.float32).T
    gain_one, gain_two = small[0], small[1]
    bias_one, bias_q, bias_v, bias_out, bias_two, bias_down = (small[2 + i] for i in range(6))
    bias_up = pick(small[8 : 8 + ups].T.reshape(dps, shards, sub), 1).reshape(-1)
    bias_mixed = jnp.concatenate(
        [pick(bias_q.reshape(shards, part), 0), jnp.zeros((part,), jnp.float32), pick(bias_v.reshape(shards, part), 0)]
    )

    every_tokens = all_tokens.reshape(shards * rows, width).astype(jnp.float32)
    hat_one, inverse_one = norm_parts(every_tokens)
    first = (hat_one * gain_one + bias_one).astype(jnp.bfloat16)
    mixed = (mat(first, full_qkv) + bias_mixed).astype(jnp.bfloat16).reshape(shards, rows, 3 * part)

    groups = GROUPS if pairs_all % GROUPS == 0 else 1
    pairs = pairs_all // groups
    wide = pairs * PAIR
    forward = [attend_forward(images, place, valid, mixed, g * pairs, pairs) for g in range(groups)]
    blocks = []
    for j in range(shards):
        for g in range(groups):
            attended = forward[g][0]
            if j > 0:
                attended = jnp.roll(shift(attended, shards, -j), j, axis=0)
            blocks.append(attended.reshape(shards * rows, wide))
    merged = jnp.concatenate(blocks, axis=1)
    turned_out = jnp.roll(full_out, -at * part, axis=0)

    branch = mat(merged, turned_out) + bias_out
    residual = every_tokens + branch
    hat_two, inverse_two = norm_parts(residual)
    second = (hat_two * gain_two + bias_two).astype(jnp.bfloat16)
    upward = mat(second, full_up) + bias_up
    cdf = 0.5 * (1.0 + lax.erf(upward * 0.5**0.5))
    activated = (upward * cdf).astype(jnp.bfloat16)
    slope = cdf + upward * (jnp.exp(-0.5 * upward * upward) * 0.3989422804014327)
    slope = slope.astype(jnp.bfloat16)

    grad_act = dot_f32(all_grad, full_down, ((1,), (1,)))
    grad_upward = (grad_act * slope.astype(jnp.float32)).astype(jnp.bfloat16)

    def summed(left, right, dims):
        parts = [
            dot_f32(left[j * rows : (j + 1) * rows], right, dims) for j in range(shards)
        ]
        total = parts[0]
        for j in range(1, shards):
            total = total + shift(parts[j].astype(jnp.bfloat16), shards, j).astype(jnp.float32)
        return total

    grad_second = summed(grad_upward, full_up, ((1,), (1,)))
    grad_down = dot_f32(activated, all_grad, ((0,), (0,))).astype(jnp.bfloat16)
    piece_down = scatter(grad_down)
    grad_up = dot_f32(second, grad_upward, ((0,), (0,))).astype(jnp.bfloat16)
    grad_up, piece_down = lax.optimization_barrier((grad_up, piece_down))
    piece_up = scatter(grad_up)

    own_hat = hat_two[:rows]
    grad_resid = flat_grad.astype(jnp.float32) + norm_back(own_hat, inverse_two[:rows], gain_two, grad_second)
    grad_gain_two, grad_bias_two = token_sum(grad_second * own_hat), token_sum(grad_second)
    grad_branch = grad_resid.astype(jnp.bfloat16)
    grad_merged = dot_f32(grad_branch, turned_out, ((1,), (1,))).astype(jnp.bfloat16)
    received = [None] * shards
    for g in range(groups):
        lo = g * wide
        blocks = [grad_merged[:, lo : lo + wide]] + [None] * (shards - 1)
        for j in range(1, shards):
            blocks[shards - j] = shift(grad_merged[:, j * part + lo : j * part + lo + wide], shards, j)
        received[g] = jnp.stack(blocks)

    grad_out = dot_f32(merged[:rows], grad_branch, ((0,), (0,))).astype(jnp.bfloat16)
    grad_out = jnp.roll(grad_out, at * part, axis=0)
    grad_out, piece_up = lax.optimization_barrier((grad_out, piece_up))
    piece_out = scatter(grad_out)

    backs = [
        attend_backward(images, place, valid, mixed, g * pairs, pairs, *forward[g], received[g]) for g in range(groups)
    ]
    grad_mixed = jnp.concatenate(
        [back[t].reshape(shards * rows, wide) for t in range(3) for back in backs], axis=1
    )
    grad_first = summed(grad_mixed, full_qkv, ((1,), (1,)))
    grad_qkv = dot_f32(first, grad_mixed, ((0,), (0,))).astype(jnp.bfloat16)

    grad_tokens = grad_resid + norm_back(hat_one[:rows], inverse_one[:rows], gain_one, grad_first)
    grad_gain_one, grad_bias_one = token_sum(grad_first * hat_one[:rows]), token_sum(grad_first)

    def spread(values, before):
        out = jnp.zeros((before, shards, values.size // before), jnp.float32)
        return lax.dynamic_update_slice_in_dim(out, values.reshape(before, 1, -1), at, 1).reshape(-1)

    bias_sums = token_sum(grad_mixed)
    small_grads = jnp.stack(
        [
            grad_gain_one, grad_gain_two, grad_bias_one, spread(bias_sums[:part], 1), spread(bias_sums[2 * part :], 1),
            token_sum(grad_branch), grad_bias_two, token_sum(flat_grad),
        ],
        axis=1,
    )
    up_sums = spread(token_sum(grad_upward), dps).reshape(width, ups)
    small_grads = jnp.concatenate([small_grads, up_sums], axis=1)
    small_grads = jnp.pad(small_grads, ((0, 0), (0, SMALL - small_grads.shape[1])))
    grad_qkvs = jnp.concatenate([grad_qkv, small_grads.astype(jnp.bfloat16)], axis=1)
    grad_qkvs, piece_out = lax.optimization_barrier((grad_qkvs, piece_out))
    piece_qkvs = scatter(grad_qkvs)

    output = summed(activated, full_down, ((1,), (0,)))
    out_tokens = (residual[:rows] + output + bias_down).astype(jnp.bfloat16)

    total_down = in_order(piece_down, shards, at).astype(jnp.float32).reshape(shards * sub, width)
    total_up = in_order(piece_up.reshape(shard_rows, dps, sub), shards, at).astype(jnp.float32)
    total_up = total_up.transpose(1, 2, 0, 3).reshape(shard_rows, hidden)
    total_out = in_order(piece_out, shards, at).astype(jnp.float32).sum(0)
    every_qkvs = in_order(piece_qkvs, shards, at).astype(jnp.float32)
    total_qkv = every_qkvs[:, :, : 3 * part].reshape(shards, shard_rows, 3, part)
    total_qkv = total_qkv.transpose(1, 2, 0, 3).reshape(shard_rows, 3 * width)
    total_small = every_qkvs[:, :, 3 * part :].sum(0)
    return (
        out_tokens.reshape(tokens.shape),
        grad_tokens.reshape(tokens.shape),
        total_qkv,
        total_out,
        total_up,
        total_down,
        total_small[:, :2],
        total_small[:, 2:8],
        total_small[:, 8 : 8 + ups].reshape(-1),
    )


def solution(mesh):
    paired = mesh.shape["seq"] == 2 and mesh.shape["dp"] == 16
    return jax.shard_map(
        per_device_pair if paired else per_device,
        mesh=mesh,
        in_specs=(
            P("dp", "seq", None),
            P("dp", None),
            P("dp", None),
            P("dp", None),
            P("dp", None),
            P("dp", None),
            P("dp", None),
            P("dp"),
            P("dp"),
            P("dp", "seq", None),
        ),
        out_specs=(
            P("dp", "seq", None),
            P("dp", "seq", None),
            P("dp", None),
            P("dp", None),
            P("dp", None),
            P("dp", None),
            P("dp", None),
            P("dp", None),
            P("dp"),
        ),
        check_vma=False,
    )
```

```python
import functools

import jax
import jax.numpy as jnp
from jax import lax
from jax.experimental import pallas as pl
from jax.experimental.pallas import tpu as pltpu
from jax.sharding import PartitionSpec as P

HD = 64
PAIR = 2 * HD
EPSILON = 1e-06
NEG_FILL = -1e30
SMALL = 128
GROUPS = 2


def dot_f32(a, b, dims):
    return lax.dot_general(a, b, (dims, ((), ())), preferred_element_type=jnp.float32)


def mat(a, b):
    return dot_f32(a, b, ((1,), (0,)))


def norm_parts(values):
    average = jnp.mean(values, axis=-1, keepdims=True)
    centered = values - average
    variance = jnp.mean(centered * centered, axis=-1, keepdims=True)
    inverse = lax.rsqrt(variance + EPSILON)
    return centered * inverse, inverse


def norm_back(hat, inverse, scales, grad):
    scaled = grad * scales
    first = jnp.mean(scaled, axis=-1, keepdims=True)
    second = jnp.mean(scaled * hat, axis=-1, keepdims=True)
    return inverse * (scaled - first - hat * second)


def lanes(head):
    lane = lax.broadcasted_iota(jnp.int32, (1, PAIR), 1)
    own = (lane < HD) if head == 0 else (lane >= HD)
    return own, lane - (HD if head == 0 else 0)


def key_bias(place_ref, valid_ref, length, shards):
    row = lax.broadcasted_iota(jnp.int32, (shards * length, 1), 0)
    position = row + place_ref[0] * length
    position = jnp.where(position >= shards * length, position - shards * length, position)
    allowed = position < valid_ref[pl.program_id(0)]
    return jnp.where(allowed, 0.0, NEG_FILL).astype(jnp.float32)


def augmented(values, head, extra):
    own, free = lanes(head)
    out = jnp.where(own, values, 0.0)
    for at, column in enumerate(extra):
        out = jnp.where(free == at, column, out)
    return out.astype(jnp.bfloat16)


def rows_with(values_t, head, extra):
    row = lax.broadcasted_iota(jnp.int32, (PAIR, 1), 0)
    own = (row < HD) if head == 0 else (row >= HD)
    free = row - (HD if head == 0 else 0)
    out = jnp.where(own, values_t, 0.0)
    for at, line in enumerate(extra):
        out = jnp.where(free == at, line, out)
    return out.astype(jnp.bfloat16)


def split_three(line):
    high = line.astype(jnp.bfloat16).astype(jnp.float32)
    rest = line - high
    middle = rest.astype(jnp.bfloat16).astype(jnp.float32)
    return high, middle, rest - middle


def forward_kernel(place_ref, valid_ref, q_ref, k_ref, v_ref, out_ref, lse_ref):
    shards, length, _ = q_ref.shape
    bias = key_bias(place_ref, valid_ref, length, shards)
    keys = k_ref[...].reshape(shards * length, PAIR).astype(jnp.float32)
    values = v_ref[...].reshape(shards * length, PAIR).astype(jnp.float32)
    keys_of = [augmented(keys, head, [bias]) for head in range(2)]
    values_of = [augmented(values, head, [1.0]).T for head in range(2)]
    for shard in range(shards):
        queries = q_ref[shard].astype(jnp.float32).T * HD**-0.5
        halves = []
        for head in range(2):
            scores = mat(keys_of[head], rows_with(queries, head, [1.0]))
            top = jnp.max(scores, axis=0, keepdims=True)
            weight = jnp.exp(scores - top).astype(jnp.bfloat16)
            part = mat(values_of[head], weight)
            at = HD * (1 - head)
            row_total = part[at : at + 1, :]
            halves.append(part[HD * head : HD * (head + 1), :] / row_total)
            lse_ref[0, 0, shard, head : head + 1, :] = top + jnp.log(row_total)
        out_ref[shard] = jnp.concatenate(halves, axis=0).T.astype(out_ref.dtype)


def backward_kernel(place_ref, valid_ref, q_ref, k_ref, v_ref, out_ref, lse_ref, da_ref, dq_ref, dk_ref, dv_ref):
    shards, length, _ = q_ref.shape
    bias = key_bias(place_ref, valid_ref, length, shards)
    keys = k_ref[...].reshape(shards * length, PAIR).astype(jnp.float32)
    values = v_ref[...].reshape(shards * length, PAIR).astype(jnp.float32)
    keys_of = [augmented(keys, head, [bias, 1.0, 1.0, 1.0]) for head in range(2)]
    values_of = [augmented(values, head, [1.0, 1.0, 1.0]) for head in range(2)]
    plain_keys = [augmented(keys, head, []).T for head in range(2)]
    dk = dv = None
    for shard in range(shards):
        queries = q_ref[shard].astype(jnp.float32) * HD**-0.5
        grads = da_ref[shard].astype(jnp.float32)
        queries_t, grads_t = queries.T, grads.T
        product = grads_t * out_ref[shard].astype(jnp.float32).T
        dq = None
        for head in range(2):
            lse = lse_ref[0, 0, shard, head : head + 1, :]
            delta = jnp.sum(product[HD * head : HD * (head + 1), :], axis=0, keepdims=True)
            scores = mat(keys_of[head], rows_with(queries_t, head, (1.0,) + split_three(-lse)))
            probs = jnp.exp(scores)
            moved = mat(values_of[head], rows_with(grads_t, head, split_three(-delta)))
            dscores = (probs * moved).astype(jnp.bfloat16)
            part_v = mat(probs.astype(jnp.bfloat16), augmented(grads, head, []))
            part_k = mat(dscores, augmented(queries, head, []))
            part_q = mat(plain_keys[head], dscores)
            dq = part_q if dq is None else dq + part_q
            dk = part_k if dk is None else dk + part_k
            dv = part_v if dv is None else dv + part_v
        dq_ref[shard] = (dq * HD**-0.5).T.astype(dq_ref.dtype)
    dk_ref[...] = dk.astype(dk_ref.dtype).reshape(dk_ref.shape)
    dv_ref[...] = dv.astype(dv_ref.dtype).reshape(dv_ref.shape)


def attention_specs(shards, length, pairs_all, first_pair):
    smem = pl.BlockSpec(memory_space=pltpu.SMEM)
    mixed = [
        pl.BlockSpec((shards, length, PAIR), lambda i, h, t=t: (0, i, t * pairs_all + first_pair + h))
        for t in range(3)
    ]
    plain = pl.BlockSpec((shards, length, PAIR), lambda i, h: (0, i, h))
    lse = pl.BlockSpec((1, 1, shards, 2, length), lambda i, h: (i, h, 0, 0, 0))
    return smem, mixed, plain, lse


def attend_forward(images, place, valid, mixed, first_pair, pairs):
    shards, rows, width3 = mixed.shape
    length = rows // images
    smem, block3, plain, lse = attention_specs(shards, length, width3 // 3 // PAIR, first_pair)
    work = shards * shards * rows * length * pairs
    return pl.pallas_call(
        forward_kernel,
        grid=(images, pairs),
        in_specs=[smem, smem] + block3,
        out_specs=[plain, lse],
        out_shape=[
            jax.ShapeDtypeStruct((shards, rows, pairs * PAIR), jnp.bfloat16),
            jax.ShapeDtypeStruct((images, pairs, shards, 2, length), jnp.float32),
        ],
        compiler_params=pltpu.CompilerParams(vmem_limit_bytes=40 * 2**20),
        cost_estimate=pl.CostEstimate(
            flops=8 * work * PAIR, bytes_accessed=8 * shards * rows * pairs * PAIR, transcendentals=2 * work,
        ),
    )(place, valid, mixed, mixed, mixed)


def attend_backward(images, place, valid, mixed, first_pair, pairs, attended, lse_in, da):
    shards, rows, width3 = mixed.shape
    length = rows // images
    smem, block3, plain, lse = attention_specs(shards, length, width3 // 3 // PAIR, first_pair)
    low = jax.ShapeDtypeStruct((shards, rows, pairs * PAIR), jnp.bfloat16)
    work = shards * shards * rows * length * pairs
    return pl.pallas_call(
        backward_kernel,
        grid=(images, pairs),
        in_specs=[smem, smem] + block3 + [plain, lse, plain],
        out_specs=[plain] * 3,
        out_shape=[low] * 3,
        compiler_params=pltpu.CompilerParams(vmem_limit_bytes=48 * 2**20),
        cost_estimate=pl.CostEstimate(
            flops=20 * work * PAIR, bytes_accessed=16 * shards * rows * pairs * PAIR, transcendentals=2 * work,
        ),
    )(place, valid, mixed, mixed, mixed, attended, lse_in, da)


def shift(values, shards, step):
    return lax.ppermute(values, "seq", [(i, (i + step) % shards) for i in range(shards)])


def everyone(values, shards, step_axis=0):
    return jnp.stack([values] + [shift(values, shards, -j) for j in range(1, shards)], axis=step_axis)


def in_order(values, shards, place):
    if shards == 2:
        other = shift(values, shards, 1)
        low = jnp.where(place == 0, values, other)
        high = jnp.where(place == 0, other, values)
        return jnp.stack([low, high])
    return lax.all_gather(values, "seq", axis=0)


def token_sum(values):
    return jnp.sum(values.astype(jnp.float32), axis=0)


MESH = pl.DeviceIdType.MESH


class Peers:
    def __init__(self, dps):
        self.dp = lax.axis_index("dp")
        self.seq = lax.axis_index("seq")
        self.levels = dps // 4
        self.z = self.dp // 4
        self.x = self.dp % 4 // 2
        self.core = self.dp % 2

    def up(self, step):
        return ((self.z + step) % self.levels * 4 + self.dp % 4, self.seq)

    def across(self):
        return (self.dp + 2 - 4 * self.x, self.seq)

    def sibling(self):
        return (self.dp + 1 - 2 * self.core, self.seq)

    def other(self):
        return (self.dp, 1 - self.seq)

    def all(self):
        return [self.up(s) for s in range(1, self.levels)] + [self.across(), self.sibling(), self.other()]

    def greet(self):
        barrier = pltpu.get_barrier_semaphore()
        for device in self.all():
            pl.semaphore_signal(barrier, inc=1, device_id=device, device_id_type=MESH)
        pl.semaphore_wait(barrier, len(self.all()))


def remote(src, dst, send, recv, device):
    return pltpu.make_async_remote_copy(
        src_ref=src, dst_ref=dst, send_sem=send, recv_sem=recv, device_id=device, device_id_type=MESH
    )


class Gather:
    def __init__(self, peers, src, full, sems, cut=(slice(None), slice(None))):
        levels = peers.levels
        at = (peers.z, peers.x, peers.core) + cut
        self.local = pltpu.make_async_copy(src, full.at[at], sems.at[0])
        self.first = [
            remote(src, full.at[at], sems.at[2 * s + 3], sems.at[2 * s + 4], peers.up(s)) for s in range(1, levels)
        ]
        column = full.at[(slice(None), peers.x, peers.core) + cut]
        self.second = remote(column, column, sems.at[1], sems.at[2], peers.across())
        half = full.at[(slice(None), slice(None), peers.core) + cut]
        self.third = remote(half, half, sems.at[3], sems.at[4], peers.sibling())

    def start(self):
        self.local.start()
        for copy in self.first:
            copy.start()

    def cross(self):
        self.local.wait()
        for copy in self.first:
            copy.wait_recv()
        self.second.start()

    def share(self):
        self.second.wait_recv()
        self.third.start()

    def arrive(self):
        self.third.wait_recv()

    def finish(self):
        for copy in self.first + [self.second, self.third]:
            copy.wait_send()


def gather_sems(levels):
    return 2 * levels + 3


def attend_pair(valid_ref, mixed, att, lse_ref, pair, base):
    shards, length, width3 = mixed.shape
    part = width3 // 3

    def columns(t):
        return pl.ds(pl.multiple_of(t * part + pair * PAIR, PAIR), PAIR)

    row = lax.broadcasted_iota(jnp.int32, (shards * length, 1), 0)
    bias = jnp.where(row < valid_ref[0], 0.0, NEG_FILL).astype(jnp.float32)
    keys = mixed[:, :, columns(1)].reshape(shards * length, PAIR).astype(jnp.float32)
    values = mixed[:, :, columns(2)].reshape(shards * length, PAIR).astype(jnp.float32)
    keys_of = [augmented(keys, head, [bias]) for head in range(2)]
    values_of = [augmented(values, head, [1.0]).T for head in range(2)]
    out_columns = pl.ds(pl.multiple_of(base + pair * PAIR, PAIR), PAIR)
    for shard in range(shards):
        queries = mixed[shard, :, columns(0)].astype(jnp.float32).T * HD**-0.5
        halves = []
        for head in range(2):
            scores = mat(keys_of[head], rows_with(queries, head, [1.0]))
            top = jnp.max(scores, axis=0, keepdims=True)
            weight = jnp.exp(scores - top).astype(jnp.bfloat16)
            product = mat(values_of[head], weight)
            at = HD * (1 - head)
            row_total = product[at : at + 1, :]
            halves.append(product[HD * head : HD * (head + 1), :] / row_total)
            lse_ref[pair, shard, head : head + 1, :] = top + jnp.log(row_total)
        att[shard, :, out_columns] = jnp.concatenate(halves, axis=0).T.astype(att.dtype)


def place_blocks(grad, z, value):
    rows = grad.shape[3]
    for x in range(2):
        for core in range(2):
            at = (2 * x + core) * rows
            grad[core, z, x] = value[at : at + rows, :].astype(grad.dtype)


ROW_TILE = 144
COL_TILE = 512


def forward_layer(
    valid_ref, tokens, cotangent, w_qkv, w_out, w_up, w_down, small,
    tok_out, dy_out, first_out, mixed_out, att_out, lse_ref, resid_out, second_out, act_out, slope_out,
    q_out, k_out, v_out, o_out, up_out, down_out, half_out, rows_ref, bup_ref,
    tok, first, mixed, att, resid, second, act, slope, fsmall, fq, fk, fv, fo, fup, fdown, my_up, dy, grad, cored, gsems, sems,
):
    levels = fq.shape[0]
    peers = Peers(4 * levels)
    p = peers.seq
    length, width = tokens.shape
    part = width // 2
    sub = fdown.shape[3]
    shard_rows = w_out.shape[0]
    peers.greet()

    send_tok = remote(tokens, tok.at[p], sems.at[0], sems.at[1], peers.other())
    send_tok.start()
    own = lambda t: w_qkv.at[:, pl.ds(pl.multiple_of(t * width + p * part, PAIR), part)]
    own_hidden = act.shape[2]
    half = own_hidden // 2
    low_up, high_up = (slice(None), pl.ds(0, half)), (slice(None), pl.ds(half, half))
    low_down, high_down = (pl.ds(0, sub // 2), slice(None)), (pl.ds(sub // 2, sub // 2), slice(None))
    down_at = lambda h: w_down.at[pl.ds(pl.multiple_of(p * sub + h * (sub // 2), 16), sub // 2)]
    g_small = Gather(peers, small, fsmall, gsems.at[0])
    g_q = Gather(peers, own(0), fq, gsems.at[1])
    g_k = Gather(peers, own(1), fk, gsems.at[2])
    g_v = Gather(peers, own(2), fv, gsems.at[3])
    g_out = Gather(peers, w_out, fo, gsems.at[4])
    g_up = Gather(peers, my_up.at[:, 0:half], fup, gsems.at[5], low_up)
    g_up2 = Gather(peers, my_up.at[:, half : 2 * half], fup, gsems.at[6], high_up)
    g_down = Gather(peers, down_at(0), fdown, gsems.at[7], low_down)
    g_down2 = Gather(peers, down_at(1), fdown, gsems.at[8], high_down)
    gathers = [g_small, g_q, g_k, g_v, g_out, g_up, g_up2, g_down, g_down2]
    for g in (g_small, g_q, g_k, g_v):
        g.start()
    for d in range(4 * levels):
        my_up[:, d * sub : (d + 1) * sub] = w_up[:, pl.ds(pl.multiple_of((2 * d + p) * sub, PAIR), sub)]

    own_tok = pltpu.make_async_copy(tokens, tok.at[p], sems.at[2])
    own_tok.start()
    own_dy = pltpu.make_async_copy(cotangent, dy.at[p], sems.at[3])
    own_dy.start()

    def normed(shard):
        @pl.loop(0, length // ROW_TILE)
        def _(i):
            at = pl.ds(pl.multiple_of(i * ROW_TILE, 16), ROW_TILE)
            resid[shard, at, :] = norm_parts(tok[shard, at, :].astype(jnp.float32))[0]

    g_small.cross()
    g_q.cross()
    own_tok.wait()
    normed(p)
    g_k.cross()
    g_v.cross()
    g_out.start()
    g_small.share()
    g_q.share()
    g_k.share()
    send_tok.wait_recv()
    normed(1 - p)
    g_small.arrive()
    vectors = fsmall[:, :, :, 0:shard_rows, :].reshape(width, SMALL).astype(jnp.float32).T
    rows_ref[...] = vectors[0:16, :]
    for d in range(4 * levels):
        at = (d // 4, d % 4 // 2, d % 2)
        pair_rows = fsmall[at + (slice(shard_rows, shard_rows + 16),)].astype(jnp.float32)
        bup_ref[0:1, d * sub : (d + 1) * sub] = jnp.where(p == 0, pair_rows[0:1, :sub], pair_rows[1:2, :sub])

    for shard in range(2):
        @pl.loop(0, length // ROW_TILE)
        def _(i):
            at = pl.ds(pl.multiple_of(i * ROW_TILE, 16), ROW_TILE)
            first[shard, at, :] = (resid[shard, at, :] * rows_ref[0:1, :] + rows_ref[2:3, :]).astype(jnp.bfloat16)

    own_columns = pl.ds(pl.multiple_of(p * part, PAIR), part)

    def project(t, full, bias):
        weight = full[...].reshape(width, part)
        @pl.loop(0, 2)
        def _(shard):
            out = mat(first[shard], weight)
            if bias is not None:
                out = out + rows_ref[bias : bias + 1, own_columns]
            mixed[shard, :, t * part : (t + 1) * part] = out.astype(jnp.bfloat16)

    saves = []

    def save(src, dst):
        copy = pltpu.make_async_copy(src, dst, sems.at[16 + len(saves)])
        saves.append(copy)
        copy.start()

    save(tok, tok_out)
    save(first, first_out)
    g_v.share()
    g_q.arrive()
    project(0, fq, 3)
    g_k.arrive()
    project(1, fk, None)
    g_out.cross()
    g_up.start()
    g_v.arrive()
    project(2, fv, 4)
    save(mixed, mixed_out)
    save(fq, q_out)
    save(fk, k_out)
    save(fv, v_out)

    pairs = part // PAIR
    att_copies = []
    for pair in range(pairs):
        columns = pl.ds(pl.multiple_of(p * part + pair * PAIR, PAIR), PAIR)
        att_copies.append(
            remote(
                att.at[:, :, columns], att.at[:, :, columns], sems.at[8 + 2 * pair], sems.at[9 + 2 * pair],
                peers.other(),
            )
        )

    @pl.loop(0, pairs)
    def _(pair):
        attend_pair(valid_ref, mixed, att, lse_ref, pair, p * part)
        for i in range(pairs):
            @pl.when(pair == i)
            def _():
                att_copies[i].start()
                if i == min(1, pairs - 1):
                    g_up.cross()
                    g_up2.start()
                    g_out.share()
                if i == pairs - 1:
                    g_up2.cross()
                    g_down.start()
                    g_up.share()

    g_out.arrive()
    save(fo, o_out)
    for copy in att_copies:
        copy.wait_recv()
    save(att, att_out)
    send_dy = remote(cotangent, dy.at[p], sems.at[4], sems.at[5], peers.other())
    send_dy.start()
    out_weight = fo[...].reshape(width, width)

    def finish_rows(shard):
        @pl.loop(0, length // ROW_TILE)
        def _(i):
            at = pl.ds(pl.multiple_of(i * ROW_TILE, 16), ROW_TILE)
            value = mat(att[shard, at, :], out_weight) + rows_ref[5:6, :] + tok[shard, at, :].astype(jnp.float32)
            resid[shard, at, :] = value
            hat, _ = norm_parts(value)
            second[shard, at, :] = (hat * rows_ref[1:2, :] + rows_ref[6:7, :]).astype(jnp.bfloat16)

    finish_rows(0)
    finish_rows(1)
    save(resid.at[p], resid_out)
    save(second, second_out)

    def into_hidden(first_tile, tiles):
        @pl.loop(0, 2 * tiles)
        def _(step):
            shard = step // tiles
            at = pl.ds(pl.multiple_of((first_tile + step % tiles) * COL_TILE, PAIR), COL_TILE)
            upward = mat(second[shard], fup[:, :, :, :, at].reshape(width, COL_TILE)) + bup_ref[0:1, at]
            cdf = 0.5 * (1.0 + lax.erf(upward * 0.5**0.5))
            act[shard, :, at] = (upward * cdf).astype(jnp.bfloat16)
            value = cdf + upward * (jnp.exp(-0.5 * upward * upward) * 0.3989422804014327)
            slope[shard, :, at] = value.astype(jnp.bfloat16)

    tiles = half // COL_TILE
    g_up.arrive()
    into_hidden(0, tiles)
    g_down.cross()
    g_down2.start()
    g_up2.share()
    g_up2.arrive()
    save(fup, up_out)
    into_hidden(tiles, tiles)
    save(act, act_out)
    save(slope, slope_out)
    g_down2.cross()
    g_down.share()
    own_dy.wait()
    send_dy.wait_recv()
    save(dy, dy_out)

    @pl.loop(0, levels)
    def _(z):
        at = pl.ds(pl.multiple_of(z * 4 * sub, PAIR), 4 * sub)
        value = dot_f32(act[:, :, at].reshape(2 * length, 4 * sub), dy[...].reshape(2 * length, width), ((0,), (0,)))
        place_blocks(grad, z, value)

    send_grad = remote(grad.at[1 - peers.core], cored, sems.at[6], sems.at[7], peers.sibling())
    send_grad.start()
    g_down.arrive()
    g_down2.share()
    g_down2.arrive()
    save(fdown, down_out)
    send_grad.wait_recv()

    @pl.loop(0, levels)
    def _(z):
        for x in range(2):
            total = grad[peers.core, z, x].astype(jnp.float32) + cored[z, x].astype(jnp.float32)
            grad[peers.core, z, x] = total.astype(jnp.bfloat16)

    save(grad.at[peers.core], half_out)
    send_grad.wait_send()
    send_tok.wait_send()
    send_dy.wait_send()
    for copy in att_copies:
        copy.wait_send()
    for g in gathers:
        g.finish()
    for copy in saves:
        copy.wait()


def run_forward(dps, tokens, cotangent, w_qkv, w_out, w_up, w_down, small, valid):
    length, width = tokens.shape
    levels = dps // 4
    part = width // 2
    shard_rows = w_out.shape[0]
    own_hidden = w_up.shape[1] // 2
    sub = w_down.shape[0] // 2
    pairs = part // PAIR
    bf, f32 = jnp.bfloat16, jnp.float32
    any_spec = pl.BlockSpec(memory_space=pl.ANY)
    vmem = pl.BlockSpec(memory_space=pltpu.VMEM)
    smem = pl.BlockSpec(memory_space=pltpu.SMEM)
    grid = (levels, 2, 2)
    whole = [
        ((2, length, width), bf),
        ((2, length, width), bf),
        ((2, length, width), bf),
        ((2, length, 3 * part), bf),
        ((2, length, width), bf),
        ((pairs, 2, 2, length), f32),
        ((length, width), f32),
        ((2, length, width), bf),
        ((2, length, own_hidden), bf),
        ((2, length, own_hidden), bf),
        (grid + (shard_rows, part), bf),
        (grid + (shard_rows, part), bf),
        (grid + (shard_rows, part), bf),
        (grid + (shard_rows, width), bf),
        (grid + (shard_rows, own_hidden), bf),
        (grid + (sub, width), bf),
        ((levels, 2, sub, width), bf),
        ((16, width), f32),
        ((8, own_hidden), f32),
    ]
    in_vmem = (5, 17, 18)
    scratch = [
        pltpu.VMEM((2, length, width), bf),
        pltpu.VMEM((2, length, width), bf),
        pltpu.VMEM((2, length, 3 * part), bf),
        pltpu.VMEM((2, length, width), bf),
        pltpu.VMEM((2, length, width), f32),
        pltpu.VMEM((2, length, width), bf),
        pltpu.VMEM((2, length, own_hidden), bf),
        pltpu.VMEM((2, length, own_hidden), bf),
        pltpu.VMEM(grid + (shard_rows + 16, SMALL), bf),
        pltpu.VMEM(grid + (shard_rows, part), bf),
        pltpu.VMEM(grid + (shard_rows, part), bf),
        pltpu.VMEM(grid + (shard_rows, part), bf),
        pltpu.VMEM(grid + (shard_rows, width), bf),
        pltpu.VMEM(grid + (shard_rows, own_hidden), bf),
        pltpu.VMEM(grid + (sub, width), bf),
        pltpu.VMEM((shard_rows, own_hidden), bf),
        pltpu.VMEM((2, length, width), bf),
        pltpu.VMEM((2, levels, 2, sub, width), bf),
        pltpu.VMEM((levels, 2, sub, width), bf),
        pltpu.SemaphoreType.DMA((9, gather_sems(levels))),
        pltpu.SemaphoreType.DMA((32,)),
    ]
    return pl.pallas_call(
        forward_layer,
        in_specs=[smem, any_spec, any_spec, vmem, vmem, vmem, vmem, vmem],
        out_specs=[vmem if i in in_vmem else any_spec for i in range(len(whole))],
        out_shape=[jax.ShapeDtypeStruct(*s) for s in whole],
        scratch_shapes=scratch,
        compiler_params=pltpu.CompilerParams(
            vmem_limit_bytes=62 * 2**20, collective_id=0, has_side_effects=True
        ),
        cost_estimate=pl.CostEstimate(flops=3 * 10**10, bytes_accessed=8 * 10**7, transcendentals=2 * 10**7),
    )(valid, tokens, cotangent, w_qkv, w_out, w_up, w_down, small)


class Scatter:
    def __init__(self, peers, grad, cored, crossed, risen, own, theirs, sems):
        core, x, z = peers.core, peers.x, peers.z
        self.peers, self.grad, self.cored, self.crossed, self.risen = peers, grad, cored, crossed, risen
        self.own = own
        self.first = remote(grad.at[1 - core], cored, sems.at[0], sems.at[1], peers.sibling())
        self.second = remote(grad.at[core, :, 1 - x], crossed, sems.at[2], sems.at[3], peers.across())
        self.third = [
            remote(
                grad.at[core, (z + s) % peers.levels, x], risen.at[s - 1], sems.at[2 * s + 4], sems.at[2 * s + 5],
                peers.up(s),
            )
            for s in range(1, peers.levels)
        ]
        self.fourth = remote(own, theirs, sems.at[4], sems.at[5], peers.other())

    def start(self):
        self.first.start()

    def cross(self):
        core = self.peers.core
        self.first.wait_recv()

        @pl.loop(0, self.peers.levels)
        def _(z):
            for x in range(2):
                total = self.grad[core, z, x].astype(jnp.float32) + self.cored[z, x].astype(jnp.float32)
                self.grad[core, z, x] = total.astype(self.grad.dtype)

        self.second.start()

    def rise(self):
        core, x = self.peers.core, self.peers.x
        self.second.wait_recv()

        @pl.loop(0, self.peers.levels)
        def _(z):
            total = self.grad[core, z, x].astype(jnp.float32) + self.crossed[z].astype(jnp.float32)
            self.grad[core, z, x] = total.astype(self.grad.dtype)

        for copy in self.third:
            copy.start()

    def own_piece(self):
        return self.grad[self.peers.core, self.peers.z, self.peers.x]

    def over(self):
        for copy in self.third:
            copy.wait_recv()
        total = self.own_piece().astype(jnp.float32)
        for s in range(self.peers.levels - 1):
            total = total + self.risen[s].astype(jnp.float32)
        self.own[...] = total.astype(self.own.dtype)
        self.fourth.start()

    def arrive(self):
        self.fourth.wait_recv()

    def finish(self):
        for copy in [self.first, self.second, self.fourth] + self.third:
            copy.wait_send()


class LateScatter(Scatter):
    def __init__(self, peers, halves, kept, crossed, risen, own, theirs, sems):
        x, z = peers.x, peers.z
        self.peers, self.kept, self.crossed, self.risen, self.own = peers, kept, crossed, risen, own
        self.second = remote(halves.at[:, 1 - x], crossed, sems.at[2], sems.at[3], peers.across())
        self.local = pltpu.make_async_copy(halves.at[:, x], kept, sems.at[0])
        self.third = [
            remote(
                kept.at[(z + s) % peers.levels], risen.at[s - 1], sems.at[2 * s + 4], sems.at[2 * s + 5], peers.up(s)
            )
            for s in range(1, peers.levels)
        ]
        self.fourth = remote(own, theirs, sems.at[4], sems.at[5], peers.other())

    def start(self):
        self.second.start()
        self.local.start()

    def rise(self):
        self.local.wait()
        self.second.wait_recv()

        @pl.loop(0, self.peers.levels)
        def _(z):
            total = self.kept[z].astype(jnp.float32) + self.crossed[z].astype(jnp.float32)
            self.kept[z] = total.astype(self.kept.dtype)

        for copy in self.third:
            copy.start()

    def own_piece(self):
        return self.kept[self.peers.z]

    def finish(self):
        for copy in [self.second, self.fourth] + self.third:
            copy.wait_send()


def scatter_sems(levels):
    return 2 * levels + 4


def scatter_buffers(levels, rows, columns, dtype):
    return [
        pltpu.VMEM((2, levels, 2, rows, columns), dtype),
        pltpu.VMEM((levels, 2, rows, columns), dtype),
        pltpu.VMEM((levels, rows, columns), dtype),
        pltpu.VMEM((levels - 1, rows, columns), dtype),
    ]


def attend_pair_back(valid_ref, mixed, att, lse_ref, datt, dmix, sums, pair, base, place):
    shards, length, width3 = mixed.shape
    part = width3 // 3
    group, within = pair // 2, pair % 2
    wide = dmix.shape[3] // 3

    def columns(t):
        return pl.ds(pl.multiple_of(t * part + pair * PAIR, PAIR), PAIR)

    def out_columns(t):
        return pl.ds(pl.multiple_of(t * wide + within * PAIR, PAIR), PAIR)

    own_columns = pl.ds(pl.multiple_of(base + pair * PAIR, PAIR), PAIR)
    da_columns = pl.ds(pl.multiple_of(pair * PAIR, PAIR), PAIR)
    row = lax.broadcasted_iota(jnp.int32, (shards * length, 1), 0)
    bias = jnp.where(row < valid_ref[0], 0.0, NEG_FILL).astype(jnp.float32)
    keys = mixed[:, :, columns(1)].reshape(shards * length, PAIR).astype(jnp.float32)
    values = mixed[:, :, columns(2)].reshape(shards * length, PAIR).astype(jnp.float32)
    keys_of = [augmented(keys, head, [bias, 1.0, 1.0, 1.0]) for head in range(2)]
    values_of = [augmented(values, head, [1.0, 1.0, 1.0]) for head in range(2)]
    plain_keys = [augmented(keys, head, []).T for head in range(2)]
    dk = dv = None
    dq_sum = None
    for shard in range(shards):
        queries = mixed[shard, :, columns(0)].astype(jnp.float32) * HD**-0.5
        grads = datt[shard, :, da_columns].astype(jnp.float32)
        queries_t, grads_t = queries.T, grads.T
        product = grads_t * att[shard, :, da_columns].astype(jnp.float32).T
        dq = None
        for head in range(2):
            lse = lse_ref[pair, shard, head : head + 1, :]
            delta = jnp.sum(product[HD * head : HD * (head + 1), :], axis=0, keepdims=True)
            scores = mat(keys_of[head], rows_with(queries_t, head, (1.0,) + split_three(-lse)))
            probs = jnp.exp(scores)
            moved = mat(values_of[head], rows_with(grads_t, head, split_three(-delta)))
            dscores = (probs * moved).astype(jnp.bfloat16)
            part_v = mat(probs.astype(jnp.bfloat16), augmented(grads, head, []))
            part_k = mat(dscores, augmented(queries, head, []))
            part_q = mat(plain_keys[head], dscores)
            dq = part_q if dq is None else dq + part_q
            dk = part_k if dk is None else dk + part_k
            dv = part_v if dv is None else dv + part_v
        dq = (dq * HD**-0.5).T.astype(jnp.bfloat16)
        dmix[group, shard, :, out_columns(0)] = dq
        total = jnp.sum(dq.astype(jnp.float32), axis=0, keepdims=True)
        dq_sum = total if dq_sum is None else dq_sum + total
    dk, dv = dk.astype(jnp.bfloat16), dv.astype(jnp.bfloat16)
    dmix[group, :, :, out_columns(1)] = dk.reshape(shards, length, PAIR)
    dmix[group, :, :, out_columns(2)] = dv.reshape(shards, length, PAIR)
    sums[3:4, own_columns] = dq_sum
    sums[4:5, own_columns] = jnp.sum(dv.astype(jnp.float32), axis=0, keepdims=True)


def column_sum(values):
    return jnp.sum(values, axis=0, keepdims=True)


def backward_layer(
    valid_ref, rows_ref, lse_ref,
    tok_in, dy_in, first_in, mixed_in, att_in, resid_in, second_in, act_in, slope_in,
    q_in, k_in, v_in, o_in, up_in, down_in, half_in,
    otok_ref, orecv_ref, gtok_ref, gqkv_ref, gout_ref, gup_ref, gdown_ref, gsmall_ref,
    down1, down2, down3, up0, up1, up2, up3, out0, out1, out2, out3, qa0, qa1, qa2, qa3, qb0, qb1, qb2, qb3,
    sm0, sm1, sm2, sm3, down_sum, up_sum, qkv_sum, out_own, out_theirs, sm_own, sm_theirs,
    ysend, yrecv, osend, dres, datt, datt_send, sums, dub, ssems, sems,
):
    levels = down2.shape[0]
    peers = Peers(4 * levels)
    p, q = peers.seq, 1 - peers.seq
    _, length, width = dy_in.shape
    part = width // 2
    own_hidden = act_in.shape[2]
    sub = own_hidden // (4 * levels)
    shard_rows = width // (4 * levels)
    wide = part // 2
    bf, f32 = jnp.bfloat16, jnp.float32
    tiles = length // ROW_TILE
    peers.greet()

    s_down = LateScatter(peers, half_in, down1, down2, down3, down_sum.at[p], down_sum.at[p], ssems.at[0])
    s_up = Scatter(peers, up0, up1, up2, up3, up_sum.at[p], up_sum.at[p], ssems.at[1])
    s_out = Scatter(peers, out0, out1, out2, out3, out_own, out_theirs, ssems.at[2])
    s_qa = Scatter(peers, qa0, qa1, qa2, qa3, qkv_sum.at[p, 0], qkv_sum.at[p, 0], ssems.at[3])
    s_qb = Scatter(peers, qb0, qb1, qb2, qb3, qkv_sum.at[p, 1], qkv_sum.at[p, 1], ssems.at[4])
    s_small = Scatter(peers, sm0, sm1, sm2, sm3, sm_own, sm_theirs, ssems.at[5])
    middle = length // 2

    def halves(at):
        rows = [slice(0, middle), slice(middle, length)]
        return [
            remote(ysend.at[r], yrecv.at[r], sems.at[at + 2 * i], sems.at[at + 1 + 2 * i], peers.other())
            for i, r in enumerate(rows)
        ]

    send_two, send_one = halves(8), halves(12)
    send_datt = [
        remote(
            datt_send.at[:, g * wide : (g + 1) * wide], datt.at[p, :, g * wide : (g + 1) * wide],
            sems.at[2 * g], sems.at[1 + 2 * g], peers.other(),
        )
        for g in range(2)
    ]
    send_out = remote(osend, orecv_ref, sems.at[4], sems.at[5], peers.other())
    s_down.start()
    sums[...] = jnp.zeros_like(sums)

    def row_at(i):
        return pl.ds(pl.multiple_of(i * ROW_TILE, 16), ROW_TILE)

    def load(src, dst, at):
        copy = pltpu.make_async_copy(src, dst, sems.at[at])
        copy.start()
        return copy

    def hidden_phase(dy, act, du, fdown, fup, second):
        early = [load(dy_in.at[q], dy.at[q], 16), load(down_in, fdown, 17), load(slope_in.at[q], du.at[q], 18)]
        copies = [
            load(up_in, fup, 19), load(dy_in.at[p], dy.at[p], 20), load(slope_in.at[p], du.at[p], 21),
            load(second_in, second, 22), load(act_in.at[q], act, 23),
        ]
        for copy in early:
            copy.wait()

        def into_hidden(shard):
            @pl.loop(0, levels)
            def _(z):
                at = pl.ds(pl.multiple_of(z * 4 * sub, PAIR), 4 * sub)
                grad = dot_f32(dy[shard], fdown[z].reshape(4 * sub, width), ((1,), (1,)))
                value = (grad * du[shard, :, at].astype(f32)).astype(bf)
                du[shard, :, at] = value
                dub[pl.ds(shard, 1), at] = column_sum(value.astype(f32))

        def back_second(shard, target, rows):
            @pl.loop(0, levels)
            def _(z):
                at = pl.ds(pl.multiple_of(z * 4 * shard_rows, PAIR), 4 * shard_rows)
                value = dot_f32(du[shard, rows, :], fup[z].reshape(4 * shard_rows, own_hidden), ((1,), (1,)))
                target[rows, at] = value.astype(target.dtype)

        into_hidden(q)
        copies[0].wait()
        for i in range(2):
            back_second(q, ysend, slice(i * middle, (i + 1) * middle))
            send_two[i].start()
        copies[1].wait()
        copies[2].wait()
        into_hidden(p)
        copies[3].wait()

        @pl.loop(0, levels)
        def _(z):
            at = pl.ds(pl.multiple_of(z * 4 * shard_rows, PAIR), 4 * shard_rows)
            value = dot_f32(
                second[:, :, at].reshape(2 * length, 4 * shard_rows), du[...].reshape(2 * length, own_hidden), ((0,), (0,))
            )
            place_blocks(up0, z, value)

        s_up.start()
        back_second(p, dres, slice(0, length))
        copies[4].wait()

        @pl.loop(0, width // COL_TILE)
        def _(t):
            at = pl.ds(pl.multiple_of(t * COL_TILE, PAIR), COL_TILE)
            weight = fdown[:, :, :, :, at].reshape(own_hidden, COL_TILE)
            osend[:, at] = mat(act[...], weight).astype(bf)

        s_down.rise()
        s_up.cross()

    pl.run_scoped(
        hidden_phase,
        pltpu.VMEM((2, length, width), bf),
        pltpu.VMEM((length, own_hidden), bf),
        pltpu.VMEM((2, length, own_hidden), bf),
        pltpu.VMEM(down_in.shape, bf),
        pltpu.VMEM(up_in.shape, bf),
        pltpu.VMEM((2, length, width), bf),
    )

    def norm_phase(dy, resid, att, fo, dbr):
        copies = [
            load(dy_in.at[p], dy, 16), load(resid_in, resid, 17), load(o_in, fo, 18), load(att_in.at[p], att, 19),
        ]
        copies[0].wait()
        copies[1].wait()

        def through_norm(i):
            at = row_at(i)
            hat, inverse = norm_parts(resid[at, :])
            grad = dres[at, :] + yrecv[at, :].astype(f32)
            grad_y = dy[at, :].astype(f32)
            value = grad_y + norm_back(hat, inverse, rows_ref[1:2, :], grad)
            dres[at, :] = value
            low = value.astype(bf)
            dbr[at, :] = low
            sums[1:2, :] += column_sum(grad * hat)
            sums[5:6, :] += column_sum(low.astype(f32))
            sums[6:7, :] += column_sum(grad)
            sums[7:8, :] += column_sum(grad_y)

        for i in range(2):
            send_two[i].wait_recv()
            pl.loop(i * (tiles // 2), (i + 1) * (tiles // 2))(through_norm)

        copies[2].wait()
        half = levels // 2
        for g in range(2):
            at = slice(g * wide, (g + 1) * wide)
            blocks = pl.ds(q * half + g * (half // 2), half // 2)
            value = dot_f32(dbr[...], fo[blocks].reshape(wide, width), ((1,), (1,)))
            datt_send[:, at] = value.astype(bf)
            send_datt[g].start()
        datt[p] = dot_f32(dbr[...], fo[pl.ds(p * half, half)].reshape(part, width), ((1,), (1,))).astype(bf)
        copies[3].wait()

        @pl.loop(0, levels)
        def _(z):
            at = pl.ds(pl.multiple_of(z * 4 * shard_rows, PAIR), 4 * shard_rows)
            place_blocks(out0, z, dot_f32(att[:, at], dbr[...], ((0,), (0,))))

        s_out.start()
        send_datt[0].wait_recv()
        send_out.start()
        s_up.rise()

    pl.run_scoped(
        norm_phase,
        pltpu.VMEM((length, width), bf),
        pltpu.VMEM((length, width), f32),
        pltpu.VMEM((length, width), bf),
        pltpu.VMEM(o_in.shape, bf),
        pltpu.VMEM((length, width), bf),
    )

    def heads_phase(dmix, first, fq, fk, fv):
        loaded = [load(first_in, first, 16), load(q_in, fq, 19), load(k_in, fk, 20), load(v_in, fv, 21)]

        def weight_grad(g, grad):
            @pl.loop(0, levels)
            def _(z):
                at = pl.ds(pl.multiple_of(z * 4 * shard_rows, PAIR), 4 * shard_rows)
                value = dot_f32(
                    first[:, :, at].reshape(2 * length, 4 * shard_rows),
                    dmix[g].reshape(2 * length, 3 * wide), ((0,), (0,)),
                )
                place_blocks(grad, z, value)

        own_part = pl.ds(pl.multiple_of(p * part, PAIR), part)

        def attention_phase(mixed, att):
            one, two = load(mixed_in, mixed, 17), load(att_in.at[:, :, own_part], att, 18)
            one.wait()
            two.wait()
            for copy in loaded:
                copy.wait()

            @pl.loop(0, part // PAIR)
            def _(pair):
                attend_pair_back(valid_ref, mixed, att, lse_ref, datt, dmix, sums, pair, p * part, p)

                @pl.when(pair == 0)
                def _():
                    s_out.cross()
                    s_down.over()

                @pl.when(pair == 1)
                def _():
                    weight_grad(0, qa0)
                    s_qa.start()
                    s_out.rise()
                    send_datt[1].wait_recv()

                @pl.when(pair == 2)
                def _():
                    s_qa.cross()
                    s_up.over()

                @pl.when(pair == 3)
                def _():
                    s_qa.rise()
                    s_out.over()

        pl.run_scoped(
            attention_phase,
            pltpu.VMEM(mixed_in.shape, bf),
            pltpu.VMEM((2, length, part), bf),
        )

        def last_phase(tok, part_one, act, fdown, resid, others):
            copies = [
                load(tok_in, tok, 17), load(act_in.at[p], act, 18), load(down_in, fdown, 19), load(resid_in, resid, 20)
            ]
            for copy in send_two:
                copy.wait_send()

            def back_first(shard, target, rows):
                @pl.loop(0, levels)
                def _(z):
                    at = pl.ds(pl.multiple_of(z * 4 * shard_rows, PAIR), 4 * shard_rows)
                    total = None
                    for g in range(2):
                        for t, full in enumerate((fq, fk, fv)):
                            value = dot_f32(
                                dmix[g, shard, rows, t * wide : (t + 1) * wide],
                                full[z, :, :, :, g * wide : (g + 1) * wide].reshape(4 * shard_rows, wide),
                                ((1,), (1,)),
                            )
                            total = value if total is None else total + value
                    target[rows, at] = total.astype(target.dtype)

            def gain_sums(shard, source):
                @pl.loop(0, tiles)
                def _(i):
                    at = row_at(i)
                    hat, _ = norm_parts(tok[shard, at, :].astype(f32))
                    grad = source[at, :].astype(f32)
                    sums[0:1, :] += column_sum(grad * hat)
                    sums[2:3, :] += column_sum(grad)

            for i in range(2):
                back_first(q, part_one, slice(i * middle, (i + 1) * middle))

                @pl.loop(i * (tiles // 2), (i + 1) * (tiles // 2))
                def _(t):
                    ysend[row_at(t), :] = part_one[row_at(t), :].astype(bf)

                send_one[i].start()
            weight_grad(1, qb0)
            s_qb.start()
            copies[0].wait()
            gain_sums(q, part_one)
            back_first(p, part_one, slice(0, length))
            s_qb.cross()
            gain_sums(p, part_one)

            vectors = jnp.concatenate([sums[...], jnp.zeros((SMALL - 16, width), f32)], axis=0).T
            ups = dub[0:1, :] + dub[1:2, :]
            line = lax.broadcasted_iota(jnp.int32, (8, 1), 0)
            for d in range(4 * levels):
                at = (d % 2, d // 4, d % 4 // 2)
                sm0[at + (slice(0, shard_rows),)] = vectors[d * shard_rows : (d + 1) * shard_rows, :]
                sm0[at + (slice(shard_rows, shard_rows + 8),)] = jnp.where(line == p, ups[:, d * sub : (d + 1) * sub], 0.0)
            s_small.start()
            for copy in copies[1:]:
                copy.wait()
            send_out.wait_recv()
            fetched = load(orecv_ref, others, 18)
            s_small.cross()
            s_qb.rise()
            s_small.rise()
            s_qa.over()
            fetched.wait()

            @pl.loop(0, width // COL_TILE)
            def _(t):
                at = pl.ds(pl.multiple_of(t * COL_TILE, PAIR), COL_TILE)
                value = mat(act[...], fdown[:, :, :, :, at].reshape(own_hidden, COL_TILE))
                value = value + resid[:, at] + rows_ref[7:8, at] + others[:, at].astype(f32)
                others[:, at] = value.astype(bf)

            finished = load(others, otok_ref, 19)
            s_out.arrive()
            gout_ref[...] = out_own[...].astype(f32) + out_theirs[...].astype(f32)
            s_small.over()
            s_qb.over()
            s_down.arrive()
            s_up.arrive()
            for side in range(2):
                resid[side * sub : (side + 1) * sub, :] = down_sum[side].astype(f32)
                for d in range(4 * levels):
                    to = (2 * d + side) * sub
                    gup_ref[:, to : to + sub] = up_sum[side, :, d * sub : (d + 1) * sub].astype(f32)

            cast = load(resid.at[0 : 2 * sub], gdown_ref, 22)

            def through_norm(i):
                at = row_at(i)
                hat, inverse = norm_parts(tok[p, at, :].astype(f32))
                grad = part_one[at, :] + yrecv[at, :].astype(f32)
                part_one[at, :] = dres[at, :] + norm_back(hat, inverse, rows_ref[0:1, :], grad)

            written = []
            for i in range(2):
                send_one[i].wait_recv()
                pl.loop(i * (tiles // 2), (i + 1) * (tiles // 2))(through_norm)
                rows = slice(i * middle, (i + 1) * middle)
                written.append(load(part_one.at[rows], gtok_ref.at[rows], 20 + i))
            s_small.arrive()
            gsmall_ref[...] = sm_own[...] + sm_theirs[...]
            for g, s in enumerate((s_qa, s_qb)):
                s.arrive()
                for side in range(2):
                    for t in range(3):
                        to = t * width + side * part + g * wide
                        gqkv_ref[:, to : to + wide] = qkv_sum[side, g, :, t * wide : (t + 1) * wide].astype(f32)
            for copy in written + [finished, cast]:
                copy.wait()

        pl.run_scoped(
            last_phase,
            pltpu.VMEM((2, length, width), bf),
            pltpu.VMEM((length, width), f32),
            pltpu.VMEM((length, own_hidden), bf),
            pltpu.VMEM(down_in.shape, bf),
            pltpu.VMEM((length, width), f32),
            pltpu.VMEM((length, width), bf),
        )

    pl.run_scoped(
        heads_phase,
        pltpu.VMEM((2, 2, length, 3 * wide), bf),
        pltpu.VMEM((2, length, width), bf),
        pltpu.VMEM(q_in.shape, bf),
        pltpu.VMEM(k_in.shape, bf),
        pltpu.VMEM(v_in.shape, bf),
    )
    send_out.wait_send()
    for copy in send_one + send_datt:
        copy.wait_send()
    for s in (s_down, s_up, s_out, s_qa, s_qb, s_small):
        s.finish()


def run_backward(dps, valid, vectors, lse, tok, dy, first, mixed, att, resid, second, act, slope, fq, fk, fv, fo, fup, fdown, half):
    levels = dps // 4
    _, length, width = dy.shape
    part = width // 2
    wide = part // 2
    own_hidden = act.shape[2]
    shard_rows, sub = width // dps, own_hidden // dps
    bf, f32 = jnp.bfloat16, jnp.float32
    any_spec = pl.BlockSpec(memory_space=pl.ANY)
    vmem = pl.BlockSpec(memory_space=pltpu.VMEM)
    smem = pl.BlockSpec(memory_space=pltpu.SMEM)
    whole = [
        ((length, width), bf),
        ((length, width), bf),
        ((length, width), f32),
        ((shard_rows, 6 * part), f32),
        ((shard_rows, width), f32),
        ((shard_rows, 2 * own_hidden), f32),
        ((2 * sub, width), f32),
        ((shard_rows + 8, SMALL), f32),
    ]
    scratch = (
        [
            pltpu.VMEM((levels, sub, width), bf),
            pltpu.VMEM((levels, sub, width), bf),
            pltpu.VMEM((levels - 1, sub, width), bf),
        ]
        + scatter_buffers(levels, shard_rows, own_hidden, bf)
        + scatter_buffers(levels, shard_rows, width, bf)
        + scatter_buffers(levels, shard_rows, 3 * wide, bf)
        + scatter_buffers(levels, shard_rows, 3 * wide, bf)
        + scatter_buffers(levels, shard_rows + 8, SMALL, f32)
        + [
            pltpu.VMEM((2, sub, width), bf),
            pltpu.VMEM((2, shard_rows, own_hidden), bf),
            pltpu.VMEM((2, 2, shard_rows, 3 * wide), bf),
            pltpu.VMEM((shard_rows, width), bf),
            pltpu.VMEM((shard_rows, width), bf),
            pltpu.VMEM((shard_rows + 8, SMALL), f32),
            pltpu.VMEM((shard_rows + 8, SMALL), f32),
            pltpu.VMEM((length, width), bf),
            pltpu.VMEM((length, width), bf),
            pltpu.VMEM((length, width), bf),
            pltpu.VMEM((length, width), f32),
            pltpu.VMEM((2, length, part), bf),
            pltpu.VMEM((length, part), bf),
            pltpu.VMEM((16, width), f32),
            pltpu.VMEM((8, own_hidden), f32),
            pltpu.SemaphoreType.DMA((6, scatter_sems(levels))),
            pltpu.SemaphoreType.DMA((24,)),
        ]
    )
    return pl.pallas_call(
        backward_layer,
        in_specs=[smem, vmem, vmem] + [any_spec] * 16,
        out_specs=[any_spec] * 3 + [vmem] * 3 + [any_spec, vmem],
        out_shape=[jax.ShapeDtypeStruct(*s) for s in whole],
        scratch_shapes=scratch,
        compiler_params=pltpu.CompilerParams(
            vmem_limit_bytes=62 * 2**20, collective_id=1, has_side_effects=True
        ),
        cost_estimate=pl.CostEstimate(flops=5 * 10**10, bytes_accessed=8 * 10**7, transcendentals=2 * 10**7),
    )(valid, vectors, lse, tok, dy, first, mixed, att, resid, second, act, slope, fq, fk, fv, fo, fup, fdown, half)


def per_device_pair(tokens, w_qkv, w_out, w_up, w_down, gains, biases, up_bias, valid, cotangent):
    _, length, width = tokens.shape
    shard_rows = w_qkv.shape[0]
    dps = lax.axis_size("dp")
    sub = w_down.shape[0] // 2

    smalls = jnp.concatenate([gains, biases], axis=1)
    smalls = jnp.concatenate(
        [
            jnp.pad(smalls, ((0, 0), (0, SMALL - smalls.shape[1]))),
            jnp.pad(up_bias.reshape(2, sub), ((0, 14), (0, 0))),
        ],
        axis=0,
    )
    (
        tok, dy, first, mixed, att, lse, residual, second, act, slope, fq, fk, fv, fo, fup, fdown, half, vectors, _
    ) = run_forward(
        dps, tokens.reshape(length, width), cotangent.reshape(length, width), w_qkv, w_out, w_up, w_down, smalls, valid
    )
    out_tokens, _, grad_tokens, grad_qkv, grad_out, grad_up, grad_down, grad_small = run_backward(
        dps, valid, vectors, lse, tok, dy, first, mixed, att, residual, second, act, slope, fq, fk, fv, fo, fup, fdown, half
    )
    return (
        out_tokens.reshape(tokens.shape),
        grad_tokens.reshape(tokens.shape),
        grad_qkv,
        grad_out,
        grad_up,
        grad_down,
        grad_small[:shard_rows, :2],
        grad_small[:shard_rows, 2:8],
        grad_small[shard_rows : shard_rows + 2, :].reshape(-1),
    )


def per_device(tokens, w_qkv, w_out, w_up, w_down, gains, biases, up_bias, valid, cotangent):
    images, length, width = tokens.shape
    rows = images * length
    shard_rows = w_qkv.shape[0]
    hidden = w_up.shape[1]
    ups = up_bias.shape[0] // shard_rows
    shards = lax.axis_size("seq")
    dps = lax.axis_size("dp")
    at = lax.axis_index("seq").astype(jnp.int32)
    place = at.reshape(1)
    part = width // shards
    own_hidden = hidden // shards
    sub = w_down.shape[0] // shards
    pairs_all = part // PAIR

    gather = functools.partial(lax.all_gather, axis_name="dp", axis=0, tiled=True)
    scatter = functools.partial(lax.psum_scatter, axis_name="dp", scatter_dimension=0, tiled=True)

    def pick(values, axis):
        return lax.dynamic_index_in_dim(values, at, axis, keepdims=False)

    smalls = jnp.concatenate([gains, biases, up_bias.reshape(shard_rows, ups)], axis=1)
    smalls = jnp.pad(smalls, ((0, 0), (0, SMALL - smalls.shape[1])))
    part_qkv = pick(w_qkv.reshape(shard_rows, 3, shards, part), 2).reshape(shard_rows, 3 * part)
    part_up = pick(w_up.reshape(shard_rows, dps, shards, sub), 2).reshape(shard_rows, own_hidden)
    part_down = pick(w_down.reshape(shards, sub, width), 0)
    full_qkvs = gather(jnp.concatenate([part_qkv, smalls], axis=1))
    w_out, full_qkvs = lax.optimization_barrier((w_out, full_qkvs))
    full_out = gather(w_out)
    part_up, full_out = lax.optimization_barrier((part_up, full_out))
    full_up = gather(part_up)
    part_down, full_up = lax.optimization_barrier((part_down, full_up))
    full_down = gather(part_down)

    flat_tokens = tokens.reshape(rows, width)
    flat_grad = cotangent.reshape(rows, width)
    all_tokens = everyone(flat_tokens, shards)
    flat_grad, all_tokens = lax.optimization_barrier((flat_grad, all_tokens))
    all_grad = everyone(flat_grad, shards).reshape(shards * rows, width)

    full_qkv = full_qkvs[:, : 3 * part]
    small = full_qkvs[:, 3 * part :].astype(jnp.float32).T
    gain_one, gain_two = small[0], small[1]
    bias_one, bias_q, bias_v, bias_out, bias_two, bias_down = (small[2 + i] for i in range(6))
    bias_up = pick(small[8 : 8 + ups].T.reshape(dps, shards, sub), 1).reshape(-1)
    bias_mixed = jnp.concatenate(
        [pick(bias_q.reshape(shards, part), 0), jnp.zeros((part,), jnp.float32), pick(bias_v.reshape(shards, part), 0)]
    )

    every_tokens = all_tokens.reshape(shards * rows, width).astype(jnp.float32)
    hat_one, inverse_one = norm_parts(every_tokens)
    first = (hat_one * gain_one + bias_one).astype(jnp.bfloat16)
    mixed = (mat(first, full_qkv) + bias_mixed).astype(jnp.bfloat16).reshape(shards, rows, 3 * part)

    groups = GROUPS if pairs_all % GROUPS == 0 else 1
    pairs = pairs_all // groups
    wide = pairs * PAIR
    forward = [attend_forward(images, place, valid, mixed, g * pairs, pairs) for g in range(groups)]
    blocks = []
    for j in range(shards):
        for g in range(groups):
            attended = forward[g][0]
            if j > 0:
                attended = jnp.roll(shift(attended, shards, -j), j, axis=0)
            blocks.append(attended.reshape(shards * rows, wide))
    merged = jnp.concatenate(blocks, axis=1)
    turned_out = jnp.roll(full_out, -at * part, axis=0)

    branch = mat(merged, turned_out) + bias_out
    residual = every_tokens + branch
    hat_two, inverse_two = norm_parts(residual)
    second = (hat_two * gain_two + bias_two).astype(jnp.bfloat16)
    upward = mat(second, full_up) + bias_up
    cdf = 0.5 * (1.0 + lax.erf(upward * 0.5**0.5))
    activated = (upward * cdf).astype(jnp.bfloat16)
    slope = cdf + upward * (jnp.exp(-0.5 * upward * upward) * 0.3989422804014327)
    slope = slope.astype(jnp.bfloat16)

    grad_act = dot_f32(all_grad, full_down, ((1,), (1,)))
    grad_upward = (grad_act * slope.astype(jnp.float32)).astype(jnp.bfloat16)

    def summed(left, right, dims):
        parts = [
            dot_f32(left[j * rows : (j + 1) * rows], right, dims) for j in range(shards)
        ]
        total = parts[0]
        for j in range(1, shards):
            total = total + shift(parts[j].astype(jnp.bfloat16), shards, j).astype(jnp.float32)
        return total

    grad_second = summed(grad_upward, full_up, ((1,), (1,)))
    grad_down = dot_f32(activated, all_grad, ((0,), (0,))).astype(jnp.bfloat16)
    piece_down = scatter(grad_down)
    grad_up = dot_f32(second, grad_upward, ((0,), (0,))).astype(jnp.bfloat16)
    grad_up, piece_down = lax.optimization_barrier((grad_up, piece_down))
    piece_up = scatter(grad_up)

    own_hat = hat_two[:rows]
    grad_resid = flat_grad.astype(jnp.float32) + norm_back(own_hat, inverse_two[:rows], gain_two, grad_second)
    grad_gain_two, grad_bias_two = token_sum(grad_second * own_hat), token_sum(grad_second)
    grad_branch = grad_resid.astype(jnp.bfloat16)
    grad_merged = dot_f32(grad_branch, turned_out, ((1,), (1,))).astype(jnp.bfloat16)
    received = [None] * shards
    for g in range(groups):
        lo = g * wide
        blocks = [grad_merged[:, lo : lo + wide]] + [None] * (shards - 1)
        for j in range(1, shards):
            blocks[shards - j] = shift(grad_merged[:, j * part + lo : j * part + lo + wide], shards, j)
        received[g] = jnp.stack(blocks)

    grad_out = dot_f32(merged[:rows], grad_branch, ((0,), (0,))).astype(jnp.bfloat16)
    grad_out = jnp.roll(grad_out, at * part, axis=0)
    grad_out, piece_up = lax.optimization_barrier((grad_out, piece_up))
    piece_out = scatter(grad_out)

    backs = [
        attend_backward(images, place, valid, mixed, g * pairs, pairs, *forward[g], received[g]) for g in range(groups)
    ]
    grad_mixed = jnp.concatenate(
        [back[t].reshape(shards * rows, wide) for t in range(3) for back in backs], axis=1
    )
    grad_first = summed(grad_mixed, full_qkv, ((1,), (1,)))
    grad_qkv = dot_f32(first, grad_mixed, ((0,), (0,))).astype(jnp.bfloat16)

    grad_tokens = grad_resid + norm_back(hat_one[:rows], inverse_one[:rows], gain_one, grad_first)
    grad_gain_one, grad_bias_one = token_sum(grad_first * hat_one[:rows]), token_sum(grad_first)

    def spread(values, before):
        out = jnp.zeros((before, shards, values.size // before), jnp.float32)
        return lax.dynamic_update_slice_in_dim(out, values.reshape(before, 1, -1), at, 1).reshape(-1)

    bias_sums = token_sum(grad_mixed)
    small_grads = jnp.stack(
        [
            grad_gain_one, grad_gain_two, grad_bias_one, spread(bias_sums[:part], 1), spread(bias_sums[2 * part :], 1),
            token_sum(grad_branch), grad_bias_two, token_sum(flat_grad),
        ],
        axis=1,
    )
    up_sums = spread(token_sum(grad_upward), dps).reshape(width, ups)
    small_grads = jnp.concatenate([small_grads, up_sums], axis=1)
    small_grads = jnp.pad(small_grads, ((0, 0), (0, SMALL - small_grads.shape[1])))
    grad_qkvs = jnp.concatenate([grad_qkv, small_grads.astype(jnp.bfloat16)], axis=1)
    grad_qkvs, piece_out = lax.optimization_barrier((grad_qkvs, piece_out))
    piece_qkvs = scatter(grad_qkvs)

    output = summed(activated, full_down, ((1,), (0,)))
    out_tokens = (residual[:rows] + output + bias_down).astype(jnp.bfloat16)

    total_down = in_order(piece_down, shards, at).astype(jnp.float32).reshape(shards * sub, width)
    total_up = in_order(piece_up.reshape(shard_rows, dps, sub), shards, at).astype(jnp.float32)
    total_up = total_up.transpose(1, 2, 0, 3).reshape(shard_rows, hidden)
    total_out = in_order(piece_out, shards, at).astype(jnp.float32).sum(0)
    every_qkvs = in_order(piece_qkvs, shards, at).astype(jnp.float32)
    total_qkv = every_qkvs[:, :, : 3 * part].reshape(shards, shard_rows, 3, part)
    total_qkv = total_qkv.transpose(1, 2, 0, 3).reshape(shard_rows, 3 * width)
    total_small = every_qkvs[:, :, 3 * part :].sum(0)
    return (
        out_tokens.reshape(tokens.shape),
        grad_tokens.reshape(tokens.shape),
        total_qkv,
        total_out,
        total_up,
        total_down,
        total_small[:, :2],
        total_small[:, 2:8],
        total_small[:, 8 : 8 + ups].reshape(-1),
    )


def solution(mesh):
    paired = mesh.shape["seq"] == 2 and mesh.shape["dp"] == 16
    return jax.shard_map(
        per_device_pair if paired else per_device,
        mesh=mesh,
        in_specs=(
            P("dp", "seq", None),
            P("dp", None),
            P("dp", None),
            P("dp", None),
            P("dp", None),
            P("dp", None),
            P("dp", None),
            P("dp"),
            P("dp"),
            P("dp", "seq", None),
        ),
        out_specs=(
            P("dp", "seq", None),
            P("dp", "seq", None),
            P("dp", None),
            P("dp", None),
            P("dp", None),
            P("dp", None),
            P("dp", None),
            P("dp", None),
            P("dp"),
        ),
        check_vma=False,
    )
```

```python
import functools

import jax
import jax.numpy as jnp
from jax import lax
from jax.experimental import pallas as pl
from jax.experimental.pallas import tpu as pltpu
from jax.sharding import PartitionSpec as P

HD = 64
PAIR = 2 * HD
EPSILON = 1e-06
NEG_FILL = -1e30
SMALL = 128
GROUPS = 2


def dot_f32(a, b, dims):
    return lax.dot_general(a, b, (dims, ((), ())), preferred_element_type=jnp.float32)


def mat(a, b):
    return dot_f32(a, b, ((1,), (0,)))


def norm_parts(values):
    average = jnp.mean(values, axis=-1, keepdims=True)
    centered = values - average
    variance = jnp.mean(centered * centered, axis=-1, keepdims=True)
    inverse = lax.rsqrt(variance + EPSILON)
    return centered * inverse, inverse


def norm_back(hat, inverse, scales, grad):
    scaled = grad * scales
    first = jnp.mean(scaled, axis=-1, keepdims=True)
    second = jnp.mean(scaled * hat, axis=-1, keepdims=True)
    return inverse * (scaled - first - hat * second)


def lanes(head):
    lane = lax.broadcasted_iota(jnp.int32, (1, PAIR), 1)
    own = (lane < HD) if head == 0 else (lane >= HD)
    return own, lane - (HD if head == 0 else 0)


def key_bias(place_ref, valid_ref, length, shards):
    row = lax.broadcasted_iota(jnp.int32, (shards * length, 1), 0)
    position = row + place_ref[0] * length
    position = jnp.where(position >= shards * length, position - shards * length, position)
    allowed = position < valid_ref[pl.program_id(0)]
    return jnp.where(allowed, 0.0, NEG_FILL).astype(jnp.float32)


def augmented(values, head, extra):
    own, free = lanes(head)
    out = jnp.where(own, values, 0.0)
    for at, column in enumerate(extra):
        out = jnp.where(free == at, column, out)
    return out.astype(jnp.bfloat16)


def rows_with(values_t, head, extra):
    row = lax.broadcasted_iota(jnp.int32, (PAIR, 1), 0)
    own = (row < HD) if head == 0 else (row >= HD)
    free = row - (HD if head == 0 else 0)
    out = jnp.where(own, values_t, 0.0)
    for at, line in enumerate(extra):
        out = jnp.where(free == at, line, out)
    return out.astype(jnp.bfloat16)


def split_three(line):
    high = line.astype(jnp.bfloat16).astype(jnp.float32)
    rest = line - high
    middle = rest.astype(jnp.bfloat16).astype(jnp.float32)
    return high, middle, rest - middle


def forward_kernel(place_ref, valid_ref, q_ref, k_ref, v_ref, out_ref, lse_ref):
    shards, length, _ = q_ref.shape
    bias = key_bias(place_ref, valid_ref, length, shards)
    keys = k_ref[...].reshape(shards * length, PAIR).astype(jnp.float32)
    values = v_ref[...].reshape(shards * length, PAIR).astype(jnp.float32)
    keys_of = [augmented(keys, head, [bias]) for head in range(2)]
    values_of = [augmented(values, head, [1.0]).T for head in range(2)]
    for shard in range(shards):
        queries = q_ref[shard].astype(jnp.float32).T * HD**-0.5
        halves = []
        for head in range(2):
            scores = mat(keys_of[head], rows_with(queries, head, [1.0]))
            top = jnp.max(scores, axis=0, keepdims=True)
            weight = jnp.exp(scores - top).astype(jnp.bfloat16)
            part = mat(values_of[head], weight)
            at = HD * (1 - head)
            row_total = part[at : at + 1, :]
            halves.append(part[HD * head : HD * (head + 1), :] / row_total)
            lse_ref[0, 0, shard, head : head + 1, :] = top + jnp.log(row_total)
        out_ref[shard] = jnp.concatenate(halves, axis=0).T.astype(out_ref.dtype)


def backward_kernel(place_ref, valid_ref, q_ref, k_ref, v_ref, out_ref, lse_ref, da_ref, dq_ref, dk_ref, dv_ref):
    shards, length, _ = q_ref.shape
    bias = key_bias(place_ref, valid_ref, length, shards)
    keys = k_ref[...].reshape(shards * length, PAIR).astype(jnp.float32)
    values = v_ref[...].reshape(shards * length, PAIR).astype(jnp.float32)
    keys_of = [augmented(keys, head, [bias, 1.0, 1.0, 1.0]) for head in range(2)]
    values_of = [augmented(values, head, [1.0, 1.0, 1.0]) for head in range(2)]
    plain_keys = [augmented(keys, head, []).T for head in range(2)]
    dk = dv = None
    for shard in range(shards):
        queries = q_ref[shard].astype(jnp.float32) * HD**-0.5
        grads = da_ref[shard].astype(jnp.float32)
        queries_t, grads_t = queries.T, grads.T
        product = grads_t * out_ref[shard].astype(jnp.float32).T
        dq = None
        for head in range(2):
            lse = lse_ref[0, 0, shard, head : head + 1, :]
            delta = jnp.sum(product[HD * head : HD * (head + 1), :], axis=0, keepdims=True)
            scores = mat(keys_of[head], rows_with(queries_t, head, (1.0,) + split_three(-lse)))
            probs = jnp.exp(scores)
            moved = mat(values_of[head], rows_with(grads_t, head, split_three(-delta)))
            dscores = (probs * moved).astype(jnp.bfloat16)
            part_v = mat(probs.astype(jnp.bfloat16), augmented(grads, head, []))
            part_k = mat(dscores, augmented(queries, head, []))
            part_q = mat(plain_keys[head], dscores)
            dq = part_q if dq is None else dq + part_q
            dk = part_k if dk is None else dk + part_k
            dv = part_v if dv is None else dv + part_v
        dq_ref[shard] = (dq * HD**-0.5).T.astype(dq_ref.dtype)
    dk_ref[...] = dk.astype(dk_ref.dtype).reshape(dk_ref.shape)
    dv_ref[...] = dv.astype(dv_ref.dtype).reshape(dv_ref.shape)


def attention_specs(shards, length, pairs_all, first_pair):
    smem = pl.BlockSpec(memory_space=pltpu.SMEM)
    mixed = [
        pl.BlockSpec((shards, length, PAIR), lambda i, h, t=t: (0, i, t * pairs_all + first_pair + h))
        for t in range(3)
    ]
    plain = pl.BlockSpec((shards, length, PAIR), lambda i, h: (0, i, h))
    lse = pl.BlockSpec((1, 1, shards, 2, length), lambda i, h: (i, h, 0, 0, 0))
    return smem, mixed, plain, lse


def attend_forward(images, place, valid, mixed, first_pair, pairs):
    shards, rows, width3 = mixed.shape
    length = rows // images
    smem, block3, plain, lse = attention_specs(shards, length, width3 // 3 // PAIR, first_pair)
    work = shards * shards * rows * length * pairs
    return pl.pallas_call(
        forward_kernel,
        grid=(images, pairs),
        in_specs=[smem, smem] + block3,
        out_specs=[plain, lse],
        out_shape=[
            jax.ShapeDtypeStruct((shards, rows, pairs * PAIR), jnp.bfloat16),
            jax.ShapeDtypeStruct((images, pairs, shards, 2, length), jnp.float32),
        ],
        compiler_params=pltpu.CompilerParams(vmem_limit_bytes=40 * 2**20),
        cost_estimate=pl.CostEstimate(
            flops=8 * work * PAIR, bytes_accessed=8 * shards * rows * pairs * PAIR, transcendentals=2 * work,
        ),
    )(place, valid, mixed, mixed, mixed)


def attend_backward(images, place, valid, mixed, first_pair, pairs, attended, lse_in, da):
    shards, rows, width3 = mixed.shape
    length = rows // images
    smem, block3, plain, lse = attention_specs(shards, length, width3 // 3 // PAIR, first_pair)
    low = jax.ShapeDtypeStruct((shards, rows, pairs * PAIR), jnp.bfloat16)
    work = shards * shards * rows * length * pairs
    return pl.pallas_call(
        backward_kernel,
        grid=(images, pairs),
        in_specs=[smem, smem] + block3 + [plain, lse, plain],
        out_specs=[plain] * 3,
        out_shape=[low] * 3,
        compiler_params=pltpu.CompilerParams(vmem_limit_bytes=48 * 2**20),
        cost_estimate=pl.CostEstimate(
            flops=20 * work * PAIR, bytes_accessed=16 * shards * rows * pairs * PAIR, transcendentals=2 * work,
        ),
    )(place, valid, mixed, mixed, mixed, attended, lse_in, da)


def shift(values, shards, step):
    return lax.ppermute(values, "seq", [(i, (i + step) % shards) for i in range(shards)])


def everyone(values, shards, step_axis=0):
    return jnp.stack([values] + [shift(values, shards, -j) for j in range(1, shards)], axis=step_axis)


def in_order(values, shards, place):
    if shards == 2:
        other = shift(values, shards, 1)
        low = jnp.where(place == 0, values, other)
        high = jnp.where(place == 0, other, values)
        return jnp.stack([low, high])
    return lax.all_gather(values, "seq", axis=0)


def token_sum(values):
    return jnp.sum(values.astype(jnp.float32), axis=0)


MESH = pl.DeviceIdType.MESH


class Peers:
    def __init__(self, dps):
        self.dp = lax.axis_index("dp")
        self.seq = lax.axis_index("seq")
        self.levels = dps // 4
        self.z = self.dp // 4
        self.x = self.dp % 4 // 2
        self.core = self.dp % 2

    def up(self, step):
        return ((self.z + step) % self.levels * 4 + self.dp % 4, self.seq)

    def across(self):
        return (self.dp + 2 - 4 * self.x, self.seq)

    def sibling(self):
        return (self.dp + 1 - 2 * self.core, self.seq)

    def other(self):
        return (self.dp, 1 - self.seq)

    def all(self):
        return [self.up(s) for s in range(1, self.levels)] + [self.across(), self.sibling(), self.other()]

    def greet(self):
        barrier = pltpu.get_barrier_semaphore()
        for device in self.all():
            pl.semaphore_signal(barrier, inc=1, device_id=device, device_id_type=MESH)
        pl.semaphore_wait(barrier, len(self.all()))


def remote(src, dst, send, recv, device):
    return pltpu.make_async_remote_copy(
        src_ref=src, dst_ref=dst, send_sem=send, recv_sem=recv, device_id=device, device_id_type=MESH
    )


class Gather:
    def __init__(self, peers, src, full, sems, cut=(slice(None), slice(None))):
        levels = peers.levels
        at = (peers.z, peers.x, peers.core) + cut
        self.local = pltpu.make_async_copy(src, full.at[at], sems.at[0])
        self.first = [
            remote(src, full.at[at], sems.at[2 * s + 3], sems.at[2 * s + 4], peers.up(s)) for s in range(1, levels)
        ]
        column = full.at[(slice(None), peers.x, peers.core) + cut]
        self.second = remote(column, column, sems.at[1], sems.at[2], peers.across())
        half = full.at[(slice(None), slice(None), peers.core) + cut]
        self.third = remote(half, half, sems.at[3], sems.at[4], peers.sibling())

    def start(self):
        self.local.start()
        for copy in self.first:
            copy.start()

    def cross(self):
        self.local.wait()
        for copy in self.first:
            copy.wait_recv()
        self.second.start()

    def share(self):
        self.second.wait_recv()
        self.third.start()

    def arrive(self):
        self.third.wait_recv()

    def finish(self):
        for copy in self.first + [self.second, self.third]:
            copy.wait_send()


def gather_sems(levels):
    return 2 * levels + 3


def query_tiles(total):
    first = max(total // 512, 1) * 256
    return [(0, first), (first, total)]


def attend_pair(valid_ref, mixed, att, lse_ref, pair, base):
    shards, length, width3 = mixed.shape
    part = width3 // 3

    def columns(t):
        return pl.ds(pl.multiple_of(t * part + pair * PAIR, PAIR), PAIR)

    row = lax.broadcasted_iota(jnp.int32, (shards * length, 1), 0)
    bias = jnp.where(row < valid_ref[0], 0.0, NEG_FILL).astype(jnp.float32)
    keys = mixed[:, :, columns(1)].reshape(shards * length, PAIR).astype(jnp.float32)
    values = mixed[:, :, columns(2)].reshape(shards * length, PAIR).astype(jnp.float32)
    keys_of = [augmented(keys, head, [bias]) for head in range(2)]
    values_of = [augmented(values, head, [1.0]).T for head in range(2)]
    out_columns = pl.ds(pl.multiple_of(base + pair * PAIR, PAIR), PAIR)
    queries_all = mixed[:, :, columns(0)].reshape(shards * length, PAIR)
    outs = []
    for start, stop in query_tiles(shards * length):
        queries = queries_all[start:stop].astype(jnp.float32).T * HD**-0.5
        halves = []
        for head in range(2):
            scores = mat(keys_of[head], rows_with(queries, head, [1.0]))
            top = jnp.max(scores, axis=0, keepdims=True)
            weight = jnp.exp(scores - top).astype(jnp.bfloat16)
            product = mat(values_of[head], weight)
            at = HD * (1 - head)
            row_total = product[at : at + 1, :]
            halves.append(product[HD * head : HD * (head + 1), :] / row_total)
            lse_ref[pair, head : head + 1, start:stop] = top + jnp.log(row_total)
        outs.append(jnp.concatenate(halves, axis=0).T.astype(att.dtype))
    att[:, :, out_columns] = jnp.concatenate(outs, axis=0).reshape(shards, length, PAIR)


def place_blocks(grad, z, value):
    rows = grad.shape[3]
    for x in range(2):
        for core in range(2):
            at = (2 * x + core) * rows
            grad[core, z, x] = value[at : at + rows, :].astype(grad.dtype)


ROW_TILE = 144
COL_TILE = 512


def forward_layer(
    valid_ref, tokens, cotangent, w_qkv, w_out, w_up, w_down, small,
    tok_out, dy_out, first_out, mixed_out, att_out, lse_ref, resid_out, second_out, act_out, slope_out,
    q_out, k_out, v_out, o_out, up_out, down_out, half_out, rows_ref, bup_ref,
    tok, first, mixed, att, resid, second, act, slope, fsmall, fq, fk, fv, fo, fup, fdown, my_up, dy, grad, cored, gsems, sems,
):
    levels = fq.shape[0]
    peers = Peers(4 * levels)
    p = peers.seq
    length, width = tokens.shape
    part = width // 2
    sub = fdown.shape[3]
    shard_rows = w_out.shape[0]
    peers.greet()

    send_tok = remote(tokens, tok.at[p], sems.at[0], sems.at[1], peers.other())
    send_tok.start()
    own = lambda t: w_qkv.at[:, pl.ds(pl.multiple_of(t * width + p * part, PAIR), part)]
    own_hidden = act.shape[2]
    half = own_hidden // 2
    low_up, high_up = (slice(None), pl.ds(0, half)), (slice(None), pl.ds(half, half))
    down_cuts = [(0, sub // 2), (sub // 2, sub // 4), (3 * sub // 4, sub // 4)]
    g_small = Gather(peers, small, fsmall, gsems.at[0])
    g_q = Gather(peers, own(0), fq, gsems.at[1])
    g_k = Gather(peers, own(1), fk, gsems.at[2])
    g_v = Gather(peers, own(2), fv, gsems.at[3])
    g_out = Gather(peers, w_out, fo, gsems.at[4])
    g_up = Gather(peers, my_up.at[:, 0:half], fup, gsems.at[5], low_up)
    g_up2 = Gather(peers, my_up.at[:, half : 2 * half], fup, gsems.at[6], high_up)
    g_down, g_down2, g_down3 = (
        Gather(
            peers, w_down.at[pl.ds(pl.multiple_of(p * sub + start, 16), size)], fdown, gsems.at[7 + i],
            (pl.ds(start, size), slice(None)),
        )
        for i, (start, size) in enumerate(down_cuts)
    )
    gathers = [g_small, g_q, g_k, g_v, g_out, g_up, g_up2, g_down, g_down2, g_down3]
    for g in (g_small, g_q, g_k, g_v):
        g.start()
    for d in range(4 * levels):
        my_up[:, d * sub : (d + 1) * sub] = w_up[:, pl.ds(pl.multiple_of((2 * d + p) * sub, PAIR), sub)]

    own_tok = pltpu.make_async_copy(tokens, tok.at[p], sems.at[2])
    own_tok.start()
    own_dy = pltpu.make_async_copy(cotangent, dy.at[p], sems.at[3])
    own_dy.start()

    def normed(shard):
        @pl.loop(0, length // ROW_TILE)
        def _(i):
            at = pl.ds(pl.multiple_of(i * ROW_TILE, 16), ROW_TILE)
            resid[shard, at, :] = norm_parts(tok[shard, at, :].astype(jnp.float32))[0]

    g_small.cross()
    g_q.cross()
    own_tok.wait()
    normed(p)
    g_k.cross()
    g_v.cross()
    g_out.start()
    g_small.share()
    g_q.share()
    g_k.share()
    middle = length // 2
    send_dy = [
        remote(
            cotangent.at[pl.ds(i * middle, middle)], dy.at[p, pl.ds(i * middle, middle)],
            sems.at[(4, 14)[i]], sems.at[(5, 15)[i]], peers.other(),
        )
        for i in range(2)
    ]
    send_tok.wait_recv()
    send_dy[0].start()
    normed(1 - p)
    g_small.arrive()
    vectors = fsmall[:, :, :, 0:shard_rows, :].reshape(width, SMALL).astype(jnp.float32).T
    rows_ref[...] = vectors[0:16, :]
    for d in range(4 * levels):
        at = (d // 4, d % 4 // 2, d % 2)
        pair_rows = fsmall[at + (slice(shard_rows, shard_rows + 16),)].astype(jnp.float32)
        bup_ref[0:1, d * sub : (d + 1) * sub] = jnp.where(p == 0, pair_rows[0:1, :sub], pair_rows[1:2, :sub])

    for shard in range(2):
        @pl.loop(0, length // ROW_TILE)
        def _(i):
            at = pl.ds(pl.multiple_of(i * ROW_TILE, 16), ROW_TILE)
            first[shard, at, :] = (resid[shard, at, :] * rows_ref[0:1, :] + rows_ref[2:3, :]).astype(jnp.bfloat16)

    own_columns = pl.ds(pl.multiple_of(p * part, PAIR), part)

    def project(t, full, bias):
        weight = full[...].reshape(width, part)
        @pl.loop(0, 2)
        def _(shard):
            out = mat(first[shard], weight)
            if bias is not None:
                out = out + rows_ref[bias : bias + 1, own_columns]
            mixed[shard, :, t * part : (t + 1) * part] = out.astype(jnp.bfloat16)

    saves = []
    pairs = part // PAIR

    def save(src, dst):
        copy = pltpu.make_async_copy(src, dst, sems.at[32 + 2 * pairs + len(saves)])
        saves.append(copy)
        copy.start()

    save(tok, tok_out)
    save(first, first_out)
    g_v.share()
    g_q.arrive()
    project(0, fq, 3)
    g_up.start()
    g_k.arrive()
    project(1, fk, None)
    g_out.cross()
    g_up2.start()
    g_v.arrive()
    project(2, fv, 4)
    save(mixed, mixed_out)
    save(fq, q_out)
    save(fk, k_out)
    save(fv, v_out)

    pairs = part // PAIR
    att_copies = []
    for pair in range(pairs):
        columns = pl.ds(pl.multiple_of(p * part + pair * PAIR, PAIR), PAIR)
        att_copies.append(
            remote(
                att.at[:, :, columns], att.at[:, :, columns], sems.at[32 + 2 * pair], sems.at[33 + 2 * pair],
                peers.other(),
            )
        )

    @pl.loop(0, pairs)
    def _(pair):
        attend_pair(valid_ref, mixed, att, lse_ref, pair, p * part)
        for i in range(pairs):
            @pl.when(pair == i)
            def _():
                att_copies[i].start()
                if i == min(1, pairs - 1):
                    g_up.cross()
                    g_down.start()
                    g_out.share()
                if i == pairs - 1:
                    g_up2.cross()
                    g_down2.start()
                    g_up.share()

    g_out.arrive()
    save(fo, o_out)
    for copy in att_copies:
        copy.wait_recv()
    save(att, att_out)
    send_dy[1].start()
    out_weight = fo[...].reshape(width, width)

    def finish_rows(shard):
        @pl.loop(0, length // ROW_TILE)
        def _(i):
            at = pl.ds(pl.multiple_of(i * ROW_TILE, 16), ROW_TILE)
            value = mat(att[shard, at, :], out_weight) + rows_ref[5:6, :] + tok[shard, at, :].astype(jnp.float32)
            resid[shard, at, :] = value
            hat, _ = norm_parts(value)
            second[shard, at, :] = (hat * rows_ref[1:2, :] + rows_ref[6:7, :]).astype(jnp.bfloat16)

    finish_rows(0)
    finish_rows(1)
    save(resid.at[p], resid_out)
    save(second, second_out)

    def into_hidden(first_tile, tiles):
        @pl.loop(0, 2 * tiles)
        def _(step):
            shard = step // tiles
            at = pl.ds(pl.multiple_of((first_tile + step % tiles) * COL_TILE, PAIR), COL_TILE)
            upward = mat(second[shard], fup[:, :, :, :, at].reshape(width, COL_TILE)) + bup_ref[0:1, at]
            cdf = 0.5 * (1.0 + lax.erf(upward * 0.5**0.5))
            act[shard, :, at] = (upward * cdf).astype(jnp.bfloat16)
            value = cdf + upward * (jnp.exp(-0.5 * upward * upward) * 0.3989422804014327)
            slope[shard, :, at] = value.astype(jnp.bfloat16)

    tiles = half // COL_TILE
    g_up.arrive()
    into_hidden(0, tiles)
    g_down.cross()
    g_down3.start()
    g_up2.share()
    g_up2.arrive()
    save(fup, up_out)
    into_hidden(tiles, tiles)
    save(act, act_out)
    save(slope, slope_out)
    g_down2.cross()
    g_down.share()
    g_down3.cross()
    own_dy.wait()
    for copy in send_dy:
        copy.wait_recv()
    save(dy, dy_out)

    @pl.loop(0, levels)
    def _(z):
        at = pl.ds(pl.multiple_of(z * 4 * sub, PAIR), 4 * sub)
        value = dot_f32(act[:, :, at].reshape(2 * length, 4 * sub), dy[...].reshape(2 * length, width), ((0,), (0,)))
        place_blocks(grad, z, value)

    send_grad = remote(grad.at[1 - peers.core], cored, sems.at[6], sems.at[7], peers.sibling())
    send_grad.start()
    g_down.arrive()
    low, high = pl.ds(0, sub // 2), pl.ds(sub // 2, sub // 2)
    save(fdown.at[:, :, :, low], down_out.at[:, :, :, low])
    g_down2.share()
    send_grad.wait_recv()

    @pl.loop(0, levels)
    def _(z):
        for x in range(2):
            total = grad[peers.core, z, x].astype(jnp.float32) + cored[z, x].astype(jnp.float32)
            grad[peers.core, z, x] = total.astype(jnp.bfloat16)

    save(grad.at[peers.core], half_out)
    g_down3.share()
    g_down2.arrive()
    g_down3.arrive()
    save(fdown.at[:, :, :, high], down_out.at[:, :, :, high])
    send_grad.wait_send()
    send_tok.wait_send()
    for copy in send_dy:
        copy.wait_send()
    for copy in att_copies:
        copy.wait_send()
    for g in gathers:
        g.finish()
    for copy in saves:
        copy.wait()


def run_forward(dps, tokens, cotangent, w_qkv, w_out, w_up, w_down, small, valid):
    length, width = tokens.shape
    levels = dps // 4
    part = width // 2
    shard_rows = w_out.shape[0]
    own_hidden = w_up.shape[1] // 2
    sub = w_down.shape[0] // 2
    pairs = part // PAIR
    bf, f32 = jnp.bfloat16, jnp.float32
    any_spec = pl.BlockSpec(memory_space=pl.ANY)
    vmem = pl.BlockSpec(memory_space=pltpu.VMEM)
    smem = pl.BlockSpec(memory_space=pltpu.SMEM)
    grid = (levels, 2, 2)
    whole = [
        ((2, length, width), bf),
        ((2, length, width), bf),
        ((2, length, width), bf),
        ((2, length, 3 * part), bf),
        ((2, length, width), bf),
        ((pairs, 2, 2 * length), f32),
        ((length, width), f32),
        ((2, length, width), bf),
        ((2, length, own_hidden), bf),
        ((2, length, own_hidden), bf),
        (grid + (shard_rows, part), bf),
        (grid + (shard_rows, part), bf),
        (grid + (shard_rows, part), bf),
        (grid + (shard_rows, width), bf),
        (grid + (shard_rows, own_hidden), bf),
        (grid + (sub, width), bf),
        ((levels, 2, sub, width), bf),
        ((16, width), f32),
        ((8, own_hidden), f32),
    ]
    in_vmem = (5, 17, 18)
    scratch = [
        pltpu.VMEM((2, length, width), bf),
        pltpu.VMEM((2, length, width), bf),
        pltpu.VMEM((2, length, 3 * part), bf),
        pltpu.VMEM((2, length, width), bf),
        pltpu.VMEM((2, length, width), f32),
        pltpu.VMEM((2, length, width), bf),
        pltpu.VMEM((2, length, own_hidden), bf),
        pltpu.VMEM((2, length, own_hidden), bf),
        pltpu.VMEM(grid + (shard_rows + 16, SMALL), bf),
        pltpu.VMEM(grid + (shard_rows, part), bf),
        pltpu.VMEM(grid + (shard_rows, part), bf),
        pltpu.VMEM(grid + (shard_rows, part), bf),
        pltpu.VMEM(grid + (shard_rows, width), bf),
        pltpu.VMEM(grid + (shard_rows, own_hidden), bf),
        pltpu.VMEM(grid + (sub, width), bf),
        pltpu.VMEM((shard_rows, own_hidden), bf),
        pltpu.VMEM((2, length, width), bf),
        pltpu.VMEM((2, levels, 2, sub, width), bf),
        pltpu.VMEM((levels, 2, sub, width), bf),
        pltpu.SemaphoreType.DMA((10, gather_sems(levels))),
        pltpu.SemaphoreType.DMA((52 + 2 * pairs,)),
    ]
    return pl.pallas_call(
        forward_layer,
        in_specs=[smem, any_spec, any_spec, vmem, vmem, vmem, vmem, vmem],
        out_specs=[vmem if i in in_vmem else any_spec for i in range(len(whole))],
        out_shape=[jax.ShapeDtypeStruct(*s) for s in whole],
        scratch_shapes=scratch,
        compiler_params=pltpu.CompilerParams(
            vmem_limit_bytes=62 * 2**20, collective_id=0, has_side_effects=True
        ),
        cost_estimate=pl.CostEstimate(flops=3 * 10**10, bytes_accessed=8 * 10**7, transcendentals=2 * 10**7),
    )(valid, tokens, cotangent, w_qkv, w_out, w_up, w_down, small)


class Scatter:
    def __init__(self, peers, grad, cored, crossed, risen, own, theirs, sems):
        core, x, z = peers.core, peers.x, peers.z
        self.peers, self.grad, self.cored, self.crossed, self.risen = peers, grad, cored, crossed, risen
        self.own = own
        self.first = remote(grad.at[1 - core], cored, sems.at[0], sems.at[1], peers.sibling())
        self.second = remote(grad.at[core, :, 1 - x], crossed, sems.at[2], sems.at[3], peers.across())
        self.third = [
            remote(
                grad.at[core, (z + s) % peers.levels, x], risen.at[s - 1], sems.at[2 * s + 4], sems.at[2 * s + 5],
                peers.up(s),
            )
            for s in range(1, peers.levels)
        ]
        self.fourth = remote(own, theirs, sems.at[4], sems.at[5], peers.other())

    def start(self):
        self.first.start()

    def cross(self):
        core = self.peers.core
        self.first.wait_recv()

        @pl.loop(0, self.peers.levels)
        def _(z):
            for x in range(2):
                total = self.grad[core, z, x].astype(jnp.float32) + self.cored[z, x].astype(jnp.float32)
                self.grad[core, z, x] = total.astype(self.grad.dtype)

        self.second.start()

    def rise(self):
        core, x = self.peers.core, self.peers.x
        self.second.wait_recv()

        @pl.loop(0, self.peers.levels)
        def _(z):
            total = self.grad[core, z, x].astype(jnp.float32) + self.crossed[z].astype(jnp.float32)
            self.grad[core, z, x] = total.astype(self.grad.dtype)

        for copy in self.third:
            copy.start()

    def own_piece(self):
        return self.grad[self.peers.core, self.peers.z, self.peers.x]

    def over(self):
        for copy in self.third:
            copy.wait_recv()
        total = self.own_piece().astype(jnp.float32)
        for s in range(self.peers.levels - 1):
            total = total + self.risen[s].astype(jnp.float32)
        self.own[...] = total.astype(self.own.dtype)
        self.fourth.start()

    def arrive(self):
        self.fourth.wait_recv()

    def finish(self):
        for copy in [self.first, self.second, self.fourth] + self.third:
            copy.wait_send()


class LateScatter(Scatter):
    def __init__(self, peers, halves, kept, crossed, risen, own, theirs, sems):
        x, z = peers.x, peers.z
        self.peers, self.kept, self.crossed, self.risen, self.own = peers, kept, crossed, risen, own
        self.second = remote(halves.at[:, 1 - x], crossed, sems.at[2], sems.at[3], peers.across())
        self.local = pltpu.make_async_copy(halves.at[:, x], kept, sems.at[0])
        self.third = [
            remote(
                kept.at[(z + s) % peers.levels], risen.at[s - 1], sems.at[2 * s + 4], sems.at[2 * s + 5], peers.up(s)
            )
            for s in range(1, peers.levels)
        ]
        self.fourth = remote(own, theirs, sems.at[4], sems.at[5], peers.other())

    def start(self):
        self.second.start()
        self.local.start()

    def rise(self):
        self.local.wait()
        self.second.wait_recv()

        @pl.loop(0, self.peers.levels)
        def _(z):
            total = self.kept[z].astype(jnp.float32) + self.crossed[z].astype(jnp.float32)
            self.kept[z] = total.astype(self.kept.dtype)

        for copy in self.third:
            copy.start()

    def own_piece(self):
        return self.kept[self.peers.z]

    def finish(self):
        for copy in [self.second, self.fourth] + self.third:
            copy.wait_send()


def scatter_sems(levels):
    return 2 * levels + 4


def scatter_buffers(levels, rows, columns, dtype):
    return [
        pltpu.VMEM((2, levels, 2, rows, columns), dtype),
        pltpu.VMEM((levels, 2, rows, columns), dtype),
        pltpu.VMEM((levels, rows, columns), dtype),
        pltpu.VMEM((levels - 1, rows, columns), dtype),
    ]


def attend_pair_back(valid_ref, mixed, att, lse_ref, datt, dmix, sums, pair, base, place):
    shards, length, width3 = mixed.shape
    part = width3 // 3
    group, within = pair // 2, pair % 2
    wide = dmix.shape[3] // 3

    def columns(t):
        return pl.ds(pl.multiple_of(t * part + pair * PAIR, PAIR), PAIR)

    def out_columns(t):
        return pl.ds(pl.multiple_of(t * wide + within * PAIR, PAIR), PAIR)

    own_columns = pl.ds(pl.multiple_of(base + pair * PAIR, PAIR), PAIR)
    da_columns = pl.ds(pl.multiple_of(pair * PAIR, PAIR), PAIR)
    row = lax.broadcasted_iota(jnp.int32, (shards * length, 1), 0)
    bias = jnp.where(row < valid_ref[0], 0.0, NEG_FILL).astype(jnp.float32)
    keys = mixed[:, :, columns(1)].reshape(shards * length, PAIR).astype(jnp.float32)
    values = mixed[:, :, columns(2)].reshape(shards * length, PAIR).astype(jnp.float32)
    keys_of = [augmented(keys, head, [bias, 1.0, 1.0, 1.0]) for head in range(2)]
    values_of = [augmented(values, head, [1.0, 1.0, 1.0]) for head in range(2)]
    plain_keys = [augmented(keys, head, []).T for head in range(2)]
    dk = dv = None
    queries_all = mixed[:, :, columns(0)].reshape(shards * length, PAIR)
    grads_all = datt[:, :, da_columns].reshape(shards * length, PAIR)
    att_all = att[:, :, da_columns].reshape(shards * length, PAIR)
    dqs = []
    for start, stop in query_tiles(shards * length):
        queries = queries_all[start:stop].astype(jnp.float32) * HD**-0.5
        grads = grads_all[start:stop].astype(jnp.float32)
        queries_t, grads_t = queries.T, grads.T
        product = grads_t * att_all[start:stop].astype(jnp.float32).T
        dq = None
        for head in range(2):
            lse = lse_ref[pair, head : head + 1, start:stop]
            delta = jnp.sum(product[HD * head : HD * (head + 1), :], axis=0, keepdims=True)
            scores = mat(keys_of[head], rows_with(queries_t, head, (1.0,) + split_three(-lse)))
            probs = jnp.exp(scores)
            moved = mat(values_of[head], rows_with(grads_t, head, split_three(-delta)))
            dscores = (probs * moved).astype(jnp.bfloat16)
            part_v = mat(probs.astype(jnp.bfloat16), augmented(grads, head, []))
            part_k = mat(dscores, augmented(queries, head, []))
            part_q = mat(plain_keys[head], dscores)
            dq = part_q if dq is None else dq + part_q
            dk = part_k if dk is None else dk + part_k
            dv = part_v if dv is None else dv + part_v
        dqs.append((dq * HD**-0.5).T.astype(jnp.bfloat16))
    dq = jnp.concatenate(dqs, axis=0)
    dmix[group, :, :, out_columns(0)] = dq.reshape(shards, length, PAIR)
    dq_sum = jnp.sum(dq.astype(jnp.float32), axis=0, keepdims=True)
    dk, dv = dk.astype(jnp.bfloat16), dv.astype(jnp.bfloat16)
    dmix[group, :, :, out_columns(1)] = dk.reshape(shards, length, PAIR)
    dmix[group, :, :, out_columns(2)] = dv.reshape(shards, length, PAIR)
    sums[3:4, own_columns] = dq_sum
    sums[4:5, own_columns] = jnp.sum(dv.astype(jnp.float32), axis=0, keepdims=True)


def column_sum(values):
    return jnp.sum(values, axis=0, keepdims=True)


def backward_layer(
    valid_ref, rows_ref, lse_ref,
    tok_in, dy_in, first_in, mixed_in, att_in, resid_in, second_in, act_in, slope_in,
    q_in, k_in, v_in, o_in, up_in, down_in, half_in,
    otok_ref, orecv_ref, gtok_ref, gqkv_ref, gout_ref, gup_ref, gdown_ref, gsmall_ref,
    down1, down2, down3, up0, up1, up2, up3, out0, out1, out2, out3, qa0, qa1, qa2, qa3, qb0, qb1, qb2, qb3,
    sm0, sm1, sm2, sm3, down_sum, up_sum, qkv_sum, out_own, out_theirs, sm_own, sm_theirs,
    ysend, yrecv, osend, dres, datt, datt_send, sums, dub, ssems, sems,
):
    levels = down2.shape[0]
    peers = Peers(4 * levels)
    p, q = peers.seq, 1 - peers.seq
    _, length, width = dy_in.shape
    part = width // 2
    own_hidden = act_in.shape[2]
    sub = own_hidden // (4 * levels)
    shard_rows = width // (4 * levels)
    wide = part // 2
    bf, f32 = jnp.bfloat16, jnp.float32
    tiles = length // ROW_TILE
    peers.greet()

    s_down = LateScatter(peers, half_in, down1, down2, down3, down_sum.at[p], down_sum.at[p], ssems.at[0])
    s_up = Scatter(peers, up0, up1, up2, up3, up_sum.at[p], up_sum.at[p], ssems.at[1])
    s_out = Scatter(peers, out0, out1, out2, out3, out_own, out_theirs, ssems.at[2])
    s_qa = Scatter(peers, qa0, qa1, qa2, qa3, qkv_sum.at[p, 0], qkv_sum.at[p, 0], ssems.at[3])
    s_qb = Scatter(peers, qb0, qb1, qb2, qb3, qkv_sum.at[p, 1], qkv_sum.at[p, 1], ssems.at[4])
    s_small = Scatter(peers, sm0, sm1, sm2, sm3, sm_own, sm_theirs, ssems.at[5])
    middle = length // 2

    def halves(at):
        rows = [slice(0, middle), slice(middle, length)]
        return [
            remote(ysend.at[r], yrecv.at[r], sems.at[at + 2 * i], sems.at[at + 1 + 2 * i], peers.other())
            for i, r in enumerate(rows)
        ]

    send_two, send_one = halves(8), halves(12)
    send_datt = [
        remote(
            datt_send.at[:, g * wide : (g + 1) * wide], datt.at[p, :, g * wide : (g + 1) * wide],
            sems.at[2 * g], sems.at[1 + 2 * g], peers.other(),
        )
        for g in range(2)
    ]
    send_out = remote(osend, orecv_ref, sems.at[4], sems.at[5], peers.other())
    s_down.start()
    sums[...] = jnp.zeros_like(sums)

    def row_at(i):
        return pl.ds(pl.multiple_of(i * ROW_TILE, 16), ROW_TILE)

    def load(src, dst, at):
        copy = pltpu.make_async_copy(src, dst, sems.at[at])
        copy.start()
        return copy

    def hidden_phase(dy, act, du, fdown, fup, second):
        early = [load(dy_in.at[q], dy.at[q], 16), load(down_in, fdown, 17), load(slope_in.at[q], du.at[q], 18)]
        copies = [
            load(up_in, fup, 19), load(dy_in.at[p], dy.at[p], 20), load(slope_in.at[p], du.at[p], 21),
            load(second_in, second, 22), load(act_in.at[q], act, 23),
        ]
        for copy in early:
            copy.wait()

        def into_hidden(shard):
            @pl.loop(0, levels)
            def _(z):
                at = pl.ds(pl.multiple_of(z * 4 * sub, PAIR), 4 * sub)
                grad = dot_f32(dy[shard], fdown[z].reshape(4 * sub, width), ((1,), (1,)))
                value = (grad * du[shard, :, at].astype(f32)).astype(bf)
                du[shard, :, at] = value
                dub[pl.ds(shard, 1), at] = column_sum(value.astype(f32))

        def back_second(shard, target, rows):
            @pl.loop(0, levels)
            def _(z):
                at = pl.ds(pl.multiple_of(z * 4 * shard_rows, PAIR), 4 * shard_rows)
                value = dot_f32(du[shard, rows, :], fup[z].reshape(4 * shard_rows, own_hidden), ((1,), (1,)))
                target[rows, at] = value.astype(target.dtype)

        into_hidden(q)
        copies[0].wait()
        for i in range(2):
            back_second(q, ysend, slice(i * middle, (i + 1) * middle))
            send_two[i].start()
        copies[1].wait()
        copies[2].wait()
        into_hidden(p)
        copies[3].wait()

        @pl.loop(0, levels)
        def _(z):
            at = pl.ds(pl.multiple_of(z * 4 * shard_rows, PAIR), 4 * shard_rows)
            value = dot_f32(
                second[:, :, at].reshape(2 * length, 4 * shard_rows), du[...].reshape(2 * length, own_hidden), ((0,), (0,))
            )
            place_blocks(up0, z, value)

        s_up.start()
        back_second(p, dres, slice(0, length))
        copies[4].wait()

        @pl.loop(0, width // COL_TILE)
        def _(t):
            at = pl.ds(pl.multiple_of(t * COL_TILE, PAIR), COL_TILE)
            weight = fdown[:, :, :, :, at].reshape(own_hidden, COL_TILE)
            osend[:, at] = mat(act[...], weight).astype(bf)

        s_down.rise()
        s_up.cross()

    pl.run_scoped(
        hidden_phase,
        pltpu.VMEM((2, length, width), bf),
        pltpu.VMEM((length, own_hidden), bf),
        pltpu.VMEM((2, length, own_hidden), bf),
        pltpu.VMEM(down_in.shape, bf),
        pltpu.VMEM(up_in.shape, bf),
        pltpu.VMEM((2, length, width), bf),
    )

    def norm_phase(dy, resid, att, fo, dbr):
        copies = [
            load(dy_in.at[p], dy, 16), load(resid_in, resid, 17), load(o_in, fo, 18), load(att_in.at[p], att, 19),
        ]
        copies[0].wait()
        copies[1].wait()

        def through_norm(i):
            at = row_at(i)
            hat, inverse = norm_parts(resid[at, :])
            grad = dres[at, :] + yrecv[at, :].astype(f32)
            grad_y = dy[at, :].astype(f32)
            value = grad_y + norm_back(hat, inverse, rows_ref[1:2, :], grad)
            dres[at, :] = value
            low = value.astype(bf)
            dbr[at, :] = low
            sums[1:2, :] += column_sum(grad * hat)
            sums[5:6, :] += column_sum(low.astype(f32))
            sums[6:7, :] += column_sum(grad)
            sums[7:8, :] += column_sum(grad_y)

        for i in range(2):
            send_two[i].wait_recv()
            pl.loop(i * (tiles // 2), (i + 1) * (tiles // 2))(through_norm)

        copies[2].wait()
        half = levels // 2
        for g in range(2):
            at = slice(g * wide, (g + 1) * wide)
            blocks = pl.ds(q * half + g * (half // 2), half // 2)
            value = dot_f32(dbr[...], fo[blocks].reshape(wide, width), ((1,), (1,)))
            datt_send[:, at] = value.astype(bf)
            send_datt[g].start()
        datt[p] = dot_f32(dbr[...], fo[pl.ds(p * half, half)].reshape(part, width), ((1,), (1,))).astype(bf)
        copies[3].wait()

        @pl.loop(0, levels)
        def _(z):
            at = pl.ds(pl.multiple_of(z * 4 * shard_rows, PAIR), 4 * shard_rows)
            place_blocks(out0, z, dot_f32(att[:, at], dbr[...], ((0,), (0,))))

        s_out.start()
        send_datt[0].wait_recv()
        send_out.start()
        s_up.rise()

    pl.run_scoped(
        norm_phase,
        pltpu.VMEM((length, width), bf),
        pltpu.VMEM((length, width), f32),
        pltpu.VMEM((length, width), bf),
        pltpu.VMEM(o_in.shape, bf),
        pltpu.VMEM((length, width), bf),
    )

    def heads_phase(dmix, first, fq, fk, fv):
        loaded = [load(first_in, first, 16), load(q_in, fq, 19), load(k_in, fk, 20), load(v_in, fv, 21)]

        def weight_grad(g, grad):
            @pl.loop(0, levels)
            def _(z):
                at = pl.ds(pl.multiple_of(z * 4 * shard_rows, PAIR), 4 * shard_rows)
                value = dot_f32(
                    first[:, :, at].reshape(2 * length, 4 * shard_rows),
                    dmix[g].reshape(2 * length, 3 * wide), ((0,), (0,)),
                )
                place_blocks(grad, z, value)

        own_part = pl.ds(pl.multiple_of(p * part, PAIR), part)

        def attention_phase(mixed, att):
            one, two = load(mixed_in, mixed, 17), load(att_in.at[:, :, own_part], att, 18)
            one.wait()
            two.wait()
            for copy in loaded:
                copy.wait()

            @pl.loop(0, part // PAIR)
            def _(pair):
                attend_pair_back(valid_ref, mixed, att, lse_ref, datt, dmix, sums, pair, p * part, p)

                @pl.when(pair == 0)
                def _():
                    s_out.cross()
                    s_down.over()

                @pl.when(pair == 1)
                def _():
                    weight_grad(0, qa0)
                    s_qa.start()
                    s_out.rise()
                    send_datt[1].wait_recv()

                @pl.when(pair == 2)
                def _():
                    s_qa.cross()
                    s_up.over()

                @pl.when(pair == 3)
                def _():
                    s_qa.rise()
                    s_out.over()

        pl.run_scoped(
            attention_phase,
            pltpu.VMEM(mixed_in.shape, bf),
            pltpu.VMEM((2, length, part), bf),
        )

        def last_phase(tok, part_one, act, fdown, resid, others):
            copies = [
                load(tok_in, tok, 17), load(act_in.at[p], act, 18), load(down_in, fdown, 19), load(resid_in, resid, 20)
            ]
            for copy in send_two:
                copy.wait_send()

            def back_first(shard, target, rows):
                @pl.loop(0, levels)
                def _(z):
                    at = pl.ds(pl.multiple_of(z * 4 * shard_rows, PAIR), 4 * shard_rows)
                    total = None
                    for g in range(2):
                        for t, full in enumerate((fq, fk, fv)):
                            value = dot_f32(
                                dmix[g, shard, rows, t * wide : (t + 1) * wide],
                                full[z, :, :, :, g * wide : (g + 1) * wide].reshape(4 * shard_rows, wide),
                                ((1,), (1,)),
                            )
                            total = value if total is None else total + value
                    target[rows, at] = total.astype(target.dtype)

            def gain_sums(shard, source):
                @pl.loop(0, tiles)
                def _(i):
                    at = row_at(i)
                    hat, _ = norm_parts(tok[shard, at, :].astype(f32))
                    grad = source[at, :].astype(f32)
                    sums[0:1, :] += column_sum(grad * hat)
                    sums[2:3, :] += column_sum(grad)

            for i in range(2):
                back_first(q, part_one, slice(i * middle, (i + 1) * middle))

                @pl.loop(i * (tiles // 2), (i + 1) * (tiles // 2))
                def _(t):
                    ysend[row_at(t), :] = part_one[row_at(t), :].astype(bf)

                send_one[i].start()
            weight_grad(1, qb0)
            s_qb.start()
            copies[0].wait()
            gain_sums(q, part_one)
            back_first(p, part_one, slice(0, length))
            s_qb.cross()
            gain_sums(p, part_one)

            vectors = jnp.concatenate([sums[...], jnp.zeros((SMALL - 16, width), f32)], axis=0).T
            ups = dub[0:1, :] + dub[1:2, :]
            line = lax.broadcasted_iota(jnp.int32, (8, 1), 0)
            for d in range(4 * levels):
                at = (d % 2, d // 4, d % 4 // 2)
                sm0[at + (slice(0, shard_rows),)] = vectors[d * shard_rows : (d + 1) * shard_rows, :]
                sm0[at + (slice(shard_rows, shard_rows + 8),)] = jnp.where(line == p, ups[:, d * sub : (d + 1) * sub], 0.0)
            s_small.start()
            for copy in copies[1:]:
                copy.wait()
            send_out.wait_recv()
            fetched = load(orecv_ref, others, 18)
            s_small.cross()
            s_qb.rise()
            s_small.rise()
            s_qa.over()
            fetched.wait()

            @pl.loop(0, width // COL_TILE)
            def _(t):
                at = pl.ds(pl.multiple_of(t * COL_TILE, PAIR), COL_TILE)
                value = mat(act[...], fdown[:, :, :, :, at].reshape(own_hidden, COL_TILE))
                value = value + resid[:, at] + rows_ref[7:8, at] + others[:, at].astype(f32)
                others[:, at] = value.astype(bf)

            finished = load(others, otok_ref, 19)
            s_out.arrive()
            gout_ref[...] = out_own[...].astype(f32) + out_theirs[...].astype(f32)
            s_small.over()
            s_qb.over()
            s_down.arrive()
            s_up.arrive()
            for side in range(2):
                resid[side * sub : (side + 1) * sub, :] = down_sum[side].astype(f32)
                for d in range(4 * levels):
                    to = (2 * d + side) * sub
                    gup_ref[:, to : to + sub] = up_sum[side, :, d * sub : (d + 1) * sub].astype(f32)

            cast = load(resid.at[0 : 2 * sub], gdown_ref, 22)

            def through_norm(i):
                at = row_at(i)
                hat, inverse = norm_parts(tok[p, at, :].astype(f32))
                grad = part_one[at, :] + yrecv[at, :].astype(f32)
                part_one[at, :] = dres[at, :] + norm_back(hat, inverse, rows_ref[0:1, :], grad)

            written = []
            for i in range(2):
                send_one[i].wait_recv()
                pl.loop(i * (tiles // 2), (i + 1) * (tiles // 2))(through_norm)
                rows = slice(i * middle, (i + 1) * middle)
                written.append(load(part_one.at[rows], gtok_ref.at[rows], 20 + i))
            s_small.arrive()
            gsmall_ref[...] = sm_own[...] + sm_theirs[...]
            for g, s in enumerate((s_qa, s_qb)):
                s.arrive()
                for side in range(2):
                    for t in range(3):
                        to = t * width + side * part + g * wide
                        gqkv_ref[:, to : to + wide] = qkv_sum[side, g, :, t * wide : (t + 1) * wide].astype(f32)
            for copy in written + [finished, cast]:
                copy.wait()

        pl.run_scoped(
            last_phase,
            pltpu.VMEM((2, length, width), bf),
            pltpu.VMEM((length, width), f32),
            pltpu.VMEM((length, own_hidden), bf),
            pltpu.VMEM(down_in.shape, bf),
            pltpu.VMEM((length, width), f32),
            pltpu.VMEM((length, width), bf),
        )

    pl.run_scoped(
        heads_phase,
        pltpu.VMEM((2, 2, length, 3 * wide), bf),
        pltpu.VMEM((2, length, width), bf),
        pltpu.VMEM(q_in.shape, bf),
        pltpu.VMEM(k_in.shape, bf),
        pltpu.VMEM(v_in.shape, bf),
    )
    send_out.wait_send()
    for copy in send_one + send_datt:
        copy.wait_send()
    for s in (s_down, s_up, s_out, s_qa, s_qb, s_small):
        s.finish()


def run_backward(dps, valid, vectors, lse, tok, dy, first, mixed, att, resid, second, act, slope, fq, fk, fv, fo, fup, fdown, half):
    levels = dps // 4
    _, length, width = dy.shape
    part = width // 2
    wide = part // 2
    own_hidden = act.shape[2]
    shard_rows, sub = width // dps, own_hidden // dps
    bf, f32 = jnp.bfloat16, jnp.float32
    any_spec = pl.BlockSpec(memory_space=pl.ANY)
    vmem = pl.BlockSpec(memory_space=pltpu.VMEM)
    smem = pl.BlockSpec(memory_space=pltpu.SMEM)
    whole = [
        ((length, width), bf),
        ((length, width), bf),
        ((length, width), f32),
        ((shard_rows, 6 * part), f32),
        ((shard_rows, width), f32),
        ((shard_rows, 2 * own_hidden), f32),
        ((2 * sub, width), f32),
        ((shard_rows + 8, SMALL), f32),
    ]
    scratch = (
        [
            pltpu.VMEM((levels, sub, width), bf),
            pltpu.VMEM((levels, sub, width), bf),
            pltpu.VMEM((levels - 1, sub, width), bf),
        ]
        + scatter_buffers(levels, shard_rows, own_hidden, bf)
        + scatter_buffers(levels, shard_rows, width, bf)
        + scatter_buffers(levels, shard_rows, 3 * wide, bf)
        + scatter_buffers(levels, shard_rows, 3 * wide, bf)
        + scatter_buffers(levels, shard_rows + 8, SMALL, f32)
        + [
            pltpu.VMEM((2, sub, width), bf),
            pltpu.VMEM((2, shard_rows, own_hidden), bf),
            pltpu.VMEM((2, 2, shard_rows, 3 * wide), bf),
            pltpu.VMEM((shard_rows, width), bf),
            pltpu.VMEM((shard_rows, width), bf),
            pltpu.VMEM((shard_rows + 8, SMALL), f32),
            pltpu.VMEM((shard_rows + 8, SMALL), f32),
            pltpu.VMEM((length, width), bf),
            pltpu.VMEM((length, width), bf),
            pltpu.VMEM((length, width), bf),
            pltpu.VMEM((length, width), f32),
            pltpu.VMEM((2, length, part), bf),
            pltpu.VMEM((length, part), bf),
            pltpu.VMEM((16, width), f32),
            pltpu.VMEM((8, own_hidden), f32),
            pltpu.SemaphoreType.DMA((6, scatter_sems(levels))),
            pltpu.SemaphoreType.DMA((24,)),
        ]
    )
    return pl.pallas_call(
        backward_layer,
        in_specs=[smem, vmem, vmem] + [any_spec] * 16,
        out_specs=[any_spec] * 3 + [vmem] * 3 + [any_spec, vmem],
        out_shape=[jax.ShapeDtypeStruct(*s) for s in whole],
        scratch_shapes=scratch,
        compiler_params=pltpu.CompilerParams(
            vmem_limit_bytes=62 * 2**20, collective_id=1, has_side_effects=True
        ),
        cost_estimate=pl.CostEstimate(flops=5 * 10**10, bytes_accessed=8 * 10**7, transcendentals=2 * 10**7),
    )(valid, vectors, lse, tok, dy, first, mixed, att, resid, second, act, slope, fq, fk, fv, fo, fup, fdown, half)


def per_device_pair(tokens, w_qkv, w_out, w_up, w_down, gains, biases, up_bias, valid, cotangent):
    _, length, width = tokens.shape
    shard_rows = w_qkv.shape[0]
    dps = lax.axis_size("dp")
    sub = w_down.shape[0] // 2

    smalls = jnp.concatenate([gains, biases], axis=1)
    smalls = jnp.concatenate(
        [
            jnp.pad(smalls, ((0, 0), (0, SMALL - smalls.shape[1]))),
            jnp.pad(up_bias.reshape(2, sub), ((0, 14), (0, 0))),
        ],
        axis=0,
    )
    (
        tok, dy, first, mixed, att, lse, residual, second, act, slope, fq, fk, fv, fo, fup, fdown, half, vectors, _
    ) = run_forward(
        dps, tokens.reshape(length, width), cotangent.reshape(length, width), w_qkv, w_out, w_up, w_down, smalls, valid
    )
    out_tokens, _, grad_tokens, grad_qkv, grad_out, grad_up, grad_down, grad_small = run_backward(
        dps, valid, vectors, lse, tok, dy, first, mixed, att, residual, second, act, slope, fq, fk, fv, fo, fup, fdown, half
    )
    return (
        out_tokens.reshape(tokens.shape),
        grad_tokens.reshape(tokens.shape),
        grad_qkv,
        grad_out,
        grad_up,
        grad_down,
        grad_small[:shard_rows, :2],
        grad_small[:shard_rows, 2:8],
        grad_small[shard_rows : shard_rows + 2, :].reshape(-1),
    )


def per_device(tokens, w_qkv, w_out, w_up, w_down, gains, biases, up_bias, valid, cotangent):
    images, length, width = tokens.shape
    rows = images * length
    shard_rows = w_qkv.shape[0]
    hidden = w_up.shape[1]
    ups = up_bias.shape[0] // shard_rows
    shards = lax.axis_size("seq")
    dps = lax.axis_size("dp")
    at = lax.axis_index("seq").astype(jnp.int32)
    place = at.reshape(1)
    part = width // shards
    own_hidden = hidden // shards
    sub = w_down.shape[0] // shards
    pairs_all = part // PAIR

    gather = functools.partial(lax.all_gather, axis_name="dp", axis=0, tiled=True)
    scatter = functools.partial(lax.psum_scatter, axis_name="dp", scatter_dimension=0, tiled=True)

    def pick(values, axis):
        return lax.dynamic_index_in_dim(values, at, axis, keepdims=False)

    smalls = jnp.concatenate([gains, biases, up_bias.reshape(shard_rows, ups)], axis=1)
    smalls = jnp.pad(smalls, ((0, 0), (0, SMALL - smalls.shape[1])))
    part_qkv = pick(w_qkv.reshape(shard_rows, 3, shards, part), 2).reshape(shard_rows, 3 * part)
    part_up = pick(w_up.reshape(shard_rows, dps, shards, sub), 2).reshape(shard_rows, own_hidden)
    part_down = pick(w_down.reshape(shards, sub, width), 0)
    full_qkvs = gather(jnp.concatenate([part_qkv, smalls], axis=1))
    w_out, full_qkvs = lax.optimization_barrier((w_out, full_qkvs))
    full_out = gather(w_out)
    part_up, full_out = lax.optimization_barrier((part_up, full_out))
    full_up = gather(part_up)
    part_down, full_up = lax.optimization_barrier((part_down, full_up))
    full_down = gather(part_down)

    flat_tokens = tokens.reshape(rows, width)
    flat_grad = cotangent.reshape(rows, width)
    all_tokens = everyone(flat_tokens, shards)
    flat_grad, all_tokens = lax.optimization_barrier((flat_grad, all_tokens))
    all_grad = everyone(flat_grad, shards).reshape(shards * rows, width)

    full_qkv = full_qkvs[:, : 3 * part]
    small = full_qkvs[:, 3 * part :].astype(jnp.float32).T
    gain_one, gain_two = small[0], small[1]
    bias_one, bias_q, bias_v, bias_out, bias_two, bias_down = (small[2 + i] for i in range(6))
    bias_up = pick(small[8 : 8 + ups].T.reshape(dps, shards, sub), 1).reshape(-1)
    bias_mixed = jnp.concatenate(
        [pick(bias_q.reshape(shards, part), 0), jnp.zeros((part,), jnp.float32), pick(bias_v.reshape(shards, part), 0)]
    )

    every_tokens = all_tokens.reshape(shards * rows, width).astype(jnp.float32)
    hat_one, inverse_one = norm_parts(every_tokens)
    first = (hat_one * gain_one + bias_one).astype(jnp.bfloat16)
    mixed = (mat(first, full_qkv) + bias_mixed).astype(jnp.bfloat16).reshape(shards, rows, 3 * part)

    groups = GROUPS if pairs_all % GROUPS == 0 else 1
    pairs = pairs_all // groups
    wide = pairs * PAIR
    forward = [attend_forward(images, place, valid, mixed, g * pairs, pairs) for g in range(groups)]
    blocks = []
    for j in range(shards):
        for g in range(groups):
            attended = forward[g][0]
            if j > 0:
                attended = jnp.roll(shift(attended, shards, -j), j, axis=0)
            blocks.append(attended.reshape(shards * rows, wide))
    merged = jnp.concatenate(blocks, axis=1)
    turned_out = jnp.roll(full_out, -at * part, axis=0)

    branch = mat(merged, turned_out) + bias_out
    residual = every_tokens + branch
    hat_two, inverse_two = norm_parts(residual)
    second = (hat_two * gain_two + bias_two).astype(jnp.bfloat16)
    upward = mat(second, full_up) + bias_up
    cdf = 0.5 * (1.0 + lax.erf(upward * 0.5**0.5))
    activated = (upward * cdf).astype(jnp.bfloat16)
    slope = cdf + upward * (jnp.exp(-0.5 * upward * upward) * 0.3989422804014327)
    slope = slope.astype(jnp.bfloat16)

    grad_act = dot_f32(all_grad, full_down, ((1,), (1,)))
    grad_upward = (grad_act * slope.astype(jnp.float32)).astype(jnp.bfloat16)

    def summed(left, right, dims):
        parts = [
            dot_f32(left[j * rows : (j + 1) * rows], right, dims) for j in range(shards)
        ]
        total = parts[0]
        for j in range(1, shards):
            total = total + shift(parts[j].astype(jnp.bfloat16), shards, j).astype(jnp.float32)
        return total

    grad_second = summed(grad_upward, full_up, ((1,), (1,)))
    grad_down = dot_f32(activated, all_grad, ((0,), (0,))).astype(jnp.bfloat16)
    piece_down = scatter(grad_down)
    grad_up = dot_f32(second, grad_upward, ((0,), (0,))).astype(jnp.bfloat16)
    grad_up, piece_down = lax.optimization_barrier((grad_up, piece_down))
    piece_up = scatter(grad_up)

    own_hat = hat_two[:rows]
    grad_resid = flat_grad.astype(jnp.float32) + norm_back(own_hat, inverse_two[:rows], gain_two, grad_second)
    grad_gain_two, grad_bias_two = token_sum(grad_second * own_hat), token_sum(grad_second)
    grad_branch = grad_resid.astype(jnp.bfloat16)
    grad_merged = dot_f32(grad_branch, turned_out, ((1,), (1,))).astype(jnp.bfloat16)
    received = [None] * shards
    for g in range(groups):
        lo = g * wide
        blocks = [grad_merged[:, lo : lo + wide]] + [None] * (shards - 1)
        for j in range(1, shards):
            blocks[shards - j] = shift(grad_merged[:, j * part + lo : j * part + lo + wide], shards, j)
        received[g] = jnp.stack(blocks)

    grad_out = dot_f32(merged[:rows], grad_branch, ((0,), (0,))).astype(jnp.bfloat16)
    grad_out = jnp.roll(grad_out, at * part, axis=0)
    grad_out, piece_up = lax.optimization_barrier((grad_out, piece_up))
    piece_out = scatter(grad_out)

    backs = [
        attend_backward(images, place, valid, mixed, g * pairs, pairs, *forward[g], received[g]) for g in range(groups)
    ]
    grad_mixed = jnp.concatenate(
        [back[t].reshape(shards * rows, wide) for t in range(3) for back in backs], axis=1
    )
    grad_first = summed(grad_mixed, full_qkv, ((1,), (1,)))
    grad_qkv = dot_f32(first, grad_mixed, ((0,), (0,))).astype(jnp.bfloat16)

    grad_tokens = grad_resid + norm_back(hat_one[:rows], inverse_one[:rows], gain_one, grad_first)
    grad_gain_one, grad_bias_one = token_sum(grad_first * hat_one[:rows]), token_sum(grad_first)

    def spread(values, before):
        out = jnp.zeros((before, shards, values.size // before), jnp.float32)
        return lax.dynamic_update_slice_in_dim(out, values.reshape(before, 1, -1), at, 1).reshape(-1)

    bias_sums = token_sum(grad_mixed)
    small_grads = jnp.stack(
        [
            grad_gain_one, grad_gain_two, grad_bias_one, spread(bias_sums[:part], 1), spread(bias_sums[2 * part :], 1),
            token_sum(grad_branch), grad_bias_two, token_sum(flat_grad),
        ],
        axis=1,
    )
    up_sums = spread(token_sum(grad_upward), dps).reshape(width, ups)
    small_grads = jnp.concatenate([small_grads, up_sums], axis=1)
    small_grads = jnp.pad(small_grads, ((0, 0), (0, SMALL - small_grads.shape[1])))
    grad_qkvs = jnp.concatenate([grad_qkv, small_grads.astype(jnp.bfloat16)], axis=1)
    grad_qkvs, piece_out = lax.optimization_barrier((grad_qkvs, piece_out))
    piece_qkvs = scatter(grad_qkvs)

    output = summed(activated, full_down, ((1,), (0,)))
    out_tokens = (residual[:rows] + output + bias_down).astype(jnp.bfloat16)

    total_down = in_order(piece_down, shards, at).astype(jnp.float32).reshape(shards * sub, width)
    total_up = in_order(piece_up.reshape(shard_rows, dps, sub), shards, at).astype(jnp.float32)
    total_up = total_up.transpose(1, 2, 0, 3).reshape(shard_rows, hidden)
    total_out = in_order(piece_out, shards, at).astype(jnp.float32).sum(0)
    every_qkvs = in_order(piece_qkvs, shards, at).astype(jnp.float32)
    total_qkv = every_qkvs[:, :, : 3 * part].reshape(shards, shard_rows, 3, part)
    total_qkv = total_qkv.transpose(1, 2, 0, 3).reshape(shard_rows, 3 * width)
    total_small = every_qkvs[:, :, 3 * part :].sum(0)
    return (
        out_tokens.reshape(tokens.shape),
        grad_tokens.reshape(tokens.shape),
        total_qkv,
        total_out,
        total_up,
        total_down,
        total_small[:, :2],
        total_small[:, 2:8],
        total_small[:, 8 : 8 + ups].reshape(-1),
    )


def solution(mesh):
    paired = mesh.shape["seq"] == 2 and mesh.shape["dp"] == 16
    return jax.shard_map(
        per_device_pair if paired else per_device,
        mesh=mesh,
        in_specs=(
            P("dp", "seq", None),
            P("dp", None),
            P("dp", None),
            P("dp", None),
            P("dp", None),
            P("dp", None),
            P("dp", None),
            P("dp"),
            P("dp"),
            P("dp", "seq", None),
        ),
        out_specs=(
            P("dp", "seq", None),
            P("dp", "seq", None),
            P("dp", None),
            P("dp", None),
            P("dp", None),
            P("dp", None),
            P("dp", None),
            P("dp", None),
            P("dp"),
        ),
        check_vma=False,
    )
```

```python
import functools

import jax
import jax.numpy as jnp
from jax import lax
from jax.experimental import pallas as pl
from jax.experimental.pallas import tpu as pltpu
from jax.sharding import PartitionSpec as P

HD = 64
PAIR = 2 * HD
EPSILON = 1e-06
NEG_FILL = -1e30
SMALL = 128
GROUPS = 2


def dot_f32(a, b, dims):
    return lax.dot_general(a, b, (dims, ((), ())), preferred_element_type=jnp.float32)


def mat(a, b):
    return dot_f32(a, b, ((1,), (0,)))


def norm_parts(values):
    average = jnp.mean(values, axis=-1, keepdims=True)
    centered = values - average
    variance = jnp.mean(centered * centered, axis=-1, keepdims=True)
    inverse = lax.rsqrt(variance + EPSILON)
    return centered * inverse, inverse


def norm_back(hat, inverse, scales, grad):
    scaled = grad * scales
    first = jnp.mean(scaled, axis=-1, keepdims=True)
    second = jnp.mean(scaled * hat, axis=-1, keepdims=True)
    return inverse * (scaled - first - hat * second)


def lanes(head):
    lane = lax.broadcasted_iota(jnp.int32, (1, PAIR), 1)
    own = (lane < HD) if head == 0 else (lane >= HD)
    return own, lane - (HD if head == 0 else 0)


def key_bias(place_ref, valid_ref, length, shards):
    row = lax.broadcasted_iota(jnp.int32, (shards * length, 1), 0)
    position = row + place_ref[0] * length
    position = jnp.where(position >= shards * length, position - shards * length, position)
    allowed = position < valid_ref[pl.program_id(0)]
    return jnp.where(allowed, 0.0, NEG_FILL).astype(jnp.float32)


def augmented(values, head, extra):
    own, free = lanes(head)
    out = jnp.where(own, values, 0.0)
    for at, column in enumerate(extra):
        out = jnp.where(free == at, column, out)
    return out.astype(jnp.bfloat16)


def rows_with(values_t, head, extra):
    row = lax.broadcasted_iota(jnp.int32, (PAIR, 1), 0)
    own = (row < HD) if head == 0 else (row >= HD)
    free = row - (HD if head == 0 else 0)
    out = jnp.where(own, values_t, 0.0)
    for at, line in enumerate(extra):
        out = jnp.where(free == at, line, out)
    return out.astype(jnp.bfloat16)


def split_three(line):
    high = line.astype(jnp.bfloat16).astype(jnp.float32)
    rest = line - high
    middle = rest.astype(jnp.bfloat16).astype(jnp.float32)
    return high, middle, rest - middle


def forward_kernel(place_ref, valid_ref, q_ref, k_ref, v_ref, out_ref, lse_ref):
    shards, length, _ = q_ref.shape
    bias = key_bias(place_ref, valid_ref, length, shards)
    keys = k_ref[...].reshape(shards * length, PAIR).astype(jnp.float32)
    values = v_ref[...].reshape(shards * length, PAIR).astype(jnp.float32)
    keys_of = [augmented(keys, head, [bias]) for head in range(2)]
    values_of = [augmented(values, head, [1.0]).T for head in range(2)]
    for shard in range(shards):
        queries = q_ref[shard].astype(jnp.float32).T * HD**-0.5
        halves = []
        for head in range(2):
            scores = mat(keys_of[head], rows_with(queries, head, [1.0]))
            top = jnp.max(scores, axis=0, keepdims=True)
            weight = jnp.exp(scores - top).astype(jnp.bfloat16)
            part = mat(values_of[head], weight)
            at = HD * (1 - head)
            row_total = part[at : at + 1, :]
            halves.append(part[HD * head : HD * (head + 1), :] / row_total)
            lse_ref[0, 0, shard, head : head + 1, :] = top + jnp.log(row_total)
        out_ref[shard] = jnp.concatenate(halves, axis=0).T.astype(out_ref.dtype)


def backward_kernel(place_ref, valid_ref, q_ref, k_ref, v_ref, out_ref, lse_ref, da_ref, dq_ref, dk_ref, dv_ref):
    shards, length, _ = q_ref.shape
    bias = key_bias(place_ref, valid_ref, length, shards)
    keys = k_ref[...].reshape(shards * length, PAIR).astype(jnp.float32)
    values = v_ref[...].reshape(shards * length, PAIR).astype(jnp.float32)
    keys_of = [augmented(keys, head, [bias, 1.0, 1.0, 1.0]) for head in range(2)]
    values_of = [augmented(values, head, [1.0, 1.0, 1.0]) for head in range(2)]
    plain_keys = [augmented(keys, head, []).T for head in range(2)]
    dk = dv = None
    for shard in range(shards):
        queries = q_ref[shard].astype(jnp.float32) * HD**-0.5
        grads = da_ref[shard].astype(jnp.float32)
        queries_t, grads_t = queries.T, grads.T
        product = grads_t * out_ref[shard].astype(jnp.float32).T
        dq = None
        for head in range(2):
            lse = lse_ref[0, 0, shard, head : head + 1, :]
            delta = jnp.sum(product[HD * head : HD * (head + 1), :], axis=0, keepdims=True)
            scores = mat(keys_of[head], rows_with(queries_t, head, (1.0,) + split_three(-lse)))
            probs = jnp.exp(scores)
            moved = mat(values_of[head], rows_with(grads_t, head, split_three(-delta)))
            dscores = (probs * moved).astype(jnp.bfloat16)
            part_v = mat(probs.astype(jnp.bfloat16), augmented(grads, head, []))
            part_k = mat(dscores, augmented(queries, head, []))
            part_q = mat(plain_keys[head], dscores)
            dq = part_q if dq is None else dq + part_q
            dk = part_k if dk is None else dk + part_k
            dv = part_v if dv is None else dv + part_v
        dq_ref[shard] = (dq * HD**-0.5).T.astype(dq_ref.dtype)
    dk_ref[...] = dk.astype(dk_ref.dtype).reshape(dk_ref.shape)
    dv_ref[...] = dv.astype(dv_ref.dtype).reshape(dv_ref.shape)


def attention_specs(shards, length, pairs_all, first_pair):
    smem = pl.BlockSpec(memory_space=pltpu.SMEM)
    mixed = [
        pl.BlockSpec((shards, length, PAIR), lambda i, h, t=t: (0, i, t * pairs_all + first_pair + h))
        for t in range(3)
    ]
    plain = pl.BlockSpec((shards, length, PAIR), lambda i, h: (0, i, h))
    lse = pl.BlockSpec((1, 1, shards, 2, length), lambda i, h: (i, h, 0, 0, 0))
    return smem, mixed, plain, lse


def attend_forward(images, place, valid, mixed, first_pair, pairs):
    shards, rows, width3 = mixed.shape
    length = rows // images
    smem, block3, plain, lse = attention_specs(shards, length, width3 // 3 // PAIR, first_pair)
    work = shards * shards * rows * length * pairs
    return pl.pallas_call(
        forward_kernel,
        grid=(images, pairs),
        in_specs=[smem, smem] + block3,
        out_specs=[plain, lse],
        out_shape=[
            jax.ShapeDtypeStruct((shards, rows, pairs * PAIR), jnp.bfloat16),
            jax.ShapeDtypeStruct((images, pairs, shards, 2, length), jnp.float32),
        ],
        compiler_params=pltpu.CompilerParams(vmem_limit_bytes=40 * 2**20),
        cost_estimate=pl.CostEstimate(
            flops=8 * work * PAIR, bytes_accessed=8 * shards * rows * pairs * PAIR, transcendentals=2 * work,
        ),
    )(place, valid, mixed, mixed, mixed)


def attend_backward(images, place, valid, mixed, first_pair, pairs, attended, lse_in, da):
    shards, rows, width3 = mixed.shape
    length = rows // images
    smem, block3, plain, lse = attention_specs(shards, length, width3 // 3 // PAIR, first_pair)
    low = jax.ShapeDtypeStruct((shards, rows, pairs * PAIR), jnp.bfloat16)
    work = shards * shards * rows * length * pairs
    return pl.pallas_call(
        backward_kernel,
        grid=(images, pairs),
        in_specs=[smem, smem] + block3 + [plain, lse, plain],
        out_specs=[plain] * 3,
        out_shape=[low] * 3,
        compiler_params=pltpu.CompilerParams(vmem_limit_bytes=48 * 2**20),
        cost_estimate=pl.CostEstimate(
            flops=20 * work * PAIR, bytes_accessed=16 * shards * rows * pairs * PAIR, transcendentals=2 * work,
        ),
    )(place, valid, mixed, mixed, mixed, attended, lse_in, da)


def shift(values, shards, step):
    return lax.ppermute(values, "seq", [(i, (i + step) % shards) for i in range(shards)])


def everyone(values, shards, step_axis=0):
    return jnp.stack([values] + [shift(values, shards, -j) for j in range(1, shards)], axis=step_axis)


def in_order(values, shards, place):
    if shards == 2:
        other = shift(values, shards, 1)
        low = jnp.where(place == 0, values, other)
        high = jnp.where(place == 0, other, values)
        return jnp.stack([low, high])
    return lax.all_gather(values, "seq", axis=0)


def token_sum(values):
    return jnp.sum(values.astype(jnp.float32), axis=0)


MESH = pl.DeviceIdType.MESH


class Peers:
    def __init__(self, dps):
        self.dp = lax.axis_index("dp")
        self.seq = lax.axis_index("seq")
        self.levels = dps // 4
        self.z = self.dp // 4
        self.x = self.dp % 4 // 2
        self.core = self.dp % 2

    def up(self, step):
        return ((self.z + step) % self.levels * 4 + self.dp % 4, self.seq)

    def across(self):
        return (self.dp + 2 - 4 * self.x, self.seq)

    def sibling(self):
        return (self.dp + 1 - 2 * self.core, self.seq)

    def other(self):
        return (self.dp, 1 - self.seq)

    def all(self):
        return [self.up(s) for s in range(1, self.levels)] + [self.across(), self.sibling(), self.other()]

    def greet(self):
        barrier = pltpu.get_barrier_semaphore()
        for device in self.all():
            pl.semaphore_signal(barrier, inc=1, device_id=device, device_id_type=MESH)
        pl.semaphore_wait(barrier, len(self.all()))


def remote(src, dst, send, recv, device):
    return pltpu.make_async_remote_copy(
        src_ref=src, dst_ref=dst, send_sem=send, recv_sem=recv, device_id=device, device_id_type=MESH
    )


class Gather:
    def __init__(self, peers, src, full, sems, cut=(slice(None), slice(None))):
        levels = peers.levels
        at = (peers.z, peers.x, peers.core) + cut
        self.local = pltpu.make_async_copy(src, full.at[at], sems.at[0])
        self.first = [
            remote(src, full.at[at], sems.at[2 * s + 3], sems.at[2 * s + 4], peers.up(s)) for s in range(1, levels)
        ]
        column = full.at[(slice(None), peers.x, peers.core) + cut]
        self.second = remote(column, column, sems.at[1], sems.at[2], peers.across())
        half = full.at[(slice(None), slice(None), peers.core) + cut]
        self.third = remote(half, half, sems.at[3], sems.at[4], peers.sibling())

    def start(self):
        self.local.start()
        for copy in self.first:
            copy.start()

    def cross(self):
        self.local.wait()
        for copy in self.first:
            copy.wait_recv()
        self.second.start()

    def share(self):
        self.second.wait_recv()
        self.third.start()

    def arrive(self):
        self.third.wait_recv()

    def finish(self):
        for copy in self.first + [self.second, self.third]:
            copy.wait_send()


def gather_sems(levels):
    return 2 * levels + 3


def query_tiles(total):
    first = max(total // 512, 1) * 256
    return [(0, first), (first, total)]


def attend_pair(valid_ref, mixed, att, lse_ref, pair, base):
    shards, length, width3 = mixed.shape
    part = width3 // 3

    def columns(t):
        return pl.ds(pl.multiple_of(t * part + pair * PAIR, PAIR), PAIR)

    row = lax.broadcasted_iota(jnp.int32, (shards * length, 1), 0)
    bias = jnp.where(row < valid_ref[0], 0.0, NEG_FILL).astype(jnp.float32)
    keys = mixed[:, :, columns(1)].reshape(shards * length, PAIR).astype(jnp.float32)
    values = mixed[:, :, columns(2)].reshape(shards * length, PAIR).astype(jnp.float32)
    keys_of = [augmented(keys, head, [bias]) for head in range(2)]
    values_of = [augmented(values, head, [1.0]).T for head in range(2)]
    out_columns = pl.ds(pl.multiple_of(base + pair * PAIR, PAIR), PAIR)
    queries_all = mixed[:, :, columns(0)].reshape(shards * length, PAIR)
    outs = []
    for start, stop in query_tiles(shards * length):
        queries = queries_all[start:stop].astype(jnp.float32).T * HD**-0.5
        halves = []
        for head in range(2):
            scores = mat(keys_of[head], rows_with(queries, head, [1.0]))
            top = jnp.max(scores, axis=0, keepdims=True)
            weight = jnp.exp(scores - top).astype(jnp.bfloat16)
            product = mat(values_of[head], weight)
            at = HD * (1 - head)
            row_total = product[at : at + 1, :]
            halves.append(product[HD * head : HD * (head + 1), :] / row_total)
            lse_ref[pair, head : head + 1, start:stop] = top + jnp.log(row_total)
        outs.append(jnp.concatenate(halves, axis=0).T.astype(att.dtype))
    att[:, :, out_columns] = jnp.concatenate(outs, axis=0).reshape(shards, length, PAIR)


def place_blocks(grad, z, value):
    rows = grad.shape[3]
    for x in range(2):
        for core in range(2):
            at = (2 * x + core) * rows
            grad[core, z, x] = value[at : at + rows, :].astype(grad.dtype)


ROW_TILE = 144
COL_TILE = 512


def forward_layer(
    valid_ref, tokens, cotangent, w_qkv, w_out, w_up, w_down, small,
    tok_out, dy_out, first_out, mixed_out, att_out, lse_ref, resid_out, second_out, act_out, slope_out,
    q_out, k_out, v_out, o_out, up_out, down_out, half_out, rows_ref, bup_ref,
    tok, first, mixed, att, resid, second, act, slope, fsmall, fq, fk, fv, fo, fup, fdown, my_up, dy, grad, cored, gsems, sems,
):
    levels = fq.shape[0]
    peers = Peers(4 * levels)
    p = peers.seq
    length, width = tokens.shape
    part = width // 2
    sub = fdown.shape[3]
    shard_rows = w_out.shape[0]
    peers.greet()

    send_tok = remote(tokens, tok.at[p], sems.at[0], sems.at[1], peers.other())
    send_tok.start()
    own = lambda t: w_qkv.at[:, pl.ds(pl.multiple_of(t * width + p * part, PAIR), part)]
    own_hidden = act.shape[2]
    half = own_hidden // 2
    low_up, high_up = (slice(None), pl.ds(0, half)), (slice(None), pl.ds(half, half))
    down_cuts = [(0, sub // 2), (sub // 2, sub // 4), (3 * sub // 4, sub // 4)]
    g_small = Gather(peers, small, fsmall, gsems.at[0])
    g_q = Gather(peers, own(0), fq, gsems.at[1])
    g_k = Gather(peers, own(1), fk, gsems.at[2])
    g_v = Gather(peers, own(2), fv, gsems.at[3])
    g_out = Gather(peers, w_out, fo, gsems.at[4])
    g_up = Gather(peers, my_up.at[:, 0:half], fup, gsems.at[5], low_up)
    g_up2 = Gather(peers, my_up.at[:, half : 2 * half], fup, gsems.at[6], high_up)
    g_down, g_down2, g_down3 = (
        Gather(
            peers, w_down.at[pl.ds(pl.multiple_of(p * sub + start, 16), size)], fdown, gsems.at[7 + i],
            (pl.ds(start, size), slice(None)),
        )
        for i, (start, size) in enumerate(down_cuts)
    )
    gathers = [g_small, g_q, g_k, g_v, g_out, g_up, g_up2, g_down, g_down2, g_down3]
    for g in (g_small, g_q, g_k, g_v):
        g.start()
    for d in range(4 * levels):
        my_up[:, d * sub : (d + 1) * sub] = w_up[:, pl.ds(pl.multiple_of((2 * d + p) * sub, PAIR), sub)]

    own_tok = pltpu.make_async_copy(tokens, tok.at[p], sems.at[2])
    own_tok.start()
    own_dy = pltpu.make_async_copy(cotangent, dy.at[p], sems.at[3])
    own_dy.start()

    def normed(shard):
        @pl.loop(0, length // ROW_TILE)
        def _(i):
            at = pl.ds(pl.multiple_of(i * ROW_TILE, 16), ROW_TILE)
            resid[shard, at, :] = norm_parts(tok[shard, at, :].astype(jnp.float32))[0]

    g_small.cross()
    g_q.cross()
    own_tok.wait()
    normed(p)
    g_k.cross()
    g_v.cross()
    g_out.start()
    g_small.share()
    g_q.share()
    g_k.share()
    middle = length // 2
    send_dy = [
        remote(
            cotangent.at[pl.ds(i * middle, middle)], dy.at[p, pl.ds(i * middle, middle)],
            sems.at[(4, 14)[i]], sems.at[(5, 15)[i]], peers.other(),
        )
        for i in range(2)
    ]
    send_tok.wait_recv()
    send_dy[0].start()
    normed(1 - p)
    g_small.arrive()
    vectors = fsmall[:, :, :, 0:shard_rows, :].reshape(width, SMALL).astype(jnp.float32).T
    rows_ref[...] = vectors[0:16, :]
    for d in range(4 * levels):
        at = (d // 4, d % 4 // 2, d % 2)
        pair_rows = fsmall[at + (slice(shard_rows, shard_rows + 16),)].astype(jnp.float32)
        bup_ref[0:1, d * sub : (d + 1) * sub] = jnp.where(p == 0, pair_rows[0:1, :sub], pair_rows[1:2, :sub])

    for shard in range(2):
        @pl.loop(0, length // ROW_TILE)
        def _(i):
            at = pl.ds(pl.multiple_of(i * ROW_TILE, 16), ROW_TILE)
            first[shard, at, :] = (resid[shard, at, :] * rows_ref[0:1, :] + rows_ref[2:3, :]).astype(jnp.bfloat16)

    own_columns = pl.ds(pl.multiple_of(p * part, PAIR), part)

    def project(t, full, bias):
        weight = full[...].reshape(width, part)
        @pl.loop(0, 2)
        def _(shard):
            out = mat(first[shard], weight)
            if bias is not None:
                out = out + rows_ref[bias : bias + 1, own_columns]
            mixed[shard, :, t * part : (t + 1) * part] = out.astype(jnp.bfloat16)

    saves = []
    pairs = part // PAIR

    def save(src, dst):
        copy = pltpu.make_async_copy(src, dst, sems.at[32 + 2 * pairs + len(saves)])
        saves.append(copy)
        copy.start()

    save(tok, tok_out)
    save(first, first_out)
    g_v.share()
    g_q.arrive()
    project(0, fq, 3)
    g_up.start()
    g_k.arrive()
    project(1, fk, None)
    g_out.cross()
    g_up2.start()
    g_v.arrive()
    project(2, fv, 4)
    save(mixed, mixed_out)
    save(fq, q_out)
    save(fk, k_out)
    save(fv, v_out)

    pairs = part // PAIR
    att_copies = []
    for pair in range(pairs):
        columns = pl.ds(pl.multiple_of(p * part + pair * PAIR, PAIR), PAIR)
        att_copies.append(
            remote(
                att.at[:, :, columns], att.at[:, :, columns], sems.at[32 + 2 * pair], sems.at[33 + 2 * pair],
                peers.other(),
            )
        )

    @pl.loop(0, pairs)
    def _(pair):
        attend_pair(valid_ref, mixed, att, lse_ref, pair, p * part)
        for i in range(pairs):
            @pl.when(pair == i)
            def _():
                att_copies[i].start()
                if i == min(1, pairs - 1):
                    g_up.cross()
                    g_down.start()
                    g_out.share()
                if i == pairs - 1:
                    g_up2.cross()
                    g_down2.start()
                    g_up.share()

    g_out.arrive()
    save(fo, o_out)
    for copy in att_copies:
        copy.wait_recv()
    save(att, att_out)
    send_dy[1].start()
    out_weight = fo[...].reshape(width, width)

    def finish_rows(shard):
        @pl.loop(0, length // ROW_TILE)
        def _(i):
            at = pl.ds(pl.multiple_of(i * ROW_TILE, 16), ROW_TILE)
            value = mat(att[shard, at, :], out_weight) + rows_ref[5:6, :] + tok[shard, at, :].astype(jnp.float32)
            resid[shard, at, :] = value
            hat, _ = norm_parts(value)
            second[shard, at, :] = (hat * rows_ref[1:2, :] + rows_ref[6:7, :]).astype(jnp.bfloat16)

    finish_rows(0)
    finish_rows(1)
    save(resid.at[p], resid_out)
    save(second, second_out)

    def into_hidden(first_tile, tiles):
        @pl.loop(0, 2 * tiles)
        def _(step):
            shard = step // tiles
            at = pl.ds(pl.multiple_of((first_tile + step % tiles) * COL_TILE, PAIR), COL_TILE)
            upward = mat(second[shard], fup[:, :, :, :, at].reshape(width, COL_TILE)) + bup_ref[0:1, at]
            cdf = 0.5 * (1.0 + lax.erf(upward * 0.5**0.5))
            act[shard, :, at] = (upward * cdf).astype(jnp.bfloat16)
            value = cdf + upward * (jnp.exp(-0.5 * upward * upward) * 0.3989422804014327)
            slope[shard, :, at] = value.astype(jnp.bfloat16)

    tiles = half // COL_TILE
    g_up.arrive()
    into_hidden(0, tiles)
    g_down.cross()
    g_down3.start()
    g_up2.share()
    g_up2.arrive()
    save(fup, up_out)
    into_hidden(tiles, tiles)
    save(act, act_out)
    save(slope, slope_out)
    g_down2.cross()
    g_down.share()
    g_down3.cross()
    own_dy.wait()
    for copy in send_dy:
        copy.wait_recv()
    save(dy, dy_out)

    @pl.loop(0, levels)
    def _(z):
        at = pl.ds(pl.multiple_of(z * 4 * sub, PAIR), 4 * sub)
        value = dot_f32(act[:, :, at].reshape(2 * length, 4 * sub), dy[...].reshape(2 * length, width), ((0,), (0,)))
        place_blocks(grad, z, value)

    send_grad = remote(grad.at[1 - peers.core], cored, sems.at[6], sems.at[7], peers.sibling())
    send_grad.start()
    g_down.arrive()
    low, high = pl.ds(0, sub // 2), pl.ds(sub // 2, sub // 2)
    save(fdown.at[:, :, :, low], down_out.at[:, :, :, low])
    g_down2.share()
    send_grad.wait_recv()

    @pl.loop(0, levels)
    def _(z):
        for x in range(2):
            total = grad[peers.core, z, x].astype(jnp.float32) + cored[z, x].astype(jnp.float32)
            grad[peers.core, z, x] = total.astype(jnp.bfloat16)

    save(grad.at[peers.core], half_out)
    g_down3.share()
    g_down2.arrive()
    g_down3.arrive()
    save(fdown.at[:, :, :, high], down_out.at[:, :, :, high])
    send_grad.wait_send()
    send_tok.wait_send()
    for copy in send_dy:
        copy.wait_send()
    for copy in att_copies:
        copy.wait_send()
    for g in gathers:
        g.finish()
    for copy in saves:
        copy.wait()


def run_forward(dps, tokens, cotangent, w_qkv, w_out, w_up, w_down, small, valid):
    length, width = tokens.shape
    levels = dps // 4
    part = width // 2
    shard_rows = w_out.shape[0]
    own_hidden = w_up.shape[1] // 2
    sub = w_down.shape[0] // 2
    pairs = part // PAIR
    bf, f32 = jnp.bfloat16, jnp.float32
    any_spec = pl.BlockSpec(memory_space=pl.ANY)
    vmem = pl.BlockSpec(memory_space=pltpu.VMEM)
    smem = pl.BlockSpec(memory_space=pltpu.SMEM)
    grid = (levels, 2, 2)
    whole = [
        ((2, length, width), bf),
        ((2, length, width), bf),
        ((2, length, width), bf),
        ((2, length, 3 * part), bf),
        ((2, length, width), bf),
        ((pairs, 2, 2 * length), f32),
        ((length, width), f32),
        ((2, length, width), bf),
        ((2, length, own_hidden), bf),
        ((2, length, own_hidden), bf),
        (grid + (shard_rows, part), bf),
        (grid + (shard_rows, part), bf),
        (grid + (shard_rows, part), bf),
        (grid + (shard_rows, width), bf),
        (grid + (shard_rows, own_hidden), bf),
        (grid + (sub, width), bf),
        ((levels, 2, sub, width), bf),
        ((16, width), f32),
        ((8, own_hidden), f32),
    ]
    in_vmem = (5, 17, 18)
    scratch = [
        pltpu.VMEM((2, length, width), bf),
        pltpu.VMEM((2, length, width), bf),
        pltpu.VMEM((2, length, 3 * part), bf),
        pltpu.VMEM((2, length, width), bf),
        pltpu.VMEM((2, length, width), f32),
        pltpu.VMEM((2, length, width), bf),
        pltpu.VMEM((2, length, own_hidden), bf),
        pltpu.VMEM((2, length, own_hidden), bf),
        pltpu.VMEM(grid + (shard_rows + 16, SMALL), bf),
        pltpu.VMEM(grid + (shard_rows, part), bf),
        pltpu.VMEM(grid + (shard_rows, part), bf),
        pltpu.VMEM(grid + (shard_rows, part), bf),
        pltpu.VMEM(grid + (shard_rows, width), bf),
        pltpu.VMEM(grid + (shard_rows, own_hidden), bf),
        pltpu.VMEM(grid + (sub, width), bf),
        pltpu.VMEM((shard_rows, own_hidden), bf),
        pltpu.VMEM((2, length, width), bf),
        pltpu.VMEM((2, levels, 2, sub, width), bf),
        pltpu.VMEM((levels, 2, sub, width), bf),
        pltpu.SemaphoreType.DMA((10, gather_sems(levels))),
        pltpu.SemaphoreType.DMA((52 + 2 * pairs,)),
    ]
    return pl.pallas_call(
        forward_layer,
        in_specs=[smem, any_spec, any_spec, vmem, vmem, vmem, vmem, vmem],
        out_specs=[vmem if i in in_vmem else any_spec for i in range(len(whole))],
        out_shape=[jax.ShapeDtypeStruct(*s) for s in whole],
        scratch_shapes=scratch,
        compiler_params=pltpu.CompilerParams(
            vmem_limit_bytes=62 * 2**20, collective_id=0, has_side_effects=True
        ),
        cost_estimate=pl.CostEstimate(flops=3 * 10**10, bytes_accessed=8 * 10**7, transcendentals=2 * 10**7),
    )(valid, tokens, cotangent, w_qkv, w_out, w_up, w_down, small)


class Scatter:
    def __init__(self, peers, grad, cored, crossed, risen, own, theirs, sems):
        core, x, z = peers.core, peers.x, peers.z
        self.peers, self.grad, self.cored, self.crossed, self.risen = peers, grad, cored, crossed, risen
        self.own = own
        self.first = remote(grad.at[1 - core], cored, sems.at[0], sems.at[1], peers.sibling())
        self.second = remote(grad.at[core, :, 1 - x], crossed, sems.at[2], sems.at[3], peers.across())
        self.third = [
            remote(
                grad.at[core, (z + s) % peers.levels, x], risen.at[s - 1], sems.at[2 * s + 4], sems.at[2 * s + 5],
                peers.up(s),
            )
            for s in range(1, peers.levels)
        ]
        self.fourth = remote(own, theirs, sems.at[4], sems.at[5], peers.other())

    def start(self):
        self.first.start()

    def cross(self):
        core = self.peers.core
        self.first.wait_recv()

        @pl.loop(0, self.peers.levels)
        def _(z):
            for x in range(2):
                total = self.grad[core, z, x].astype(jnp.float32) + self.cored[z, x].astype(jnp.float32)
                self.grad[core, z, x] = total.astype(self.grad.dtype)

        self.second.start()

    def rise(self):
        core, x = self.peers.core, self.peers.x
        self.second.wait_recv()

        @pl.loop(0, self.peers.levels)
        def _(z):
            total = self.grad[core, z, x].astype(jnp.float32) + self.crossed[z].astype(jnp.float32)
            self.grad[core, z, x] = total.astype(self.grad.dtype)

        for copy in self.third:
            copy.start()

    def own_piece(self):
        return self.grad[self.peers.core, self.peers.z, self.peers.x]

    def over(self):
        for copy in self.third:
            copy.wait_recv()
        total = self.own_piece().astype(jnp.float32)
        for s in range(self.peers.levels - 1):
            total = total + self.risen[s].astype(jnp.float32)
        self.own[...] = total.astype(self.own.dtype)
        self.fourth.start()

    def arrive(self):
        self.fourth.wait_recv()

    def finish(self):
        for copy in [self.first, self.second, self.fourth] + self.third:
            copy.wait_send()


class LateScatter(Scatter):
    def __init__(self, peers, halves, kept, crossed, risen, own, theirs, sems):
        x, z = peers.x, peers.z
        self.peers, self.kept, self.crossed, self.risen, self.own = peers, kept, crossed, risen, own
        self.second = remote(halves.at[:, 1 - x], crossed, sems.at[2], sems.at[3], peers.across())
        self.local = pltpu.make_async_copy(halves.at[:, x], kept, sems.at[0])
        self.third = [
            remote(
                kept.at[(z + s) % peers.levels], risen.at[s - 1], sems.at[2 * s + 4], sems.at[2 * s + 5], peers.up(s)
            )
            for s in range(1, peers.levels)
        ]
        self.fourth = remote(own, theirs, sems.at[4], sems.at[5], peers.other())

    def start(self):
        self.second.start()
        self.local.start()

    def rise(self):
        self.local.wait()
        self.second.wait_recv()

        @pl.loop(0, self.peers.levels)
        def _(z):
            total = self.kept[z].astype(jnp.float32) + self.crossed[z].astype(jnp.float32)
            self.kept[z] = total.astype(self.kept.dtype)

        for copy in self.third:
            copy.start()

    def own_piece(self):
        return self.kept[self.peers.z]

    def finish(self):
        for copy in [self.second, self.fourth] + self.third:
            copy.wait_send()


def scatter_sems(levels):
    return 2 * levels + 4


def scatter_buffers(levels, rows, columns, dtype):
    return [
        pltpu.VMEM((2, levels, 2, rows, columns), dtype),
        pltpu.VMEM((levels, 2, rows, columns), dtype),
        pltpu.VMEM((levels, rows, columns), dtype),
        pltpu.VMEM((levels - 1, rows, columns), dtype),
    ]


def attend_pair_back(valid_ref, mixed, att, lse_ref, datt, dmix, sums, pair, base, place):
    shards, length, width3 = mixed.shape
    part = width3 // 3
    group, within = pair // 2, pair % 2
    wide = dmix.shape[3] // 3

    def columns(t):
        return pl.ds(pl.multiple_of(t * part + pair * PAIR, PAIR), PAIR)

    def out_columns(t):
        return pl.ds(pl.multiple_of(t * wide + within * PAIR, PAIR), PAIR)

    own_columns = pl.ds(pl.multiple_of(base + pair * PAIR, PAIR), PAIR)
    da_columns = pl.ds(pl.multiple_of(pair * PAIR, PAIR), PAIR)
    row = lax.broadcasted_iota(jnp.int32, (shards * length, 1), 0)
    bias = jnp.where(row < valid_ref[0], 0.0, NEG_FILL).astype(jnp.float32)
    keys = mixed[:, :, columns(1)].reshape(shards * length, PAIR).astype(jnp.float32)
    values = mixed[:, :, columns(2)].reshape(shards * length, PAIR).astype(jnp.float32)
    keys_of = [augmented(keys, head, [bias, 1.0, 1.0, 1.0]) for head in range(2)]
    values_of = [augmented(values, head, [1.0, 1.0, 1.0]) for head in range(2)]
    plain_keys = [augmented(keys, head, []).T for head in range(2)]
    dk = dv = None
    queries_all = mixed[:, :, columns(0)].reshape(shards * length, PAIR)
    grads_all = datt[:, :, da_columns].reshape(shards * length, PAIR)
    att_all = att[:, :, da_columns].reshape(shards * length, PAIR)
    dqs = []
    for start, stop in query_tiles(shards * length):
        queries = queries_all[start:stop].astype(jnp.float32) * HD**-0.5
        grads = grads_all[start:stop].astype(jnp.float32)
        queries_t, grads_t = queries.T, grads.T
        product = grads_t * att_all[start:stop].astype(jnp.float32).T
        dq = None
        for head in range(2):
            lse = lse_ref[pair, head : head + 1, start:stop]
            delta = jnp.sum(product[HD * head : HD * (head + 1), :], axis=0, keepdims=True)
            scores = mat(keys_of[head], rows_with(queries_t, head, (1.0,) + split_three(-lse)))
            probs = jnp.exp(scores)
            moved = mat(values_of[head], rows_with(grads_t, head, split_three(-delta)))
            dscores = (probs * moved).astype(jnp.bfloat16)
            part_v = mat(probs.astype(jnp.bfloat16), augmented(grads, head, []))
            part_k = mat(dscores, augmented(queries, head, []))
            part_q = mat(plain_keys[head], dscores)
            dq = part_q if dq is None else dq + part_q
            dk = part_k if dk is None else dk + part_k
            dv = part_v if dv is None else dv + part_v
        dqs.append((dq * HD**-0.5).T.astype(jnp.bfloat16))
    dq = jnp.concatenate(dqs, axis=0)
    dmix[group, :, :, out_columns(0)] = dq.reshape(shards, length, PAIR)
    dq_sum = jnp.sum(dq.astype(jnp.float32), axis=0, keepdims=True)
    dk, dv = dk.astype(jnp.bfloat16), dv.astype(jnp.bfloat16)
    dmix[group, :, :, out_columns(1)] = dk.reshape(shards, length, PAIR)
    dmix[group, :, :, out_columns(2)] = dv.reshape(shards, length, PAIR)
    sums[3:4, own_columns] = dq_sum
    sums[4:5, own_columns] = jnp.sum(dv.astype(jnp.float32), axis=0, keepdims=True)


def column_sum(values):
    return jnp.sum(values, axis=0, keepdims=True)


def backward_layer(
    valid_ref, rows_ref, lse_ref,
    tok_in, dy_in, first_in, mixed_in, att_in, resid_in, second_in, act_in, slope_in,
    q_in, k_in, v_in, o_in, up_in, down_in, half_in,
    otok_ref, orecv_ref, gtok_ref, gqkv_ref, gout_ref, gup_ref, gdown_ref, gsmall_ref,
    down1, down2, down3, up0, up1, up2, up3, out0, out1, out2, out3, qa0, qa1, qa2, qa3, qb0, qb1, qb2, qb3,
    sm0, sm1, sm2, sm3, down_sum, up_sum, qkv_sum, out_own, out_theirs, sm_own, sm_theirs,
    ysend, yrecv, osend, dres, datt, datt_send, sums, dub, ssems, sems,
):
    levels = down2.shape[0]
    peers = Peers(4 * levels)
    p, q = peers.seq, 1 - peers.seq
    _, length, width = dy_in.shape
    part = width // 2
    own_hidden = act_in.shape[2]
    sub = own_hidden // (4 * levels)
    shard_rows = width // (4 * levels)
    wide = part // 2
    bf, f32 = jnp.bfloat16, jnp.float32
    tiles = length // ROW_TILE
    peers.greet()

    s_down = LateScatter(peers, half_in, down1, down2, down3, down_sum.at[p], down_sum.at[p], ssems.at[0])
    s_up = Scatter(peers, up0, up1, up2, up3, up_sum.at[p], up_sum.at[p], ssems.at[1])
    s_out = Scatter(peers, out0, out1, out2, out3, out_own, out_theirs, ssems.at[2])
    s_qa = Scatter(peers, qa0, qa1, qa2, qa3, qkv_sum.at[p, 0], qkv_sum.at[p, 0], ssems.at[3])
    s_qb = Scatter(peers, qb0, qb1, qb2, qb3, qkv_sum.at[p, 1], qkv_sum.at[p, 1], ssems.at[4])
    s_small = Scatter(peers, sm0, sm1, sm2, sm3, sm_own, sm_theirs, ssems.at[5])
    middle = length // 2

    def halves(at):
        rows = [slice(0, middle), slice(middle, length)]
        return [
            remote(ysend.at[r], yrecv.at[r], sems.at[at + 2 * i], sems.at[at + 1 + 2 * i], peers.other())
            for i, r in enumerate(rows)
        ]

    send_two, send_one = halves(8), halves(12)
    send_datt = [
        remote(
            datt_send.at[:, g * wide : (g + 1) * wide], datt.at[p, :, g * wide : (g + 1) * wide],
            sems.at[2 * g], sems.at[1 + 2 * g], peers.other(),
        )
        for g in range(2)
    ]
    send_out = remote(osend, orecv_ref, sems.at[4], sems.at[5], peers.other())
    s_down.start()
    sums[...] = jnp.zeros_like(sums)

    def row_at(i):
        return pl.ds(pl.multiple_of(i * ROW_TILE, 16), ROW_TILE)

    def load(src, dst, at):
        copy = pltpu.make_async_copy(src, dst, sems.at[at])
        copy.start()
        return copy

    def hidden_phase(dy, act, du, fdown, fup, second):
        early = [load(dy_in.at[q], dy.at[q], 16), load(down_in, fdown, 17), load(slope_in.at[q], du.at[q], 18)]
        copies = [
            load(up_in, fup, 19), load(dy_in.at[p], dy.at[p], 20), load(slope_in.at[p], du.at[p], 21),
            load(second_in, second, 22), load(act_in.at[q], act, 23),
        ]
        for copy in early:
            copy.wait()

        def into_hidden(shard):
            @pl.loop(0, levels)
            def _(z):
                at = pl.ds(pl.multiple_of(z * 4 * sub, PAIR), 4 * sub)
                grad = dot_f32(dy[shard], fdown[z].reshape(4 * sub, width), ((1,), (1,)))
                value = (grad * du[shard, :, at].astype(f32)).astype(bf)
                du[shard, :, at] = value
                dub[pl.ds(shard, 1), at] = column_sum(value.astype(f32))

        def back_second(shard, target, rows):
            @pl.loop(0, levels)
            def _(z):
                at = pl.ds(pl.multiple_of(z * 4 * shard_rows, PAIR), 4 * shard_rows)
                value = dot_f32(du[shard, rows, :], fup[z].reshape(4 * shard_rows, own_hidden), ((1,), (1,)))
                target[rows, at] = value.astype(target.dtype)

        into_hidden(q)
        copies[0].wait()
        for i in range(2):
            back_second(q, ysend, slice(i * middle, (i + 1) * middle))
            send_two[i].start()
        copies[1].wait()
        copies[2].wait()
        into_hidden(p)
        copies[3].wait()

        @pl.loop(0, levels)
        def _(z):
            at = pl.ds(pl.multiple_of(z * 4 * shard_rows, PAIR), 4 * shard_rows)
            value = dot_f32(
                second[:, :, at].reshape(2 * length, 4 * shard_rows), du[...].reshape(2 * length, own_hidden), ((0,), (0,))
            )
            place_blocks(up0, z, value)

        s_up.start()
        back_second(p, dres, slice(0, length))
        copies[4].wait()

        @pl.loop(0, width // COL_TILE)
        def _(t):
            at = pl.ds(pl.multiple_of(t * COL_TILE, PAIR), COL_TILE)
            weight = fdown[:, :, :, :, at].reshape(own_hidden, COL_TILE)
            osend[:, at] = mat(act[...], weight).astype(bf)

        s_down.rise()
        s_up.cross()

    pl.run_scoped(
        hidden_phase,
        pltpu.VMEM((2, length, width), bf),
        pltpu.VMEM((length, own_hidden), bf),
        pltpu.VMEM((2, length, own_hidden), bf),
        pltpu.VMEM(down_in.shape, bf),
        pltpu.VMEM(up_in.shape, bf),
        pltpu.VMEM((2, length, width), bf),
    )

    def norm_phase(dy, resid, att, fo, dbr):
        copies = [
            load(dy_in.at[p], dy, 16), load(resid_in, resid, 17), load(o_in, fo, 18), load(att_in.at[p], att, 19),
        ]
        copies[0].wait()
        copies[1].wait()

        def through_norm(i):
            at = row_at(i)
            hat, inverse = norm_parts(resid[at, :])
            grad = dres[at, :] + yrecv[at, :].astype(f32)
            grad_y = dy[at, :].astype(f32)
            value = grad_y + norm_back(hat, inverse, rows_ref[1:2, :], grad)
            dres[at, :] = value
            low = value.astype(bf)
            dbr[at, :] = low
            sums[1:2, :] += column_sum(grad * hat)
            sums[5:6, :] += column_sum(low.astype(f32))
            sums[6:7, :] += column_sum(grad)
            sums[7:8, :] += column_sum(grad_y)

        for i in range(2):
            send_two[i].wait_recv()
            pl.loop(i * (tiles // 2), (i + 1) * (tiles // 2))(through_norm)

        copies[2].wait()
        half = levels // 2
        for g in range(2):
            at = slice(g * wide, (g + 1) * wide)
            blocks = pl.ds(q * half + g * (half // 2), half // 2)
            value = dot_f32(dbr[...], fo[blocks].reshape(wide, width), ((1,), (1,)))
            datt_send[:, at] = value.astype(bf)
            send_datt[g].start()
        datt[p] = dot_f32(dbr[...], fo[pl.ds(p * half, half)].reshape(part, width), ((1,), (1,))).astype(bf)
        copies[3].wait()

        @pl.loop(0, levels)
        def _(z):
            at = pl.ds(pl.multiple_of(z * 4 * shard_rows, PAIR), 4 * shard_rows)
            place_blocks(out0, z, dot_f32(att[:, at], dbr[...], ((0,), (0,))))

        s_out.start()
        send_datt[0].wait_recv()
        send_out.start()
        s_up.rise()

    pl.run_scoped(
        norm_phase,
        pltpu.VMEM((length, width), bf),
        pltpu.VMEM((length, width), f32),
        pltpu.VMEM((length, width), bf),
        pltpu.VMEM(o_in.shape, bf),
        pltpu.VMEM((length, width), bf),
    )

    def heads_phase(dmix, first, fq, fk, fv):
        loaded = [load(first_in, first, 16), load(q_in, fq, 19), load(k_in, fk, 20), load(v_in, fv, 21)]

        def weight_grad(g, grad):
            @pl.loop(0, levels)
            def _(z):
                at = pl.ds(pl.multiple_of(z * 4 * shard_rows, PAIR), 4 * shard_rows)
                value = dot_f32(
                    first[:, :, at].reshape(2 * length, 4 * shard_rows),
                    dmix[g].reshape(2 * length, 3 * wide), ((0,), (0,)),
                )
                place_blocks(grad, z, value)

        own_part = pl.ds(pl.multiple_of(p * part, PAIR), part)

        def attention_phase(mixed, att):
            one, two = load(mixed_in, mixed, 17), load(att_in.at[:, :, own_part], att, 18)
            one.wait()
            two.wait()
            for copy in loaded:
                copy.wait()

            @pl.loop(0, part // PAIR)
            def _(pair):
                attend_pair_back(valid_ref, mixed, att, lse_ref, datt, dmix, sums, pair, p * part, p)

                @pl.when(pair == 0)
                def _():
                    s_out.cross()
                    s_down.over()

                @pl.when(pair == 1)
                def _():
                    weight_grad(0, qa0)
                    s_qa.start()
                    s_out.rise()
                    send_datt[1].wait_recv()

                @pl.when(pair == 2)
                def _():
                    s_qa.cross()
                    s_up.over()

                @pl.when(pair == 3)
                def _():
                    s_qa.rise()

        pl.run_scoped(
            attention_phase,
            pltpu.VMEM(mixed_in.shape, bf),
            pltpu.VMEM((2, length, part), bf),
        )

        def last_phase(tok, part_one, act, fdown, resid, others):
            copies = [
                load(tok_in, tok, 17), load(act_in.at[p], act, 18), load(down_in, fdown, 19), load(resid_in, resid, 20)
            ]
            for copy in send_two:
                copy.wait_send()

            def back_first(shard, target, rows):
                @pl.loop(0, levels)
                def _(z):
                    at = pl.ds(pl.multiple_of(z * 4 * shard_rows, PAIR), 4 * shard_rows)
                    total = None
                    for g in range(2):
                        for t, full in enumerate((fq, fk, fv)):
                            value = dot_f32(
                                dmix[g, shard, rows, t * wide : (t + 1) * wide],
                                full[z, :, :, :, g * wide : (g + 1) * wide].reshape(4 * shard_rows, wide),
                                ((1,), (1,)),
                            )
                            total = value if total is None else total + value
                    target[rows, at] = total.astype(target.dtype)

            def gain_sums(shard, source):
                @pl.loop(0, tiles)
                def _(i):
                    at = row_at(i)
                    hat, _ = norm_parts(tok[shard, at, :].astype(f32))
                    grad = source[at, :].astype(f32)
                    sums[0:1, :] += column_sum(grad * hat)
                    sums[2:3, :] += column_sum(grad)

            for i in range(2):
                back_first(q, part_one, slice(i * middle, (i + 1) * middle))

                @pl.loop(i * (tiles // 2), (i + 1) * (tiles // 2))
                def _(t):
                    ysend[row_at(t), :] = part_one[row_at(t), :].astype(bf)

                send_one[i].start()
            weight_grad(1, qb0)
            s_qb.start()
            copies[0].wait()
            gain_sums(q, part_one)
            back_first(p, part_one, slice(0, length))
            s_qb.cross()
            gain_sums(p, part_one)
            s_out.over()

            vectors = jnp.concatenate([sums[...], jnp.zeros((SMALL - 16, width), f32)], axis=0).T
            ups = dub[0:1, :] + dub[1:2, :]
            line = lax.broadcasted_iota(jnp.int32, (8, 1), 0)
            for d in range(4 * levels):
                at = (d % 2, d // 4, d % 4 // 2)
                sm0[at + (slice(0, shard_rows),)] = vectors[d * shard_rows : (d + 1) * shard_rows, :]
                sm0[at + (slice(shard_rows, shard_rows + 8),)] = jnp.where(line == p, ups[:, d * sub : (d + 1) * sub], 0.0)
            s_small.start()
            for copy in copies[1:]:
                copy.wait()
            send_out.wait_recv()
            fetched = load(orecv_ref, others, 18)
            s_small.cross()
            s_qb.rise()
            s_small.rise()
            s_qa.over()
            fetched.wait()

            @pl.loop(0, width // COL_TILE)
            def _(t):
                at = pl.ds(pl.multiple_of(t * COL_TILE, PAIR), COL_TILE)
                value = mat(act[...], fdown[:, :, :, :, at].reshape(own_hidden, COL_TILE))
                value = value + resid[:, at] + rows_ref[7:8, at] + others[:, at].astype(f32)
                others[:, at] = value.astype(bf)

            finished = load(others, otok_ref, 19)
            s_out.arrive()
            gout_ref[...] = out_own[...].astype(f32) + out_theirs[...].astype(f32)
            s_small.over()
            s_qb.over()
            s_down.arrive()
            s_up.arrive()
            for side in range(2):
                resid[side * sub : (side + 1) * sub, :] = down_sum[side].astype(f32)
                for d in range(4 * levels):
                    to = (2 * d + side) * sub
                    gup_ref[:, to : to + sub] = up_sum[side, :, d * sub : (d + 1) * sub].astype(f32)

            cast = load(resid.at[0 : 2 * sub], gdown_ref, 22)

            def through_norm(i):
                at = row_at(i)
                hat, inverse = norm_parts(tok[p, at, :].astype(f32))
                grad = part_one[at, :] + yrecv[at, :].astype(f32)
                part_one[at, :] = dres[at, :] + norm_back(hat, inverse, rows_ref[0:1, :], grad)

            written = []
            for i in range(2):
                send_one[i].wait_recv()
                pl.loop(i * (tiles // 2), (i + 1) * (tiles // 2))(through_norm)
                rows = slice(i * middle, (i + 1) * middle)
                written.append(load(part_one.at[rows], gtok_ref.at[rows], 20 + i))
            s_small.arrive()
            gsmall_ref[...] = sm_own[...] + sm_theirs[...]
            for g, s in enumerate((s_qa, s_qb)):
                s.arrive()
                for side in range(2):
                    for t in range(3):
                        to = t * width + side * part + g * wide
                        gqkv_ref[:, to : to + wide] = qkv_sum[side, g, :, t * wide : (t + 1) * wide].astype(f32)
            for copy in written + [finished, cast]:
                copy.wait()

        pl.run_scoped(
            last_phase,
            pltpu.VMEM((2, length, width), bf),
            pltpu.VMEM((length, width), f32),
            pltpu.VMEM((length, own_hidden), bf),
            pltpu.VMEM(down_in.shape, bf),
            pltpu.VMEM((length, width), f32),
            pltpu.VMEM((length, width), bf),
        )

    pl.run_scoped(
        heads_phase,
        pltpu.VMEM((2, 2, length, 3 * wide), bf),
        pltpu.VMEM((2, length, width), bf),
        pltpu.VMEM(q_in.shape, bf),
        pltpu.VMEM(k_in.shape, bf),
        pltpu.VMEM(v_in.shape, bf),
    )
    send_out.wait_send()
    for copy in send_one + send_datt:
        copy.wait_send()
    for s in (s_down, s_up, s_out, s_qa, s_qb, s_small):
        s.finish()


def run_backward(dps, valid, vectors, lse, tok, dy, first, mixed, att, resid, second, act, slope, fq, fk, fv, fo, fup, fdown, half):
    levels = dps // 4
    _, length, width = dy.shape
    part = width // 2
    wide = part // 2
    own_hidden = act.shape[2]
    shard_rows, sub = width // dps, own_hidden // dps
    bf, f32 = jnp.bfloat16, jnp.float32
    any_spec = pl.BlockSpec(memory_space=pl.ANY)
    vmem = pl.BlockSpec(memory_space=pltpu.VMEM)
    smem = pl.BlockSpec(memory_space=pltpu.SMEM)
    whole = [
        ((length, width), bf),
        ((length, width), bf),
        ((length, width), f32),
        ((shard_rows, 6 * part), f32),
        ((shard_rows, width), f32),
        ((shard_rows, 2 * own_hidden), f32),
        ((2 * sub, width), f32),
        ((shard_rows + 8, SMALL), f32),
    ]
    scratch = (
        [
            pltpu.VMEM((levels, sub, width), bf),
            pltpu.VMEM((levels, sub, width), bf),
            pltpu.VMEM((levels - 1, sub, width), bf),
        ]
        + scatter_buffers(levels, shard_rows, own_hidden, bf)
        + scatter_buffers(levels, shard_rows, width, bf)
        + scatter_buffers(levels, shard_rows, 3 * wide, bf)
        + scatter_buffers(levels, shard_rows, 3 * wide, bf)
        + scatter_buffers(levels, shard_rows + 8, SMALL, f32)
        + [
            pltpu.VMEM((2, sub, width), bf),
            pltpu.VMEM((2, shard_rows, own_hidden), bf),
            pltpu.VMEM((2, 2, shard_rows, 3 * wide), bf),
            pltpu.VMEM((shard_rows, width), bf),
            pltpu.VMEM((shard_rows, width), bf),
            pltpu.VMEM((shard_rows + 8, SMALL), f32),
            pltpu.VMEM((shard_rows + 8, SMALL), f32),
            pltpu.VMEM((length, width), bf),
            pltpu.VMEM((length, width), bf),
            pltpu.VMEM((length, width), bf),
            pltpu.VMEM((length, width), f32),
            pltpu.VMEM((2, length, part), bf),
            pltpu.VMEM((length, part), bf),
            pltpu.VMEM((16, width), f32),
            pltpu.VMEM((8, own_hidden), f32),
            pltpu.SemaphoreType.DMA((6, scatter_sems(levels))),
            pltpu.SemaphoreType.DMA((24,)),
        ]
    )
    return pl.pallas_call(
        backward_layer,
        in_specs=[smem, vmem, vmem] + [any_spec] * 16,
        out_specs=[any_spec] * 3 + [vmem] * 3 + [any_spec, vmem],
        out_shape=[jax.ShapeDtypeStruct(*s) for s in whole],
        scratch_shapes=scratch,
        compiler_params=pltpu.CompilerParams(
            vmem_limit_bytes=62 * 2**20, collective_id=1, has_side_effects=True
        ),
        cost_estimate=pl.CostEstimate(flops=5 * 10**10, bytes_accessed=8 * 10**7, transcendentals=2 * 10**7),
    )(valid, vectors, lse, tok, dy, first, mixed, att, resid, second, act, slope, fq, fk, fv, fo, fup, fdown, half)


def per_device_pair(tokens, w_qkv, w_out, w_up, w_down, gains, biases, up_bias, valid, cotangent):
    _, length, width = tokens.shape
    shard_rows = w_qkv.shape[0]
    dps = lax.axis_size("dp")
    sub = w_down.shape[0] // 2

    smalls = jnp.concatenate([gains, biases], axis=1)
    smalls = jnp.concatenate(
        [
            jnp.pad(smalls, ((0, 0), (0, SMALL - smalls.shape[1]))),
            jnp.pad(up_bias.reshape(2, sub), ((0, 14), (0, 0))),
        ],
        axis=0,
    )
    (
        tok, dy, first, mixed, att, lse, residual, second, act, slope, fq, fk, fv, fo, fup, fdown, half, vectors, _
    ) = run_forward(
        dps, tokens.reshape(length, width), cotangent.reshape(length, width), w_qkv, w_out, w_up, w_down, smalls, valid
    )
    out_tokens, _, grad_tokens, grad_qkv, grad_out, grad_up, grad_down, grad_small = run_backward(
        dps, valid, vectors, lse, tok, dy, first, mixed, att, residual, second, act, slope, fq, fk, fv, fo, fup, fdown, half
    )
    return (
        out_tokens.reshape(tokens.shape),
        grad_tokens.reshape(tokens.shape),
        grad_qkv,
        grad_out,
        grad_up,
        grad_down,
        grad_small[:shard_rows, :2],
        grad_small[:shard_rows, 2:8],
        grad_small[shard_rows : shard_rows + 2, :].reshape(-1),
    )


def per_device(tokens, w_qkv, w_out, w_up, w_down, gains, biases, up_bias, valid, cotangent):
    images, length, width = tokens.shape
    rows = images * length
    shard_rows = w_qkv.shape[0]
    hidden = w_up.shape[1]
    ups = up_bias.shape[0] // shard_rows
    shards = lax.axis_size("seq")
    dps = lax.axis_size("dp")
    at = lax.axis_index("seq").astype(jnp.int32)
    place = at.reshape(1)
    part = width // shards
    own_hidden = hidden // shards
    sub = w_down.shape[0] // shards
    pairs_all = part // PAIR

    gather = functools.partial(lax.all_gather, axis_name="dp", axis=0, tiled=True)
    scatter = functools.partial(lax.psum_scatter, axis_name="dp", scatter_dimension=0, tiled=True)

    def pick(values, axis):
        return lax.dynamic_index_in_dim(values, at, axis, keepdims=False)

    smalls = jnp.concatenate([gains, biases, up_bias.reshape(shard_rows, ups)], axis=1)
    smalls = jnp.pad(smalls, ((0, 0), (0, SMALL - smalls.shape[1])))
    part_qkv = pick(w_qkv.reshape(shard_rows, 3, shards, part), 2).reshape(shard_rows, 3 * part)
    part_up = pick(w_up.reshape(shard_rows, dps, shards, sub), 2).reshape(shard_rows, own_hidden)
    part_down = pick(w_down.reshape(shards, sub, width), 0)
    full_qkvs = gather(jnp.concatenate([part_qkv, smalls], axis=1))
    w_out, full_qkvs = lax.optimization_barrier((w_out, full_qkvs))
    full_out = gather(w_out)
    part_up, full_out = lax.optimization_barrier((part_up, full_out))
    full_up = gather(part_up)
    part_down, full_up = lax.optimization_barrier((part_down, full_up))
    full_down = gather(part_down)

    flat_tokens = tokens.reshape(rows, width)
    flat_grad = cotangent.reshape(rows, width)
    all_tokens = everyone(flat_tokens, shards)
    flat_grad, all_tokens = lax.optimization_barrier((flat_grad, all_tokens))
    all_grad = everyone(flat_grad, shards).reshape(shards * rows, width)

    full_qkv = full_qkvs[:, : 3 * part]
    small = full_qkvs[:, 3 * part :].astype(jnp.float32).T
    gain_one, gain_two = small[0], small[1]
    bias_one, bias_q, bias_v, bias_out, bias_two, bias_down = (small[2 + i] for i in range(6))
    bias_up = pick(small[8 : 8 + ups].T.reshape(dps, shards, sub), 1).reshape(-1)
    bias_mixed = jnp.concatenate(
        [pick(bias_q.reshape(shards, part), 0), jnp.zeros((part,), jnp.float32), pick(bias_v.reshape(shards, part), 0)]
    )

    every_tokens = all_tokens.reshape(shards * rows, width).astype(jnp.float32)
    hat_one, inverse_one = norm_parts(every_tokens)
    first = (hat_one * gain_one + bias_one).astype(jnp.bfloat16)
    mixed = (mat(first, full_qkv) + bias_mixed).astype(jnp.bfloat16).reshape(shards, rows, 3 * part)

    groups = GROUPS if pairs_all % GROUPS == 0 else 1
    pairs = pairs_all // groups
    wide = pairs * PAIR
    forward = [attend_forward(images, place, valid, mixed, g * pairs, pairs) for g in range(groups)]
    blocks = []
    for j in range(shards):
        for g in range(groups):
            attended = forward[g][0]
            if j > 0:
                attended = jnp.roll(shift(attended, shards, -j), j, axis=0)
            blocks.append(attended.reshape(shards * rows, wide))
    merged = jnp.concatenate(blocks, axis=1)
    turned_out = jnp.roll(full_out, -at * part, axis=0)

    branch = mat(merged, turned_out) + bias_out
    residual = every_tokens + branch
    hat_two, inverse_two = norm_parts(residual)
    second = (hat_two * gain_two + bias_two).astype(jnp.bfloat16)
    upward = mat(second, full_up) + bias_up
    cdf = 0.5 * (1.0 + lax.erf(upward * 0.5**0.5))
    activated = (upward * cdf).astype(jnp.bfloat16)
    slope = cdf + upward * (jnp.exp(-0.5 * upward * upward) * 0.3989422804014327)
    slope = slope.astype(jnp.bfloat16)

    grad_act = dot_f32(all_grad, full_down, ((1,), (1,)))
    grad_upward = (grad_act * slope.astype(jnp.float32)).astype(jnp.bfloat16)

    def summed(left, right, dims):
        parts = [
            dot_f32(left[j * rows : (j + 1) * rows], right, dims) for j in range(shards)
        ]
        total = parts[0]
        for j in range(1, shards):
            total = total + shift(parts[j].astype(jnp.bfloat16), shards, j).astype(jnp.float32)
        return total

    grad_second = summed(grad_upward, full_up, ((1,), (1,)))
    grad_down = dot_f32(activated, all_grad, ((0,), (0,))).astype(jnp.bfloat16)
    piece_down = scatter(grad_down)
    grad_up = dot_f32(second, grad_upward, ((0,), (0,))).astype(jnp.bfloat16)
    grad_up, piece_down = lax.optimization_barrier((grad_up, piece_down))
    piece_up = scatter(grad_up)

    own_hat = hat_two[:rows]
    grad_resid = flat_grad.astype(jnp.float32) + norm_back(own_hat, inverse_two[:rows], gain_two, grad_second)
    grad_gain_two, grad_bias_two = token_sum(grad_second * own_hat), token_sum(grad_second)
    grad_branch = grad_resid.astype(jnp.bfloat16)
    grad_merged = dot_f32(grad_branch, turned_out, ((1,), (1,))).astype(jnp.bfloat16)
    received = [None] * shards
    for g in range(groups):
        lo = g * wide
        blocks = [grad_merged[:, lo : lo + wide]] + [None] * (shards - 1)
        for j in range(1, shards):
            blocks[shards - j] = shift(grad_merged[:, j * part + lo : j * part + lo + wide], shards, j)
        received[g] = jnp.stack(blocks)

    grad_out = dot_f32(merged[:rows], grad_branch, ((0,), (0,))).astype(jnp.bfloat16)
    grad_out = jnp.roll(grad_out, at * part, axis=0)
    grad_out, piece_up = lax.optimization_barrier((grad_out, piece_up))
    piece_out = scatter(grad_out)

    backs = [
        attend_backward(images, place, valid, mixed, g * pairs, pairs, *forward[g], received[g]) for g in range(groups)
    ]
    grad_mixed = jnp.concatenate(
        [back[t].reshape(shards * rows, wide) for t in range(3) for back in backs], axis=1
    )
    grad_first = summed(grad_mixed, full_qkv, ((1,), (1,)))
    grad_qkv = dot_f32(first, grad_mixed, ((0,), (0,))).astype(jnp.bfloat16)

    grad_tokens = grad_resid + norm_back(hat_one[:rows], inverse_one[:rows], gain_one, grad_first)
    grad_gain_one, grad_bias_one = token_sum(grad_first * hat_one[:rows]), token_sum(grad_first)

    def spread(values, before):
        out = jnp.zeros((before, shards, values.size // before), jnp.float32)
        return lax.dynamic_update_slice_in_dim(out, values.reshape(before, 1, -1), at, 1).reshape(-1)

    bias_sums = token_sum(grad_mixed)
    small_grads = jnp.stack(
        [
            grad_gain_one, grad_gain_two, grad_bias_one, spread(bias_sums[:part], 1), spread(bias_sums[2 * part :], 1),
            token_sum(grad_branch), grad_bias_two, token_sum(flat_grad),
        ],
        axis=1,
    )
    up_sums = spread(token_sum(grad_upward), dps).reshape(width, ups)
    small_grads = jnp.concatenate([small_grads, up_sums], axis=1)
    small_grads = jnp.pad(small_grads, ((0, 0), (0, SMALL - small_grads.shape[1])))
    grad_qkvs = jnp.concatenate([grad_qkv, small_grads.astype(jnp.bfloat16)], axis=1)
    grad_qkvs, piece_out = lax.optimization_barrier((grad_qkvs, piece_out))
    piece_qkvs = scatter(grad_qkvs)

    output = summed(activated, full_down, ((1,), (0,)))
    out_tokens = (residual[:rows] + output + bias_down).astype(jnp.bfloat16)

    total_down = in_order(piece_down, shards, at).astype(jnp.float32).reshape(shards * sub, width)
    total_up = in_order(piece_up.reshape(shard_rows, dps, sub), shards, at).astype(jnp.float32)
    total_up = total_up.transpose(1, 2, 0, 3).reshape(shard_rows, hidden)
    total_out = in_order(piece_out, shards, at).astype(jnp.float32).sum(0)
    every_qkvs = in_order(piece_qkvs, shards, at).astype(jnp.float32)
    total_qkv = every_qkvs[:, :, : 3 * part].reshape(shards, shard_rows, 3, part)
    total_qkv = total_qkv.transpose(1, 2, 0, 3).reshape(shard_rows, 3 * width)
    total_small = every_qkvs[:, :, 3 * part :].sum(0)
    return (
        out_tokens.reshape(tokens.shape),
        grad_tokens.reshape(tokens.shape),
        total_qkv,
        total_out,
        total_up,
        total_down,
        total_small[:, :2],
        total_small[:, 2:8],
        total_small[:, 8 : 8 + ups].reshape(-1),
    )


def solution(mesh):
    paired = mesh.shape["seq"] == 2 and mesh.shape["dp"] == 16
    return jax.shard_map(
        per_device_pair if paired else per_device,
        mesh=mesh,
        in_specs=(
            P("dp", "seq", None),
            P("dp", None),
            P("dp", None),
            P("dp", None),
            P("dp", None),
            P("dp", None),
            P("dp", None),
            P("dp"),
            P("dp"),
            P("dp", "seq", None),
        ),
        out_specs=(
            P("dp", "seq", None),
            P("dp", "seq", None),
            P("dp", None),
            P("dp", None),
            P("dp", None),
            P("dp", None),
            P("dp", None),
            P("dp", None),
            P("dp"),
        ),
        check_vma=False,
    )
```
